32 devices in a mesh: blk: 16 (over z, y, core), tp: 2 (over x).
Axes of the slice: x: 2, y: 2, z: 4, core: 2. Of those that a mesh axis runs over, the one named last changes fastest.
Arguments:
- frames: bfloat16 [4096, 1024], P('blk'), may hold values from -6 to 6
- clip_lengths: int32 [8], replicated, may hold values from 1 to 3841, 4096 in all
- text_states: bfloat16 [128, 1024], replicated, may hold values from -6 to 6
- text_segments: int32 [128], replicated, may hold values from 0 to 7, never falling along the last dimension, each value on 1 to 32 neighbouring positions
- gain_one: float32 [1024], replicated, may hold values from 0.1 to 1.9
- shift_one: float32 [1024], replicated, may hold values from -1.5 to 1.5
- gain_two: float32 [1024], replicated, may hold values from 0.1 to 1.9
- shift_two: float32 [1024], replicated, may hold values from -1.5 to 1.5
- gain_three: float32 [1024], replicated, may hold values from 0.1 to 1.9
- shift_three: float32 [1024], replicated, may hold values from -1.5 to 1.5
- query_weight: bfloat16 [1024, 1024], P(None, 'tp'), may hold values from -0.1875 to 0.1875
- key_weight: bfloat16 [1024, 1024], P(None, 'tp'), may hold values from -0.1875 to 0.1875
- value_weight: bfloat16 [1024, 1024], P(None, 'tp'), may hold values from -0.1875 to 0.1875
- output_weight: bfloat16 [1024, 1024], P('tp'), may hold values from -0.75 to 0.75
- cross_query: bfloat16 [1024, 1024], P(None, 'tp'), may hold values from -0.1875 to 0.1875
- cross_key: bfloat16 [1024, 1024], P(None, 'tp'), may hold values from -0.1875 to 0.1875
- cross_value: bfloat16 [1024, 1024], P(None, 'tp'), may hold values from -0.1875 to 0.1875
- cross_output: bfloat16 [1024, 1024], P('tp'), may hold values from -0.375 to 0.375
- inner_weight: bfloat16 [1024, 4096], P(None, 'tp'), may hold values from -0.1875 to 0.1875
- outer_weight: bfloat16 [4096, 1024], P('tp'), may hold values from -0.09375 to 0.09375
- cotangent: bfloat16 [4096, 1024], P('blk'), may hold values from -6 to 6
Outputs:
- result: bfloat16 [4096, 1024], P('blk')
- grad_frames: bfloat16 [4096, 1024], P('blk')
- grad_text: float32 [128, 1024], replicated
- grad_gain_one: float32 [1024], replicated
- grad_shift_one: float32 [1024], replicated
- grad_gain_two: float32 [1024], replicated
- grad_shift_two: float32 [1024], replicated
- grad_gain_three: float32 [1024], replicated
- grad_shift_three: float32 [1024], replicated
- grad_query_weight: float32 [1024, 1024], P(None, 'tp')
- grad_key_weight: float32 [1024, 1024], P(None, 'tp')
- grad_value_weight: float32 [1024, 1024], P(None, 'tp')
- grad_output_weight: float32 [1024, 1024], P('tp')
- grad_cross_query: float32 [1024, 1024], P(None, 'tp')
- grad_cross_key: float32 [1024, 1024], P(None, 'tp')
- grad_cross_value: float32 [1024, 1024], P(None, 'tp')
- grad_cross_output: float32 [1024, 1024], P('tp')
- grad_inner_weight: float32 [1024, 4096], P(None, 'tp')
- grad_outer_weight: float32 [4096, 1024], P('tp')
The draws below stay inside these ranges and needn't reach their ends.
Inputs may be any that keep to these rules, and one draw needn't show every extreme that they name: `clip_lengths`: clips follow one another in the pack; one of them has 3841 frames. `text_segments`: text tokens of a clip stand together and in clip order; every clip has 1 to 32 of them, one exactly 32.
All inputs are finite; a program needn't handle non-finite values.
Results may differ from the reference program's by a relative error of at most 0.028.
Values may be sent and summed in bfloat16 or wider, within the bound.
No kernel may reach another device: no remote copies, remote signals or barrier semaphores. Data moves between devices by JAX's collectives and lax.ppermute only.
A program may use at most 384 MiB of HBM per device.

```python
import math
import jax
import jax.numpy as jnp
import numpy as np
from jax import lax

D = 1024
HEADS = 16
HEAD_DIM = 64
FF = 4096
TOK_DEV = 256
NCLIP = 8
TXT = 128
TEXT_MOST = 32
TOKENS = 4096


def block_levels(own_key, shape, split, least, top_value):
    level, own = 1.0, jax.random.fold_in(own_key, 6)
    for position, blocks in split:
        heights = jnp.exp(jax.random.uniform(jax.random.fold_in(own, position), (blocks,), jnp.float32, least / len(split), top_value / len(split)))
        level = level * jnp.repeat(heights, shape[position] // blocks).reshape([-1 if axis == position else 1 for axis in range(len(shape))])
    return level


def profile(count, total, bound, slope):
    weights = [(1 << 20) // math.isqrt(rank ** slope) + 1 for rank in range(2, count + 1)]
    surplus, holding = total - bound - (count - 1), [1] * (count - 1)
    while surplus > 0:
        movable = [i for i in range(count - 1) if holding[i] < bound]
        mass, remaining = sum([weights[i] for i in movable]), surplus
        for i in movable:
            more = min(bound - holding[i], max(1, remaining * weights[i] // mass), surplus)
            holding[i] = holding[i] + more
            surplus = surplus - more
    return np.array([bound] + holding)


def ragged_sizes(stream_key, amount, total, bound, lean):
    if amount == 2:
        one = jax.random.randint(stream_key, (), max(1, total - bound), min(bound, total - 1) + 1)
        return jnp.stack([one, total - one])
    lengths = jnp.asarray(profile(amount, total, bound, lean), jnp.int32)
    twos = (amount - 1) // 2
    giver, receiver = lengths[1:1 + 2 * twos:2], lengths[2:2 + 2 * twos:2]
    room = jnp.minimum(giver - 1, bound - receiver)
    passed = jax.random.randint(jax.random.fold_in(stream_key, 1), (twos,), 0, 1 << 20) % (room + 1)
    lengths = lengths.at[1:1 + 2 * twos:2].set(giver - passed).at[2:2 + 2 * twos:2].set(receiver + passed)
    return lengths[jax.random.permutation(jax.random.fold_in(stream_key, 2), amount)]


def noise(stream_key, shape, scale, bound, split=(), held_as=jnp.bfloat16):
    level = block_levels(stream_key, shape, split, -0.22, 0.18) if split else 1.0
    values = jax.random.normal(stream_key, shape, jnp.float32) * scale * level
    return jnp.minimum(jnp.maximum(values, -bound), bound).astype(held_as)


def setup_inputs(seed: int = 0) -> dict:
    key_list = jax.random.split(jax.random.key(seed), 22)
    frames = noise(key_list[0], (TOKENS, D), 1.0, 6.0, ((0, 16),))
    clip_lengths = ragged_sizes(key_list[1], NCLIP, TOKENS, TOKENS - TOK_DEV + 1, 2).astype(jnp.int32)
    text_states = noise(key_list[2], (TXT, D), 1.0, 6.0)
    text_segments = jnp.searchsorted(jnp.cumsum(ragged_sizes(key_list[3], NCLIP, TXT, TEXT_MOST, 1)), jnp.arange(TXT), side="right").astype(jnp.int32)
    gain_one = jnp.clip(1.0 + 0.18 * jax.random.normal(key_list[4], (D,), jnp.float32), 0.1, 1.9)
    shift_one = noise(key_list[5], (D,), 0.3, 1.5, (), jnp.float32)
    gain_two = jnp.clip(1.0 + 0.18 * jax.random.normal(key_list[6], (D,), jnp.float32), 0.1, 1.9)
    shift_two = noise(key_list[7], (D,), 0.3, 1.5, (), jnp.float32)
    gain_three = jnp.clip(1.0 + 0.18 * jax.random.normal(key_list[8], (D,), jnp.float32), 0.1, 1.9)
    shift_three = noise(key_list[9], (D,), 0.3, 1.5, (), jnp.float32)
    query_weight = noise(key_list[10], (D, D), D ** -0.5, 0.1875, ((1, 2),))
    key_weight = noise(key_list[11], (D, D), D ** -0.5, 0.1875, ((1, 2),))
    value_weight = noise(key_list[12], (D, D), D ** -0.5, 0.1875, ((1, 2),))
    output_weight = noise(key_list[13], (D, D), (D // 16) ** -0.5, 0.75, ((0, 2),))
    cross_query = noise(key_list[14], (D, D), D ** -0.5, 0.1875, ((1, 2),))
    cross_key = noise(key_list[15], (D, D), D ** -0.5, 0.1875, ((1, 2),))
    cross_value = noise(key_list[16], (D, D), D ** -0.5, 0.1875, ((1, 2),))
    cross_output = noise(key_list[17], (D, D), (D // 4) ** -0.5, 0.375, ((0, 2),))
    inner_weight = noise(key_list[18], (D, FF), D ** -0.5, 0.1875, ((1, 2),))
    outer_weight = noise(key_list[19], (FF, D), FF ** -0.5, 0.09375, ((0, 2),))
    cotangent = noise(key_list[20], (TOKENS, D), 1.0, 6.0, ((0, 16),))
    return {"frames": frames, "clip_lengths": clip_lengths, "text_states": text_states, "text_segments": text_segments, "gain_one": gain_one, "shift_one": shift_one, "gain_two": gain_two, "shift_two": shift_two, "gain_three": gain_three, "shift_three": shift_three, "query_weight": query_weight, "key_weight": key_weight, "value_weight": value_weight, "output_weight": output_weight, "cross_query": cross_query, "cross_key": cross_key, "cross_value": cross_value, "cross_output": cross_output, "inner_weight": inner_weight, "outer_weight": outer_weight, "cotangent": cotangent}


EPSILON = 1e-05
NEGATIVE = -1e+30
HIGHEST = lax.Precision.HIGHEST

@jax.custom_vjp
def low(v):
    return lax.optimization_barrier(v.astype(jnp.bfloat16)).astype(jnp.float32)

@jax.custom_vjp
def low_back(v):
    return v

def low_keep(v):
    return (low(v), None)

def low_pass(kept, grad):
    return (grad,)

def back_keep(v):
    return (v, None)

def back_low(kept, grad):
    return (low(grad),)
low.defvjp(low_keep, low_pass)
low_back.defvjp(back_keep, back_low)

def twice_low(values):
    return low(low_back(values))

def layer_norm(values, gain, shift):
    centre = values - lax.optimization_barrier(jnp.mean(values, axis=-1, keepdims=True))
    spread = lax.optimization_barrier(jnp.mean(centre * centre, axis=-1, keepdims=True))
    return centre * lax.rsqrt(spread + EPSILON) * gain + shift

def clip_rows(positions, clip_lengths):
    ends = jnp.cumsum(clip_lengths).astype(jnp.int32)
    starts = (ends - clip_lengths).astype(jnp.int32)
    segment = lax.optimization_barrier(jnp.sum((positions[:, None] >= ends[None, :]).astype(jnp.int32), axis=1)).astype(jnp.int32)
    match = segment[:, None] == jnp.arange(clip_lengths.shape[0], dtype=jnp.int32)[None, :]
    first = lax.optimization_barrier(jnp.sum(jnp.where(match, starts[None, :], 0), axis=1)).astype(jnp.int32)
    return (segment, first)

def attend(queries, keys, values, allowed):
    scores = low_back(jnp.einsum('qhd,khd->hqk', queries, keys, precision=HIGHEST))
    masked = jnp.where(allowed[None], scores, NEGATIVE)
    largest = lax.optimization_barrier(jnp.max(masked, axis=-1, keepdims=True))
    expo = jnp.where(allowed[None], jnp.exp(masked - largest), 0.0)
    weights = low(expo / lax.optimization_barrier(jnp.sum(expo, axis=-1, keepdims=True)))
    result = jnp.einsum('hqk,khd->qhd', weights, values, precision=HIGHEST)
    return result.reshape(result.shape[0], -1)

def mult(left, right):
    return jnp.dot(left, right, precision=HIGHEST)

def reference(frames, clip_lengths, text_states, text_segments, gain_one, shift_one, gain_two, shift_two, gain_three, shift_three, query_weight, key_weight, value_weight, output_weight, cross_query, cross_key, cross_value, cross_output, inner_weight, outer_weight, cotangent):
    positions = jnp.arange(TOKENS, dtype=jnp.int32)
    segment, first = clip_rows(positions, clip_lengths)
    qblock = math.gcd(TOKENS, 512)
    nblock = TOKENS // qblock
    scale = float(HEAD_DIM) ** (-0.5)

    def forward(inputs, texts, g_one, b_one, g_two, b_two, g_three, b_three, w_query, w_key, w_value, w_output, c_query, c_key, c_value, c_output, w_inner, w_outer):
        normed_one = low(layer_norm(inputs, g_one, b_one))
        queries = twice_low(mult(normed_one, w_query) * scale)
        keys = twice_low(mult(normed_one, w_key)).reshape(TOKENS, HEADS, HEAD_DIM)
        values = twice_low(mult(normed_one, w_value)).reshape(TOKENS, HEADS, HEAD_DIM)

        def self_block(item):
            block_query, block_rows, block_first = item
            allowed = (positions[None, :] <= block_rows[:, None]) & (positions[None, :] >= block_first[:, None])
            return attend(block_query, keys, values, allowed)
        attended = lax.map(jax.checkpoint(self_block), (queries.reshape(nblock, qblock, HEADS, HEAD_DIM), positions.reshape(nblock, qblock), first.reshape(nblock, qblock)))
        attended = twice_low(attended.reshape(TOKENS, D))
        first_sum = inputs + low_back(mult(attended, w_output))
        normed_two = low(layer_norm(first_sum, g_two, b_two))
        cross_queries = twice_low(mult(normed_two, c_query) * scale)
        text_keys = twice_low(mult(texts, c_key)).reshape(TXT, HEADS, HEAD_DIM)
        text_values = twice_low(mult(texts, c_value)).reshape(TXT, HEADS, HEAD_DIM)

        def cross_block(item):
            block_query, block_segment = item
            allowed = block_segment[:, None] == text_segments[None, :]
            return attend(block_query, text_keys, text_values, allowed)
        crossed = lax.map(jax.checkpoint(cross_block), (cross_queries.reshape(nblock, qblock, HEADS, HEAD_DIM), segment.reshape(nblock, qblock)))
        crossed = twice_low(crossed.reshape(TOKENS, D))
        second_sum = first_sum + low_back(mult(crossed, c_output))
        normed_three = low(layer_norm(second_sum, g_three, b_three))
        hidden = low(jax.nn.gelu(low_back(mult(normed_three, w_inner)), approximate=False))
        return second_sum + low_back(mult(hidden, w_outer))
    primals = (frames.astype(jnp.float32), text_states.astype(jnp.float32), gain_one, shift_one, gain_two, shift_two, gain_three, shift_three, query_weight.astype(jnp.float32), key_weight.astype(jnp.float32), value_weight.astype(jnp.float32), output_weight.astype(jnp.float32), cross_query.astype(jnp.float32), cross_key.astype(jnp.float32), cross_value.astype(jnp.float32), cross_output.astype(jnp.float32), inner_weight.astype(jnp.float32), outer_weight.astype(jnp.float32))
    output, pullback = jax.vjp(forward, *primals)
    grads = pullback(cotangent.astype(jnp.float32))
    return (output.astype(jnp.bfloat16), grads[0].astype(jnp.bfloat16), grads[1], grads[2], grads[3], grads[4], grads[5], grads[6], grads[7], grads[8], grads[9], grads[10], grads[11], grads[12], grads[13], grads[14], grads[15], grads[16], grads[17])
```

```python
import functools
import jax
import jax.numpy as jnp
from jax import lax
from jax.experimental import pallas as pl
from jax.experimental.pallas import tpu as pltpu
from jax.sharding import PartitionSpec as P

HEAD_DIM = 64
NEGATIVE = -1e30
BF, F32 = jnp.bfloat16, jnp.float32


def dg(left, right, dims):
    return lax.dot_general(left, right, (dims, ((), ())), preferred_element_type=F32)


def tile_ranges(positions, first, tile, chunk):
    rows = positions.reshape(-1, tile)
    starts = first.reshape(-1, tile)
    low = jnp.min(starts, axis=1) // chunk
    high = jnp.max(rows, axis=1) // chunk + 1
    clear = jnp.clip((jnp.max(starts, axis=1) + chunk - 1) // chunk, low, high)
    stop = jnp.clip((jnp.min(rows, axis=1) + 1) // chunk, clear, high)
    return jnp.stack([low, clear, stop, high], axis=1)


def allowed_keys(base, flip, chunk, rows, first):
    keys = (base + lax.broadcasted_iota(jnp.int32, (chunk, rows.shape[1]), 0)) ^ flip
    return (keys <= rows) & (keys >= first)


def attend_kernel(ranges, flips, q_ref, k_ref, v_ref, row_ref, first_ref, out_ref, log_ref, k_rows, chunk):
    tile = pl.program_id(0)
    total = k_ref.shape[1]

    @pl.when(tile == 0)
    def _():
        for base in range(0, total, chunk):
            k_rows[base : base + chunk, :] = k_ref[:, base : base + chunk].T

    queries = q_ref[...]
    rows, first = row_ref[...], first_ref[...]
    width = queries.shape[1]

    def work(masked):
        def step(index, carry):
            best, total_weight, acc = carry
            base = pl.multiple_of(index * chunk, chunk)
            score = jnp.dot(k_rows[pl.ds(base, chunk), :], queries, preferred_element_type=F32)
            if masked:
                allowed = allowed_keys(base, flips[0], chunk, rows, first)
                score = jnp.where(allowed, score, NEGATIVE)
            new_best = jnp.maximum(best, jnp.max(score, axis=0, keepdims=True))
            expo = jnp.exp(score - new_best)
            if masked:
                expo = jnp.where(allowed, expo, 0.0)
            fade = jnp.exp(best - new_best)
            total_weight = total_weight * fade + jnp.sum(expo, axis=0, keepdims=True)
            acc = acc * fade + jnp.dot(
                v_ref[:, pl.ds(base, chunk)], expo.astype(BF), preferred_element_type=F32
            )
            return new_best, total_weight, acc

        return step

    carry = (
        jnp.full((1, width), NEGATIVE, F32),
        jnp.zeros((1, width), F32),
        jnp.zeros((HEAD_DIM, width), F32),
    )
    carry = lax.fori_loop(ranges[tile, 0], ranges[tile, 1], work(True), carry)
    carry = lax.fori_loop(ranges[tile, 1], ranges[tile, 2], work(False), carry)
    best, total_weight, acc = lax.fori_loop(ranges[tile, 2], ranges[tile, 3], work(True), carry)
    out_ref[...] = acc / total_weight
    log_ref[...] = best + jnp.log(total_weight)


def attend(queries, keys, values, rows, first, flip, tile=512, chunk=1024):
    count, total = queries.shape[1], keys.shape[1]
    tile = min(tile, count)
    chunk = min(chunk, total)
    ranges = tile_ranges(rows, first, tile, chunk)
    whole = lambda i, r, f: (0, 0)
    part = lambda i, r, f: (0, i)
    return pl.pallas_call(
        functools.partial(attend_kernel, chunk=chunk),
        grid_spec=pltpu.PrefetchScalarGridSpec(
            num_scalar_prefetch=2,
            grid=(count // tile,),
            in_specs=[
                pl.BlockSpec((HEAD_DIM, tile), part),
                pl.BlockSpec((HEAD_DIM, total), whole),
                pl.BlockSpec((HEAD_DIM, total), whole),
                pl.BlockSpec((1, tile), part),
                pl.BlockSpec((1, tile), part),
            ],
            out_specs=[pl.BlockSpec((HEAD_DIM, tile), part), pl.BlockSpec((1, tile), part)],
            scratch_shapes=[pltpu.VMEM((total, HEAD_DIM), BF)],
        ),
        out_shape=[
            jax.ShapeDtypeStruct((HEAD_DIM, count), F32),
            jax.ShapeDtypeStruct((1, count), F32),
        ],
        compiler_params=pltpu.CompilerParams(vmem_limit_bytes=40 << 20),
        name="attend",
    )(ranges, flip.reshape(1), queries, keys, values, rows.reshape(1, -1), first.reshape(1, -1))


def attend_back_kernel(
    ranges, flips, q_ref, k_ref, v_ref, row_ref, first_ref, out_ref, log_ref, do_ref,
    dq_ref, dk_ref, dv_ref, k_rows, v_rows, chunk,
):
    tile = pl.program_id(0)
    total = k_ref.shape[1]

    @pl.when(tile == 0)
    def _():
        for base in range(0, total, chunk):
            k_rows[base : base + chunk, :] = k_ref[:, base : base + chunk].T
            v_rows[base : base + chunk, :] = v_ref[:, base : base + chunk].T
        dk_ref[...] = jnp.zeros_like(dk_ref)
        dv_ref[...] = jnp.zeros_like(dv_ref)

    queries, grads = q_ref[...], do_ref[...]
    rows, first = row_ref[...], first_ref[...]
    log_total = log_ref[...]
    delta = jnp.sum(grads.astype(F32) * out_ref[...], axis=0, keepdims=True)

    def work(masked):
        def step(index, acc):
            base = pl.multiple_of(index * chunk, chunk)
            span = pl.ds(base, chunk)
            score = jnp.dot(k_rows[span, :], queries, preferred_element_type=F32)
            weights = jnp.exp(score - log_total)
            if masked:
                allowed = allowed_keys(base, flips[0], chunk, rows, first)
                weights = jnp.where(allowed, weights, 0.0)
            grad_weights = jnp.dot(v_rows[span, :], grads, preferred_element_type=F32)
            grad_score = (weights * (grad_weights - delta)).astype(BF)
            dv_ref[:, span] += dg(grads, weights.astype(BF), ((1,), (1,)))
            dk_ref[:, span] += dg(queries, grad_score, ((1,), (1,)))
            return acc + jnp.dot(k_ref[:, span], grad_score, preferred_element_type=F32)

        return step

    acc = jnp.zeros(queries.shape, F32)
    acc = lax.fori_loop(ranges[tile, 0], ranges[tile, 1], work(True), acc)
    acc = lax.fori_loop(ranges[tile, 1], ranges[tile, 2], work(False), acc)
    dq_ref[...] = lax.fori_loop(ranges[tile, 2], ranges[tile, 3], work(True), acc).astype(BF)


def attend_back(queries, keys, values, rows, first, flip, out, log_total, grads, tile=512, chunk=1024):
    count, total = queries.shape[1], keys.shape[1]
    tile = min(tile, count)
    chunk = min(chunk, total)
    ranges = tile_ranges(rows, first, tile, chunk)
    whole = lambda i, r, f: (0, 0)
    part = lambda i, r, f: (0, i)
    return pl.pallas_call(
        functools.partial(attend_back_kernel, chunk=chunk),
        grid_spec=pltpu.PrefetchScalarGridSpec(
            num_scalar_prefetch=2,
            grid=(count // tile,),
            in_specs=[
                pl.BlockSpec((HEAD_DIM, tile), part),
                pl.BlockSpec((HEAD_DIM, total), whole),
                pl.BlockSpec((HEAD_DIM, total), whole),
                pl.BlockSpec((1, tile), part),
                pl.BlockSpec((1, tile), part),
                pl.BlockSpec((HEAD_DIM, tile), part),
                pl.BlockSpec((1, tile), part),
                pl.BlockSpec((HEAD_DIM, tile), part),
            ],
            out_specs=[
                pl.BlockSpec((HEAD_DIM, tile), part),
                pl.BlockSpec((HEAD_DIM, total), whole),
                pl.BlockSpec((HEAD_DIM, total), whole),
            ],
            scratch_shapes=[pltpu.VMEM((total, HEAD_DIM), BF), pltpu.VMEM((total, HEAD_DIM), BF)],
        ),
        out_shape=[
            jax.ShapeDtypeStruct((HEAD_DIM, count), BF),
            jax.ShapeDtypeStruct((HEAD_DIM, total), F32),
            jax.ShapeDtypeStruct((HEAD_DIM, total), F32),
        ],
        compiler_params=pltpu.CompilerParams(vmem_limit_bytes=48 << 20),
        name="attend_back",
    )(ranges, flip.reshape(1), queries, keys, values, rows.reshape(1, -1), first.reshape(1, -1), out, log_total, grads)


EPSILON = 1e-05
SWAP = [(0, 1), (1, 0)]


def over_x(value):
    return lax.ppermute(value, "tp", SWAP)


def over_blk(value, bit):
    return lax.ppermute(value, "blk", [(i, i ^ bit) for i in range(lax.axis_size("blk"))])


def normalize(values):
    centre = values - jnp.mean(values, axis=-1, keepdims=True)
    spread = lax.rsqrt(jnp.mean(centre * centre, axis=-1, keepdims=True) + EPSILON)
    return centre * spread, spread


def norm_back(values, gain, grad):
    hat, spread = normalize(values)
    scaled = grad * gain
    through = spread * (
        scaled
        - jnp.mean(scaled, axis=-1, keepdims=True)
        - hat * jnp.mean(scaled * hat, axis=-1, keepdims=True)
    )
    return through, jnp.sum(grad * hat, axis=0), jnp.sum(grad, axis=0)


def clip_rows(positions, clip_lengths):
    index = jnp.arange(clip_lengths.shape[0], dtype=jnp.int32)
    starts = jnp.sum(jnp.where(index[None, :] < index[:, None], clip_lengths[None, :], 0), axis=1)
    ends = starts + clip_lengths
    segment = jnp.sum((positions[:, None] >= ends[None, :]).astype(jnp.int32), axis=1)
    match = segment[:, None] == index[None, :]
    first = jnp.sum(jnp.where(match, starts[None, :], 0), axis=1)
    return segment, first


def matmul(left, right):
    return jnp.dot(left, right, preferred_element_type=F32)


def matmul_nt(left, right):
    return dg(left, right, ((1,), (1,)))


def matmul_tn(left, right):
    return dg(left, right, ((0,), (0,)))


def other_half(weight, core):
    rows = weight.shape[0] // 2
    sent = lax.dynamic_slice_in_dim(weight, core * rows, rows, 0)
    got = over_x(sent)
    more = over_blk(got, 1)
    return jnp.concatenate([jnp.where(core == 0, got, more), jnp.where(core == 0, more, got)])


def in_order(own, other, tp):
    return jnp.concatenate([jnp.where(tp == 0, own, other), jnp.where(tp == 0, other, own)])


def shards(
    frames,
    clip_lengths,
    text_states,
    text_segments,
    gain_one,
    shift_one,
    gain_two,
    shift_two,
    gain_three,
    shift_three,
    query_weight,
    key_weight,
    value_weight,
    output_weight,
    cross_query,
    cross_key,
    cross_value,
    cross_output,
    inner_weight,
    outer_weight,
    cotangent,
):
    row_count = frames.shape[0]
    width_here = query_weight.shape[1]
    heads_here = width_here // HEAD_DIM
    blk_count, tp_count = lax.axis_size("blk"), lax.axis_size("tp")
    blk, tp = lax.axis_index("blk"), lax.axis_index("tp")
    core = blk % 2
    copies = blk_count // heads_here
    sub = row_count // copies
    half = row_count // tp_count
    mine = blk % copies
    scale = float(HEAD_DIM) ** (-0.5)

    def own_rows(array):
        return lax.dynamic_slice_in_dim(array, tp * half, half, 0)

    def other_rows(array):
        return lax.dynamic_slice_in_dim(array, (1 - tp) * half, half, 0)

    inputs = frames.astype(F32)
    hat, _ = normalize(inputs)
    normed_one = (hat * gain_one + shift_one).astype(BF)
    q_t = (dg(query_weight, normed_one, ((0,), (1,))) * scale).astype(BF)
    k_t = dg(key_weight, normed_one, ((0,), (1,))).astype(BF)
    v_t = dg(value_weight, normed_one, ((0,), (1,))).astype(BF)

    weights_two = [output_weight, cross_query, cross_output]
    output_both, query_both, cross_both = [[w, other_half(w, core)] for w in weights_two]
    text_k = matmul(text_states, cross_key).astype(BF)
    text_v = matmul(text_states, cross_value).astype(BF)
    text_other = over_x(jnp.stack([text_k, text_v]))
    text_keys, text_values = [text_k, text_other[0]], [text_v, text_other[1]]

    def spread_heads(array):
        count = array.shape[0]
        array = array.reshape(count, heads_here, HEAD_DIM, copies, sub).transpose(1, 3, 0, 2, 4)
        return lax.all_to_all(
            array.reshape(blk_count, count, HEAD_DIM, sub), "blk", 0, 0, tiled=True
        )

    def bring_heads(array):
        got = lax.all_to_all(array, "blk", 0, 0, tiled=True)
        return got.reshape(heads_here, copies, array.shape[1], HEAD_DIM, sub)

    got = spread_heads(jnp.stack([q_t, k_t, v_t]))
    queries = got[:, 0].transpose(1, 0, 2).reshape(HEAD_DIM, blk_count * sub)
    both = got[:, 1:][:, :, :, None, :]
    bit = 1
    while bit < copies:
        both = jnp.concatenate([both, over_blk(both, bit)], axis=3)
        bit *= 2
    both = both.transpose(1, 2, 0, 3, 4).reshape(2, HEAD_DIM, blk_count * row_count)
    keys, values = both[0], both[1]
    rows_all = jnp.arange(blk_count, dtype=jnp.int32)[:, None] * row_count
    rows_all = (rows_all + mine * sub + jnp.arange(sub, dtype=jnp.int32)[None, :]).reshape(-1)
    _, first = clip_rows(rows_all, clip_lengths)
    flip = mine * sub
    out, log_total = attend(queries, keys, values, rows_all, first, flip)
    out_low = out.astype(BF).reshape(HEAD_DIM, blk_count, sub).transpose(1, 0, 2)[:, None]
    attended = bring_heads(out_low)[:, :, 0]

    def token_half(array, which):
        array = array.reshape(heads_here, tp_count, copies // tp_count, HEAD_DIM, sub)
        array = lax.dynamic_index_in_dim(array, which, 1, keepdims=False)
        return array.transpose(0, 2, 1, 3).reshape(width_here, half)

    a_own, a_sent = token_half(attended, tp), token_half(attended, 1 - tp)
    a_both = [a_own, over_x(a_sent)]

    rows = blk * row_count + tp * half + jnp.arange(half, dtype=jnp.int32)
    segment, _ = clip_rows(rows, clip_lengths)
    x_own = own_rows(frames).astype(F32)
    first_sum = x_own + matmul_tn(a_both[0], output_both[0]) + matmul_tn(a_both[1], output_both[1])
    hat, _ = normalize(first_sum)
    normed_two = (hat * gain_two + shift_two).astype(BF)
    allowed_text = text_segments[:, None] == segment[None, :]
    second_sum = first_sum
    crossed, cross_outs, cross_weights, cross_qs = [], [], [], []
    for side in range(2):
        qc = (matmul(normed_two, query_both[side]) * scale).astype(BF)
        qh = qc.reshape(half, heads_here, HEAD_DIM)
        kh = text_keys[side].reshape(-1, heads_here, HEAD_DIM)
        vh = text_values[side].reshape(-1, heads_here, HEAD_DIM)
        score = jnp.einsum("khd,qhd->hkq", kh, qh, preferred_element_type=F32)
        score = jnp.where(allowed_text[None], score, NEGATIVE)
        expo = jnp.exp(score - jnp.max(score, axis=1, keepdims=True))
        expo = jnp.where(allowed_text[None], expo, 0.0)
        weights = expo / jnp.sum(expo, axis=1, keepdims=True)
        oc = jnp.einsum("hkq,khd->qhd", weights.astype(BF), vh, preferred_element_type=F32)
        c = oc.reshape(half, width_here).astype(BF)
        second_sum = second_sum + matmul(c, cross_both[side])
        crossed.append(c), cross_outs.append(oc), cross_weights.append(weights), cross_qs.append(qh)
    hat, _ = normalize(second_sum)
    h3_own = (hat * gain_three + shift_three).astype(BF)

    h3_all = jnp.concatenate([h3_own, over_x(h3_own)])
    dy_own = own_rows(cotangent)
    dy_all = jnp.concatenate([dy_own, other_rows(cotangent)])
    hidden_pre = matmul(h3_all, inner_weight)
    hidden_grad = matmul_nt(dy_all, outer_weight)
    cdf = 0.5 * (1.0 + lax.erf(hidden_pre * (0.5**0.5)))
    density = jnp.exp(-0.5 * hidden_pre * hidden_pre) * 0.3989422804014327
    hidden = (hidden_pre * cdf).astype(BF)
    grad_pre = (hidden_grad * (cdf + hidden_pre * density)).astype(BF)
    dh3 = matmul_nt(grad_pre, inner_weight).astype(BF)
    dh3_own = dh3[:half].astype(F32) + over_x(dh3[half:]).astype(F32)
    y = matmul(hidden, outer_weight)
    y_own = second_sum + y[:half] + over_x(y[half:].astype(BF)).astype(F32)
    y_own = y_own.astype(BF)
    result = in_order(y_own, over_x(y_own), tp)
    grad_outer = matmul_tn(hidden, dy_all).astype(BF)
    grad_inner = matmul_tn(h3_all, grad_pre).astype(BF)

    through, grad_gain_three, grad_shift_three = norm_back(second_sum, gain_three, dh3_own)
    dx2 = dy_own.astype(F32) + through
    dx2_low = dx2.astype(BF)
    dh2 = 0.0
    dqcs, dk_parts, dv_parts = [], [], []
    for side in range(2):
        kh = text_keys[side].reshape(-1, heads_here, HEAD_DIM)
        vh = text_values[side].reshape(-1, heads_here, HEAD_DIM)
        dc = matmul_nt(dx2_low, cross_both[side]).astype(BF).reshape(half, heads_here, HEAD_DIM)
        delta = jnp.sum(dc.astype(F32) * cross_outs[side], axis=-1).T
        dweights = jnp.einsum("khd,qhd->hkq", vh, dc, preferred_element_type=F32)
        dscore = (cross_weights[side] * (dweights - delta[:, None, :])).astype(BF)
        dqc = jnp.einsum("hkq,khd->qhd", dscore, kh, preferred_element_type=F32).astype(BF)
        dqc = (dqc * scale).reshape(half, width_here)
        dk_parts.append(jnp.einsum("hkq,qhd->khd", dscore, cross_qs[side], preferred_element_type=F32))
        dv_parts.append(
            jnp.einsum("hkq,qhd->khd", cross_weights[side].astype(BF), dc, preferred_element_type=F32)
        )
        dh2 = dh2 + matmul_nt(dqc, query_both[side])
        dqcs.append(dqc)
    through, grad_gain_two, grad_shift_two = norm_back(first_sum, gain_two, dh2)
    dx1 = dx2 + through
    dx1_low = dx1.astype(BF)
    da_t = [dg(w, dx1_low, ((1,), (1,))).astype(BF) for w in output_both]
    da_other = over_x(da_t[1])

    def as_heads(array):
        return array.reshape(heads_here, HEAD_DIM, copies // tp_count, sub).transpose(0, 2, 1, 3)

    low = jnp.where(tp == 0, as_heads(da_t[0]), as_heads(da_other))
    high = jnp.where(tp == 0, as_heads(da_other), as_heads(da_t[0]))
    sent = jnp.concatenate([low, high], axis=1).reshape(blk_count, 1, HEAD_DIM, sub)
    grads = lax.all_to_all(sent, "blk", 0, 0, tiled=True)[:, 0]
    grads = grads.transpose(1, 0, 2).reshape(HEAD_DIM, blk_count * sub)
    dq, dk, dv = attend_back(queries, keys, values, rows_all, first, flip, out, log_total, grads)
    parts = jnp.stack([dk, dv]).reshape(2, HEAD_DIM, blk_count, copies, sub)
    bit = copies // 2
    while bit:
        split = parts.reshape(2, HEAD_DIM, blk_count, 2, bit, sub)
        parts = split[:, :, :, 0] + over_blk(split[:, :, :, 1].astype(BF), bit).astype(F32)
        bit //= 2
    parts = parts.reshape(2, HEAD_DIM, blk_count, sub).transpose(2, 0, 1, 3).astype(BF)
    dq_part = dq.reshape(HEAD_DIM, blk_count, sub).transpose(1, 0, 2)[:, None]
    back = bring_heads(jnp.concatenate([dq_part, parts], axis=1))
    back = back.transpose(2, 0, 3, 1, 4).reshape(3, width_here, row_count)
    dq_t, dk_t, dv_t = back[0] * jnp.asarray(scale, BF), back[1], back[2]
    dh1 = (
        dg(dq_t, query_weight, ((0,), (1,)))
        + dg(dk_t, key_weight, ((0,), (1,)))
        + dg(dv_t, value_weight, ((0,), (1,)))
    ).astype(BF)
    dh1_own = own_rows(dh1).astype(F32) + over_x(other_rows(dh1)).astype(F32)
    through, grad_gain_one, grad_shift_one = norm_back(x_own, gain_one, dh1_own)
    dx = (dx1 + through).astype(BF)
    grad_frames = in_order(dx, over_x(dx), tp)

    grad_query = dg(normed_one, dq_t, ((0,), (1,))).astype(BF)
    grad_key = dg(normed_one, dk_t, ((0,), (1,))).astype(BF)
    grad_value = dg(normed_one, dv_t, ((0,), (1,))).astype(BF)
    dx1_other = over_x(dx1_low)
    grad_output = (matmul(a_own, dx1_low) + matmul(a_sent, dx1_other)).astype(BF)
    dx2_other = over_x(dx2_low)
    c_other = over_x(crossed[1])
    grad_cross_output = (
        matmul_tn(crossed[0], dx2_low) + matmul_tn(c_other, dx2_other)
    ).astype(BF)
    h2_other = over_x(normed_two)
    dqc_other = over_x(dqcs[1])
    grad_cross_query = (matmul_tn(normed_two, dqcs[0]) + matmul_tn(h2_other, dqc_other)).astype(BF)

    parts = [jnp.stack([dk_parts[i], dv_parts[i]]).reshape(2, -1, width_here) for i in range(2)]
    text_part = parts[0] + over_x(parts[1].astype(BF)).astype(F32)
    text_total = lax.psum(text_part, "blk").astype(BF)
    grad_cross_key = matmul_tn(text_states, text_total[0])
    grad_cross_value = matmul_tn(text_states, text_total[1])
    grad_text = matmul_nt(text_total[0], cross_key) + matmul_nt(text_total[1], cross_value)
    grad_text = grad_text.astype(BF)
    grad_text = grad_text.astype(F32) + over_x(grad_text).astype(F32)

    small = jnp.stack(
        [grad_gain_one, grad_shift_one, grad_gain_two, grad_shift_two, grad_gain_three, grad_shift_three]
    )
    small = lax.psum(small, ("blk", "tp"))
    grads = [
        grad_query, grad_key, grad_value, grad_output, grad_cross_query, grad_cross_output,
        grad_inner, grad_outer,
    ]
    grads = [g.astype(F32) for g in lax.psum(grads, "blk")]
    return (
        result,
        grad_frames,
        grad_text,
        small[0],
        small[1],
        small[2],
        small[3],
        small[4],
        small[5],
        grads[0],
        grads[1],
        grads[2],
        grads[3],
        grads[4],
        grad_cross_key,
        grad_cross_value,
        grads[5],
        grads[6],
        grads[7],
    )


def solution(mesh):
    return jax.shard_map(
        shards,
        mesh=mesh,
        in_specs=(
            P("blk", None),
            P(),
            P(),
            P(),
            P(),
            P(),
            P(),
            P(),
            P(),
            P(),
            P(None, "tp"),
            P(None, "tp"),
            P(None, "tp"),
            P("tp", None),
            P(None, "tp"),
            P(None, "tp"),
            P(None, "tp"),
            P("tp", None),
            P(None, "tp"),
            P("tp", None),
            P("blk", None),
        ),
        out_specs=(
            P("blk", None),
            P("blk", None),
            P(),
            P(),
            P(),
            P(),
            P(),
            P(),
            P(),
            P(None, "tp"),
            P(None, "tp"),
            P(None, "tp"),
            P("tp", None),
            P(None, "tp"),
            P(None, "tp"),
            P(None, "tp"),
            P("tp", None),
            P(None, "tp"),
            P("tp", None),
        ),
        check_vma=False,
    )
```

```python
import functools
import math
import jax
import jax.numpy as jnp
from jax import lax
from jax.experimental import pallas as pl
from jax.experimental.pallas import tpu as pltpu
from jax.sharding import PartitionSpec as P

HEAD_DIM = 64
NEGATIVE = -1e30
LARGE = 1 << 16
BF, F32 = jnp.bfloat16, jnp.float32


def lasting(microseconds):
    return pl.CostEstimate(flops=0, bytes_accessed=int(microseconds * 3.7e6), transcendentals=0)


def kernel_call(body, *, out_shape, **options):
    many = isinstance(out_shape, (list, tuple))
    outs = [
        pltpu.HBM(o.shape, o.dtype) if math.prod(o.shape) >= LARGE else o
        for o in (out_shape if many else [out_shape])
    ]
    call = pl.pallas_call(body, out_shape=outs if many else outs[0], **options)

    def run(*args):
        return call(
            *[
                pltpu.with_memory_space_constraint(a, pltpu.HBM) if a.size >= LARGE else a
                for a in args
            ]
        )

    return run


def dg(left, right, dims):
    return lax.dot_general(left, right, (dims, ((), ())), preferred_element_type=F32)


def tile_ranges(positions, first, tile, chunk):
    rows = positions.reshape(-1, tile)
    starts = first.reshape(-1, tile)
    low = jnp.min(starts, axis=1) // chunk
    high = jnp.max(rows, axis=1) // chunk + 1
    clear = jnp.clip((jnp.max(starts, axis=1) + chunk - 1) // chunk, low, high)
    stop = jnp.clip((jnp.min(rows, axis=1) + 1) // chunk, clear, high)
    return jnp.stack([low, clear, stop, high], axis=1)


def allowed_keys(base, flip, chunk, rows, first):
    keys = (base + lax.broadcasted_iota(jnp.int32, (chunk, rows.shape[1]), 0)) ^ flip
    return (keys <= rows) & (keys >= first)


def attend_kernel(ranges, flips, q_ref, k_ref, v_ref, row_ref, first_ref, out_ref, log_ref, k_rows, chunk):
    tile = pl.program_id(0)
    total = k_ref.shape[1]

    @pl.when(tile == 0)
    def _():
        for base in range(0, total, chunk):
            k_rows[base : base + chunk, :] = k_ref[:, base : base + chunk].T

    queries = q_ref[...]
    rows, first = row_ref[...], first_ref[...]
    width = queries.shape[1]

    def work(masked):
        def step(index, carry):
            best, total_weight, acc = carry
            base = pl.multiple_of(index * chunk, chunk)
            score = jnp.dot(k_rows[pl.ds(base, chunk), :], queries, preferred_element_type=F32)
            if masked:
                allowed = allowed_keys(base, flips[0], chunk, rows, first)
                score = jnp.where(allowed, score, NEGATIVE)
            new_best = jnp.maximum(best, jnp.max(score, axis=0, keepdims=True))
            expo = jnp.exp(score - new_best)
            if masked:
                expo = jnp.where(allowed, expo, 0.0)
            fade = jnp.exp(best - new_best)
            total_weight = total_weight * fade + jnp.sum(expo, axis=0, keepdims=True)
            acc = acc * fade + jnp.dot(
                v_ref[:, pl.ds(base, chunk)], expo.astype(BF), preferred_element_type=F32
            )
            return new_best, total_weight, acc

        return step

    carry = (
        jnp.full((1, width), NEGATIVE, F32),
        jnp.zeros((1, width), F32),
        jnp.zeros((HEAD_DIM, width), F32),
    )
    carry = lax.fori_loop(ranges[tile, 0], ranges[tile, 1], work(True), carry)
    carry = lax.fori_loop(ranges[tile, 1], ranges[tile, 2], work(False), carry)
    best, total_weight, acc = lax.fori_loop(ranges[tile, 2], ranges[tile, 3], work(True), carry)
    out_ref[...] = acc / total_weight
    log_ref[...] = best + jnp.log(total_weight)


def attend(queries, keys, values, rows, first, flip, tile=512, chunk=1024):
    count, total = queries.shape[1], keys.shape[1]
    tile = min(tile, count)
    chunk = min(chunk, total)
    ranges = tile_ranges(rows, first, tile, chunk)
    whole = lambda i, r, f: (0, 0)
    part = lambda i, r, f: (0, i)
    return kernel_call(
        functools.partial(attend_kernel, chunk=chunk),
        grid_spec=pltpu.PrefetchScalarGridSpec(
            num_scalar_prefetch=2,
            grid=(count // tile,),
            in_specs=[
                pl.BlockSpec((HEAD_DIM, tile), part),
                pl.BlockSpec((HEAD_DIM, total), whole),
                pl.BlockSpec((HEAD_DIM, total), whole),
                pl.BlockSpec((1, tile), part),
                pl.BlockSpec((1, tile), part),
            ],
            out_specs=[pl.BlockSpec((HEAD_DIM, tile), part), pl.BlockSpec((1, tile), part)],
            scratch_shapes=[pltpu.VMEM((total, HEAD_DIM), BF)],
        ),
        out_shape=[
            jax.ShapeDtypeStruct((HEAD_DIM, count), F32),
            jax.ShapeDtypeStruct((1, count), F32),
        ],
        compiler_params=pltpu.CompilerParams(vmem_limit_bytes=(16 if total <= 4096 else 48) << 20),
        cost_estimate=lasting(15),
        name="attend",
    )(ranges, flip.reshape(1), queries, keys, values, rows.reshape(1, -1), first.reshape(1, -1))


def attend_back_kernel(
    ranges, flips, q_ref, k_ref, v_ref, row_ref, first_ref, out_ref, log_ref, do_ref,
    dq_ref, parts_ref, k_rows, v_rows, dk_ref, dv_ref, chunk,
):
    tile = pl.program_id(0)
    total = k_ref.shape[1]
    copies, blocks, _, _, sub = parts_ref.shape

    @pl.when(tile == 0)
    def _():
        for base in range(0, total, chunk):
            k_rows[base : base + chunk, :] = k_ref[:, base : base + chunk].T
            v_rows[base : base + chunk, :] = v_ref[:, base : base + chunk].T
        dk_ref[...] = jnp.zeros_like(dk_ref)
        dv_ref[...] = jnp.zeros_like(dv_ref)

    queries, grads = q_ref[...], do_ref[...]
    rows, first = row_ref[...], first_ref[...]
    log_total = log_ref[...]
    delta = jnp.sum(grads.astype(F32) * out_ref[...], axis=0, keepdims=True)

    def work(masked):
        def step(index, acc):
            base = pl.multiple_of(index * chunk, chunk)
            span = pl.ds(base, chunk)
            score = jnp.dot(k_rows[span, :], queries, preferred_element_type=F32)
            weights = jnp.exp(score - log_total)
            if masked:
                allowed = allowed_keys(base, flips[0], chunk, rows, first)
                weights = jnp.where(allowed, weights, 0.0)
            grad_weights = jnp.dot(v_rows[span, :], grads, preferred_element_type=F32)
            grad_score = (weights * (grad_weights - delta)).astype(BF)
            dv_ref[:, span] += dg(grads, weights.astype(BF), ((1,), (1,)))
            dk_ref[:, span] += dg(queries, grad_score, ((1,), (1,)))
            return acc + jnp.dot(k_ref[:, span], grad_score, preferred_element_type=F32)

        return step

    acc = jnp.zeros(queries.shape, F32)
    acc = lax.fori_loop(ranges[tile, 0], ranges[tile, 1], work(True), acc)
    acc = lax.fori_loop(ranges[tile, 1], ranges[tile, 2], work(False), acc)
    dq = lax.fori_loop(ranges[tile, 2], ranges[tile, 3], work(True), acc).astype(BF)
    for block in range(dq_ref.shape[0]):
        dq_ref[block] = dq[:, block * sub : (block + 1) * sub]

    @pl.when(tile == pl.num_programs(0) - 1)
    def _():
        for block in range(blocks):
            for copy in range(copies):
                at = (block * copies + copy) * sub
                parts_ref[copy, block, 0] = dk_ref[:, at : at + sub].astype(BF)
                parts_ref[copy, block, 1] = dv_ref[:, at : at + sub].astype(BF)


def attend_back(queries, keys, values, rows, first, flip, out, log_total, grads, sub, tile=512, chunk=1024):
    count, total = queries.shape[1], keys.shape[1]
    blocks, copies = count // sub, total // count
    tile = min(tile, count)
    chunk = min(chunk, total)
    ranges = tile_ranges(rows, first, tile, chunk)
    whole = lambda i, r, f: (0, 0)
    part = lambda i, r, f: (0, i)
    return kernel_call(
        functools.partial(attend_back_kernel, chunk=chunk),
        grid_spec=pltpu.PrefetchScalarGridSpec(
            num_scalar_prefetch=2,
            grid=(count // tile,),
            in_specs=[
                pl.BlockSpec((HEAD_DIM, tile), part),
                pl.BlockSpec((HEAD_DIM, total), whole),
                pl.BlockSpec((HEAD_DIM, total), whole),
                pl.BlockSpec((1, tile), part),
                pl.BlockSpec((1, tile), part),
                pl.BlockSpec((HEAD_DIM, tile), part),
                pl.BlockSpec((1, tile), part),
                pl.BlockSpec((HEAD_DIM, tile), part),
            ],
            out_specs=[
                pl.BlockSpec((tile // sub, HEAD_DIM, sub), lambda i, r, f: (i, 0, 0)),
                pl.BlockSpec((copies, blocks, 2, HEAD_DIM, sub), lambda i, r, f: (0, 0, 0, 0, 0)),
            ],
            scratch_shapes=[
                pltpu.VMEM((total, HEAD_DIM), BF),
                pltpu.VMEM((total, HEAD_DIM), BF),
                pltpu.VMEM((HEAD_DIM, total), F32),
                pltpu.VMEM((HEAD_DIM, total), F32),
            ],
        ),
        out_shape=[
            jax.ShapeDtypeStruct((blocks, HEAD_DIM, sub), BF),
            jax.ShapeDtypeStruct((copies, blocks, 2, HEAD_DIM, sub), BF),
        ],
        compiler_params=pltpu.CompilerParams(vmem_limit_bytes=(24 if total <= 4096 else 60) << 20),
        cost_estimate=lasting(17),
        name="attend_back",
    )(ranges, flip.reshape(1), queries, keys, values, rows.reshape(1, -1), first.reshape(1, -1), out, log_total, grads)


EPSILON = 1e-05
SWAP = [(0, 1), (1, 0)]


def after(values, token):
    return lax.optimization_barrier((values, token))[0]


def over_x(value):
    return lax.ppermute(value, "tp", SWAP)


def over_blk(value, bit):
    return lax.ppermute(value, "blk", [(i, i ^ bit) for i in range(lax.axis_size("blk"))])


def normalize(values):
    centre = values - jnp.mean(values, axis=-1, keepdims=True)
    spread = lax.rsqrt(jnp.mean(centre * centre, axis=-1, keepdims=True) + EPSILON)
    return centre * spread, spread


def norm_back(values, gain, grad):
    hat, spread = normalize(values)
    scaled = grad * gain
    through = spread * (
        scaled
        - jnp.mean(scaled, axis=-1, keepdims=True)
        - hat * jnp.mean(scaled * hat, axis=-1, keepdims=True)
    )
    return through, jnp.sum(grad * hat, axis=0), jnp.sum(grad, axis=0)


def clip_rows(positions, clip_lengths):
    index = jnp.arange(clip_lengths.shape[0], dtype=jnp.int32)
    starts = jnp.sum(jnp.where(index[None, :] < index[:, None], clip_lengths[None, :], 0), axis=1)
    ends = starts + clip_lengths
    segment = jnp.sum((positions[:, None] >= ends[None, :]).astype(jnp.int32), axis=1)
    match = segment[:, None] == index[None, :]
    first = jnp.sum(jnp.where(match, starts[None, :], 0), axis=1)
    return segment, first


def matmul(left, right):
    return jnp.dot(left, right, preferred_element_type=F32)


def matmul_nt(left, right):
    return dg(left, right, ((1,), (1,)))


def matmul_tn(left, right):
    return dg(left, right, ((0,), (0,)))


def first_hop(weight, core):
    return over_x(halves(weight, core))


def weld_kernel(core, *refs):
    count = len(refs) // 3
    for which in range(count):
        first, second, out = refs[which], refs[count + which], refs[2 * count + which]
        chosen = pl.program_id(0) == core[0]

        @pl.when(chosen)
        def _():
            out[...] = first[...]

        @pl.when(jnp.logical_not(chosen))
        def _():
            out[...] = second[...]


def weld(own, other, core):
    outs = [jax.ShapeDtypeStruct((2 * a.shape[0], a.shape[1]), a.dtype) for a in own]
    return kernel_call(
        weld_kernel,
        grid_spec=pltpu.PrefetchScalarGridSpec(
            num_scalar_prefetch=1,
            grid=(2,),
            in_specs=[whole_spec(a) for a in list(own) + list(other)],
            out_specs=[pl.BlockSpec(a.shape, lambda i, c: (i, 0)) for a in own],
        ),
        out_shape=outs,
        compiler_params=pltpu.CompilerParams(vmem_limit_bytes=24 << 20),
        cost_estimate=lasting(4),
        name="weld",
    )(core.reshape(1), *own, *other)


def in_order(own, other, tp):
    return jnp.concatenate([jnp.where(tp == 0, own, other), jnp.where(tp == 0, other, own)])


def whole_spec(array):
    shape = array.shape
    return pl.BlockSpec(shape, lambda *_: (0,) * len(shape))


def norm_rows(values):
    centre = values - jnp.mean(values, axis=-1, keepdims=True)
    spread = lax.rsqrt(jnp.mean(centre * centre, axis=-1, keepdims=True) + EPSILON)
    return centre * spread, spread


def norm_rows_back(values, gain, grad):
    hat, spread = norm_rows(values)
    scaled = grad * gain
    through = spread * (
        scaled
        - jnp.mean(scaled, axis=-1, keepdims=True)
        - hat * jnp.mean(scaled * hat, axis=-1, keepdims=True)
    )
    return through, jnp.sum(grad * hat, axis=0, keepdims=True), jnp.sum(grad, axis=0, keepdims=True)


def text_weights(keys, queries, allowed):
    score = dg(keys, queries, ((0,), (0,)))
    score = jnp.where(allowed, score, NEGATIVE)
    expo = jnp.exp(score - jnp.max(score, axis=0, keepdims=True))
    expo = jnp.where(allowed, expo, 0.0)
    return expo / jnp.sum(expo, axis=0, keepdims=True)


def cross_kernel(
    a_own, a_other, x_ref, gain_two, shift_two, gain_three, shift_three, wo_own, wo_other,
    wq_own, wq_other, wc_own, wc_other, tk_ref, tv_ref, segment, text_segment,
    x1_ref, x2_ref, h2_ref, h3_ref, q_ref, oc_ref, c_own, c_other, scale,
):
    width = a_own.shape[0]
    change = jnp.dot(a_own[...].T, wo_own[...], preferred_element_type=F32)
    change += jnp.dot(a_other[...].T, wo_other[...], preferred_element_type=F32)
    x1 = x_ref[...].astype(F32) + change
    x1_ref[...] = x1
    hat, _ = norm_rows(x1)
    h2 = (hat * gain_two[...] + shift_two[...]).astype(BF)
    h2_ref[...] = h2
    allowed = text_segment[...] == segment[...]
    crosses = []
    for side, wq in enumerate([wq_own, wq_other]):
        qc = (jnp.dot(h2, wq[...], preferred_element_type=F32) * scale).astype(BF)
        q_t = qc.T
        q_ref[side] = q_t
        parts = []
        for head in range(width // HEAD_DIM):
            span = slice(head * HEAD_DIM, (head + 1) * HEAD_DIM)
            weights = text_weights(tk_ref[side, span, :], q_t[span, :], allowed)
            parts.append(
                jnp.dot(tv_ref[side, span, :], weights.astype(BF), preferred_element_type=F32)
            )
        oc = jnp.concatenate(parts, axis=0)
        oc_ref[side] = oc
        crossed = oc.astype(BF)
        (c_own if side == 0 else c_other)[...] = crossed
        crosses.append(crossed.T)
    change = jnp.dot(crosses[0], wc_own[...], preferred_element_type=F32)
    change += jnp.dot(crosses[1], wc_other[...], preferred_element_type=F32)
    x2 = x1 + change
    x2_ref[...] = x2
    hat, _ = norm_rows(x2)
    h3_ref[...] = (hat * gain_three[...] + shift_three[...]).astype(BF)


def cross_forward(a_both, x_own, norms, output_both, query_both, cross_both, tk, tv, segment, text_segment, scale):
    half, depth = x_own.shape
    width = a_both[0].shape[0]
    args = [*a_both, x_own, *norms, *output_both, *query_both, *cross_both, tk, tv, segment, text_segment]
    shape = jax.ShapeDtypeStruct
    outs = [
        shape((half, depth), F32), shape((half, depth), F32), shape((half, depth), BF),
        shape((half, depth), BF), shape((2, width, half), BF), shape((2, width, half), F32),
        shape((width, half), BF), shape((width, half), BF),
    ]
    return kernel_call(
        functools.partial(cross_kernel, scale=scale),
        grid=(1,),
        in_specs=[whole_spec(a) for a in args],
        out_specs=[whole_spec(o) for o in outs],
        out_shape=outs,
        compiler_params=pltpu.CompilerParams(vmem_limit_bytes=28 << 20),
        cost_estimate=lasting(7),
        name="cross_forward",
    )(*args)


def cross_back_kernel(
    dh_own, dh_got, dy_ref, x1_ref, x2_ref, gain_two, gain_three, wo_own, wo_other,
    wq_own, wq_other, wc_own, wc_other, tk_ref, tv_ref, q_ref, oc_ref, segment, text_segment,
    dx1_ref, dx1_low_ref, dx2_low_ref, dq_own, dq_other, da_own, da_other, text_own, text_other,
    small_ref, scale,
):
    width = tk_ref.shape[1]
    dh3 = dh_own[...].astype(F32) + dh_got[...].astype(F32)
    through, gain_grad, shift_grad = norm_rows_back(x2_ref[...], gain_three[...], dh3)
    small_ref[2:3, :] = gain_grad
    small_ref[3:4, :] = shift_grad
    dx2 = dy_ref[...].astype(F32) + through
    low = dx2.astype(BF)
    dx2_low_ref[...] = low
    allowed = text_segment[...] == segment[...]
    dqs = []
    for side, wc in enumerate([wc_own, wc_other]):
        dc_t = dg(low, wc[...], ((1,), (1,))).astype(BF).T
        parts = []
        for head in range(width // HEAD_DIM):
            span = slice(head * HEAD_DIM, (head + 1) * HEAD_DIM)
            queries, grads = q_ref[side, span, :], dc_t[span, :]
            weights = text_weights(tk_ref[side, span, :], queries, allowed)
            delta = jnp.sum(grads.astype(F32) * oc_ref[side, span, :], axis=0, keepdims=True)
            grad_weights = dg(tv_ref[side, span, :], grads, ((0,), (0,)))
            grad_score = (weights * (grad_weights - delta)).astype(BF)
            dq = jnp.dot(tk_ref[side, span, :], grad_score, preferred_element_type=F32).astype(BF)
            parts.append(dq * jnp.asarray(scale, BF))
            text_ref = text_own if side == 0 else text_other
            text_ref[0, span, :] = dg(queries, grad_score, ((1,), (1,))).astype(text_ref.dtype)
            text_ref[1, span, :] = dg(grads, weights.astype(BF), ((1,), (1,))).astype(text_ref.dtype)
        dq = jnp.concatenate(parts, axis=0)
        (dq_own if side == 0 else dq_other)[...] = dq
        dqs.append(dq.T)
    dh2 = dg(dqs[0], wq_own[...], ((1,), (1,))) + dg(dqs[1], wq_other[...], ((1,), (1,)))
    through, gain_grad, shift_grad = norm_rows_back(x1_ref[...], gain_two[...], dh2)
    small_ref[0:1, :] = gain_grad
    small_ref[1:2, :] = shift_grad
    dx1 = dx2 + through
    dx1_ref[...] = dx1
    low = dx1.astype(BF)
    dx1_low_ref[...] = low
    for ref, wo in [(da_own, wo_own), (da_other, wo_other)]:
        ref[...] = dg(low, wo[...], ((1,), (1,))).astype(BF).T


def cross_backward(
    dh_own, dh_got, dy_own, x1, x2, gain_two, gain_three, output_both, query_both, cross_both,
    tk, tv, q_t, oc, segment, text_segment, scale,
):
    half, depth = x1.shape
    width, text = tk.shape[1], tk.shape[2]
    args = [
        dh_own, dh_got, dy_own, x1, x2, gain_two, gain_three, *output_both, *query_both,
        *cross_both, tk, tv, q_t, oc, segment, text_segment,
    ]
    shape = jax.ShapeDtypeStruct
    outs = [
        shape((half, depth), F32), shape((half, depth), BF), shape((half, depth), BF),
        *[shape((width, half), BF)] * 4, shape((2, width, text), F32), shape((2, width, text), BF),
        shape((4, depth), F32),
    ]
    return kernel_call(
        functools.partial(cross_back_kernel, scale=scale),
        grid=(1,),
        in_specs=[whole_spec(a) for a in args],
        out_specs=[whole_spec(o) for o in outs],
        out_shape=outs,
        compiler_params=pltpu.CompilerParams(vmem_limit_bytes=28 << 20),
        cost_estimate=lasting(9),
        name="cross_backward",
    )(*args)


def hidden_kernel(tp_ref, h_own, h_other, dy_ref, wi_ref, wo_ref, g_ref, du_ref, own_ref, other_ref, acc):
    step, half = pl.program_id(0), h_own.shape[0]
    tp = tp_ref[0]

    @pl.when(step == 0)
    def _():
        acc[...] = jnp.zeros_like(acc)

    for part, h_ref in enumerate([h_own, h_other]):
        rows = slice(part * half, (part + 1) * half)
        base = jnp.where(tp == part, 0, half)
        dy = dy_ref[pl.ds(pl.multiple_of(base, half), half), :]
        pre = jnp.dot(h_ref[...], wi_ref[...], preferred_element_type=F32)
        cdf = 0.5 * (1.0 + lax.erf(pre * (0.5**0.5)))
        density = jnp.exp(-0.5 * pre * pre) * 0.3989422804014327
        g_ref[rows, :] = (pre * cdf).astype(BF)
        grad = dg(dy, wo_ref[...], ((1,), (1,)))
        grad = (grad * (cdf + pre * density)).astype(BF)
        du_ref[rows, :] = grad
        acc[rows, :] += dg(grad, wi_ref[...], ((1,), (1,)))

    @pl.when(step == pl.num_programs(0) - 1)
    def _():
        own_ref[...] = acc[:half, :]
        other_ref[...] = acc[half:, :].astype(BF)


def hidden_pass(h_own, h_other, cotangent, inner, outer, tp, tile=512):
    half, depth = h_own.shape
    units = inner.shape[1]
    shape = jax.ShapeDtypeStruct
    return kernel_call(
        hidden_kernel,
        grid_spec=pltpu.PrefetchScalarGridSpec(
            num_scalar_prefetch=1,
            grid=(units // tile,),
            in_specs=[
                whole_spec(h_own), whole_spec(h_other), whole_spec(cotangent),
                pl.BlockSpec((depth, tile), lambda i, t: (0, i)),
                pl.BlockSpec((tile, depth), lambda i, t: (i, 0)),
            ],
            out_specs=[
                pl.BlockSpec((2 * half, tile), lambda i, t: (0, i)),
                pl.BlockSpec((2 * half, tile), lambda i, t: (0, i)),
                pl.BlockSpec((half, depth), lambda i, t: (0, 0)),
                pl.BlockSpec((half, depth), lambda i, t: (0, 0)),
            ],
            scratch_shapes=[pltpu.VMEM((2 * half, depth), F32)],
        ),
        out_shape=[
            shape((2 * half, units), BF), shape((2 * half, units), BF),
            shape((half, depth), F32), shape((half, depth), BF),
        ],
        compiler_params=pltpu.CompilerParams(vmem_limit_bytes=20 << 20),
        cost_estimate=lasting(10),
        name="hidden_pass",
    )(tp.reshape(1), h_own, h_other, cotangent, inner, outer)


def hidden_grads_kernel(
    place, h_own, h_other, dy_ref, g_ref, du_ref, wo_ref, both_ref, y_own, y_other, h_all, dy_all, acc
):
    step, half = pl.program_id(0), h_own.shape[0]
    tp = place[0]

    @pl.when(step == 0)
    def _():
        acc[...] = jnp.zeros_like(acc)
        h_all[:half, :] = h_own[...]
        h_all[half:, :] = h_other[...]
        for part in range(2):
            base = jnp.where(tp == part, 0, half)
            dy_all[part * half : (part + 1) * half, :] = dy_ref[
                pl.ds(pl.multiple_of(base, half), half), :
            ]

    acc[...] += jnp.dot(g_ref[...], wo_ref[...], preferred_element_type=F32)
    depth = h_own.shape[1]
    both_ref[:, :depth] = jnp.dot(g_ref[...].T, dy_all[...], preferred_element_type=F32).astype(BF)
    both_ref[:, depth:] = jnp.dot(du_ref[...].T, h_all[...], preferred_element_type=F32).astype(BF)

    @pl.when(step == pl.num_programs(0) - 1)
    def _():
        y_own[...] = acc[:half, :]
        y_other[...] = acc[half:, :].astype(BF)


def hidden_grads(h_own, h_other, cotangent, g, du, outer, tp, tile=256):
    half, depth = h_own.shape
    units = outer.shape[0]
    shape = jax.ShapeDtypeStruct
    across = lambda i, p: (0, i)
    down = lambda i, p: (i, 0)
    still = lambda i, p: (0, 0)
    return kernel_call(
        hidden_grads_kernel,
        grid_spec=pltpu.PrefetchScalarGridSpec(
            num_scalar_prefetch=1,
            grid=(units // tile,),
            in_specs=[
                whole_spec(h_own), whole_spec(h_other), whole_spec(cotangent),
                pl.BlockSpec((2 * half, tile), across), pl.BlockSpec((2 * half, tile), across),
                pl.BlockSpec((tile, depth), down),
            ],
            out_specs=[
                pl.BlockSpec((tile, 2 * depth), down),
                pl.BlockSpec((half, depth), still), pl.BlockSpec((half, depth), still),
            ],
            scratch_shapes=[
                pltpu.VMEM((2 * half, depth), BF),
                pltpu.VMEM((2 * half, depth), BF),
                pltpu.VMEM((2 * half, depth), F32),
            ],
        ),
        out_shape=[
            shape((units, 2 * depth), BF), shape((half, depth), F32), shape((half, depth), BF),
        ],
        compiler_params=pltpu.CompilerParams(vmem_limit_bytes=20 << 20),
        cost_estimate=lasting(9),
        name="hidden_grads",
    )(tp.reshape(1), h_own, h_other, cotangent, g, du, outer)


def hidden_out_kernel(both_ref, outer_ref, inner_ref):
    depth = outer_ref.shape[1]
    outer_ref[...] = both_ref[:, :depth].astype(F32)
    inner_ref[...] = both_ref[:, depth:].astype(F32).T


def hidden_out(both, tile=256):
    units, depth = both.shape[0], both.shape[1] // 2
    return kernel_call(
        hidden_out_kernel,
        grid=(units // tile,),
        in_specs=[pl.BlockSpec((tile, 2 * depth), lambda i: (i, 0))],
        out_specs=[
            pl.BlockSpec((tile, depth), lambda i: (i, 0)), pl.BlockSpec((depth, tile), lambda i: (0, i))
        ],
        out_shape=[
            jax.ShapeDtypeStruct((units, depth), F32), jax.ShapeDtypeStruct((depth, units), F32)
        ],
        compiler_params=pltpu.CompilerParams(vmem_limit_bytes=16 << 20),
        cost_estimate=lasting(9),
        name="hidden_out",
    )(both)


def pair_grads_kernel(core, *refs):
    send, keep = refs[-2:]
    ins = refs[:-2]
    rows = send.shape[0]
    for which in range(len(ins) // 4):
        left_own, left_other, right_own, right_other = ins[4 * which : 4 * which + 4]
        depth = right_own.shape[1]
        for ref, side in [(send, 1 - core[0]), (keep, core[0])]:
            span = pl.ds(pl.multiple_of(side * rows, rows), rows)
            total = jnp.dot(left_own[span, :], right_own[...], preferred_element_type=F32)
            total += jnp.dot(left_other[span, :], right_other[...], preferred_element_type=F32)
            ref[:, which * depth : (which + 1) * depth] = total.astype(BF)


def pair_grads(groups, core):
    args = [array for group in groups for array in group]
    features, depth = groups[0][0].shape[0], groups[0][2].shape[1]
    columns = depth * len(groups)
    out = jax.ShapeDtypeStruct((features // 2, columns), BF)
    return kernel_call(
        pair_grads_kernel,
        grid_spec=pltpu.PrefetchScalarGridSpec(
            num_scalar_prefetch=1,
            grid=(1,),
            in_specs=[whole_spec(a) for a in args],
            out_specs=[whole_spec(out), whole_spec(out)],
        ),
        out_shape=[out, out],
        compiler_params=pltpu.CompilerParams(vmem_limit_bytes=24 << 20),
        cost_estimate=lasting(4),
        name="pair_grads",
    )(core.reshape(1), *args)


def fold_kernel(sides, *refs):
    count = len(refs) // 4
    ins, outs = refs[: 2 * count], refs[2 * count :]
    first = pl.program_id(0) < pl.num_programs(0) // 2
    for which in range(count):
        total = ins[2 * which][...].astype(F32) + ins[2 * which + 1][...].astype(F32)
        total = total.astype(BF)

        @pl.when(first)
        def _():
            outs[2 * which][...] = total

        @pl.when(jnp.logical_not(first))
        def _():
            outs[2 * which + 1][...] = total


def fold(pairs, sides):
    least = min(keep.shape[0] for keep, _ in pairs)
    if least % 16:
        sums = [(keep.astype(F32) + got.astype(F32)).astype(BF) for keep, got in pairs]
        return [(halves(t, 1 - side), halves(t, side)) for t, side in zip(sums, sides)]
    parts = 2 if least % 32 == 0 else 1
    args, in_specs, out_specs, outs = [], [], [], []
    for which, (keep, got) in enumerate(pairs):
        rows, columns = keep.shape
        block = rows // (2 * parts)
        place = lambda i, s, which=which: (
            jnp.where(i < parts, (1 - s[which]) * parts + i, s[which] * parts + i - parts), 0
        )
        args += [keep, got]
        in_specs += [pl.BlockSpec((block, columns), place)] * 2
        out_specs += [
            pl.BlockSpec((block, columns), lambda i, s: (jnp.minimum(i, parts - 1), 0)),
            pl.BlockSpec((block, columns), lambda i, s: (jnp.maximum(i - parts, 0), 0)),
        ]
        outs += [jax.ShapeDtypeStruct((rows // 2, columns), BF)] * 2
    got = kernel_call(
        fold_kernel,
        grid_spec=pltpu.PrefetchScalarGridSpec(
            num_scalar_prefetch=1,
            grid=(2 * parts,),
            in_specs=in_specs,
            out_specs=out_specs,
        ),
        out_shape=outs,
        compiler_params=pltpu.CompilerParams(vmem_limit_bytes=12 << 20),
        cost_estimate=lasting(3),
        name="fold",
    )(jnp.stack(sides), *args)
    return [(got[2 * i], got[2 * i + 1]) for i in range(len(pairs))]


def piece_places(count, order):
    places = []
    for device in range(count):
        index = 0
        for bit in order:
            index = index * 2 + (device // bit) % 2
        places.append(index)
    return places


def widen_kernel(places, in_ref, *out_refs, rows_of, head_count):
    columns = in_ref.shape[2]
    for slot in range(in_ref.shape[0]):
        device = pl.program_id(0) * in_ref.shape[0] + slot
        for kind, outs in enumerate([out_refs[:head_count], out_refs[head_count:]]):
            rows = rows_of[kind]
            start = pl.multiple_of(places[kind, device] * rows, rows)
            place = pl.ds(start, rows)
            at = 0
            for out_ref in outs:
                filled = 0
                while filled < out_ref.shape[1]:
                    part, column = divmod(at, columns)
                    count = min(columns - column, out_ref.shape[1] - filled)
                    row = part * rows + kind * rows_of[0]
                    out_ref[place, filled : filled + count] = in_ref[
                        slot, row : row + rows, column : column + count
                    ].astype(F32)
                    filled, at = filled + count, at + count


def widen(gathered, orders, rows_of, head_widths, pair_widths):
    count, rows, columns = gathered.shape
    outs = [jax.ShapeDtypeStruct((count * rows_of[0], width), F32) for width in head_widths]
    outs += [jax.ShapeDtypeStruct((count * rows_of[1], width), F32) for width in pair_widths]
    places = jnp.asarray([piece_places(count, order) for order in orders], jnp.int32)
    return kernel_call(
        functools.partial(widen_kernel, rows_of=rows_of, head_count=len(head_widths)),
        grid_spec=pltpu.PrefetchScalarGridSpec(
            num_scalar_prefetch=1,
            grid=(4,),
            in_specs=[pl.BlockSpec((count // 4, rows, columns), lambda j, p: (j, 0, 0))],
            out_specs=[whole_spec(out) for out in outs],
        ),
        out_shape=outs,
        compiler_params=pltpu.CompilerParams(vmem_limit_bytes=40 << 20),
        cost_estimate=lasting(8),
        name="widen",
    )(places, gathered)


class Stream:
    def __init__(self, send, keep, order, blk):
        self.order, self.blk, self.phase, self.keep = order, blk, 0, keep
        self.got, self.sent = over_blk(send, order[0]), send

    def step(self):
        count, phase = len(self.order), self.phase
        if phase is None:
            return
        self.phase += 1
        if phase < count - 1:
            bit = self.order[phase + 1]
            ((send, self.keep),) = fold([(self.keep, self.got)], [(self.blk // bit) % 2])
            self.got, self.sent = over_blk(send, bit), send
        elif phase < 2 * count - 1:
            if phase == count - 1:
                piece = self.keep.astype(F32) + self.got.astype(F32)
                self.keep = piece.astype(BF)[None]
            else:
                self.keep = join(self.keep, self.got)
            self.got, self.sent = over_blk(self.keep, self.order[2 * count - 2 - phase]), self.keep
            if phase == 2 * count - 2:
                self.phase = None

    def piece(self):
        return (self.keep.astype(F32) + self.got.astype(F32)).astype(BF)

    def result(self, widths):
        return unpack(self.keep, self.got, self.order, widths)


class Butterfly:
    def __init__(self, value, order, wire):
        self.value, self.order, self.phase, self.wire = value, order, 0, wire
        self.got, self.sent = over_blk(value.astype(wire), order[0]), value

    def step(self):
        if self.phase is None:
            return
        self.value = self.value + self.got.astype(F32)
        self.phase += 1
        if self.phase < len(self.order):
            self.got = over_blk(self.value.astype(self.wire), self.order[self.phase])
            self.sent = self.value
        else:
            self.got, self.phase = jnp.zeros((), F32), None


def meet(streams, others):
    got, others = lax.optimization_barrier(([s.got for s in streams], others))
    for stream, value in zip(streams, got):
        stream.got = value
    return others


def project_back_kernel(tp, back_ref, *refs):
    weights, (own_ref, other_ref) = refs[:3], refs[3:]
    half = own_ref.shape[0]
    total = None
    for which, weight in enumerate(weights):
        part = dg(back_ref[which].T, weight[...], ((1,), (1,)))
        total = part if total is None else total + part
    first, second = total[:half, :], total[half:, :]
    own_ref[...] = jnp.where(tp[0] == 0, first, second)
    other_ref[...] = jnp.where(tp[0] == 0, second, first).astype(BF)


def project_back(back, weights, tp):
    rows, depth = back.shape[2], weights[0].shape[0]
    args = [back, *weights]
    outs = [
        jax.ShapeDtypeStruct((rows // 2, depth), F32), jax.ShapeDtypeStruct((rows // 2, depth), BF)
    ]
    return kernel_call(
        project_back_kernel,
        grid_spec=pltpu.PrefetchScalarGridSpec(
            num_scalar_prefetch=1,
            grid=(1,),
            in_specs=[whole_spec(a) for a in args],
            out_specs=[whole_spec(o) for o in outs],
        ),
        out_shape=outs,
        compiler_params=pltpu.CompilerParams(vmem_limit_bytes=16 << 20),
        cost_estimate=lasting(4),
        name="project_back",
    )(tp.reshape(1), *args)


def head_grads_kernel(core, back_ref, rows_ref, send, keep, turned):
    turned[...] = rows_ref[...].T
    rows, width = send.shape[0], back_ref.shape[1]
    for ref, side in [(send, 1 - core[0]), (keep, core[0])]:
        part = turned[pl.ds(pl.multiple_of(side * rows, rows), rows), :]
        for which in range(3):
            ref[:, which * width : (which + 1) * width] = dg(
                part, back_ref[which], ((1,), (1,))
            ).astype(BF)


def head_grads(back, normed, core):
    rows, depth = normed.shape
    out = jax.ShapeDtypeStruct((depth // 2, 3 * back.shape[1]), BF)
    return kernel_call(
        head_grads_kernel,
        grid_spec=pltpu.PrefetchScalarGridSpec(
            num_scalar_prefetch=1,
            grid=(1,),
            in_specs=[whole_spec(back), whole_spec(normed)],
            out_specs=[whole_spec(out), whole_spec(out)],
            scratch_shapes=[pltpu.VMEM((depth, rows), BF)],
        ),
        out_shape=[out, out],
        compiler_params=pltpu.CompilerParams(vmem_limit_bytes=16 << 20),
        cost_estimate=lasting(4),
        name="head_grads",
    )(core.reshape(1), back, normed)


def combine_kernel(dq_ref, parts_ref, got_ref, out_ref, scale):
    out_ref[:, 0] = dq_ref[...] * jnp.asarray(scale, BF)
    out_ref[:, 1:] = (parts_ref[0].astype(F32) + got_ref[...].astype(F32)).astype(BF)


def combine(dq, parts, got, scale):
    blocks, _, sub = dq.shape
    part = min(4, blocks)
    return kernel_call(
        functools.partial(combine_kernel, scale=scale),
        grid=(blocks // part,),
        in_specs=[
            pl.BlockSpec((part, HEAD_DIM, sub), lambda i: (i, 0, 0)),
            pl.BlockSpec((1, part, 2, HEAD_DIM, sub), lambda i: (0, i, 0, 0, 0)),
            pl.BlockSpec((part, 2, HEAD_DIM, sub), lambda i: (i, 0, 0, 0)),
        ],
        out_specs=pl.BlockSpec((part, 3, HEAD_DIM, sub), lambda i: (i, 0, 0, 0)),
        out_shape=jax.ShapeDtypeStruct((blocks, 3, HEAD_DIM, sub), BF),
        cost_estimate=lasting(3.5),
        name="combine",
    )(dq, parts, got)


def join_kernel(low_ref, high_ref, out_ref):
    for part, ref in enumerate([low_ref, high_ref]):

        @pl.when(pl.program_id(0) == part)
        def _():
            out_ref[...] = ref[...]


def join(low, high):
    shape = low.shape
    still = lambda i: (0,) * len(shape)
    return kernel_call(
        join_kernel,
        grid=(2,),
        in_specs=[pl.BlockSpec(shape, still)] * 2,
        out_specs=pl.BlockSpec(shape, lambda i: (i,) + (0,) * (len(shape) - 1)),
        out_shape=jax.ShapeDtypeStruct((2 * shape[0],) + shape[1:], low.dtype),
        compiler_params=pltpu.CompilerParams(vmem_limit_bytes=12 << 20),
        cost_estimate=lasting(2),
        name="join",
    )(low, high)


def halves(value, which):
    rows = value.shape[0] // 2
    return lax.dynamic_slice_in_dim(value, which * rows, rows, 0)


def piece_index(order):
    blk = lax.axis_index("blk")
    index = 0
    for bit in order:
        index = index * 2 + (blk // bit) % 2
    return index


def unpack_kernel(index, low_ref, high_ref, *out_refs):
    low = pl.program_id(0) < pl.num_programs(0) // 2
    group, rows, _ = low_ref.shape
    at = 0
    for out_ref in out_refs:
        width = out_ref.shape[1]
        for source, chosen in [(low_ref, low), (high_ref, jnp.logical_not(low))]:

            @pl.when(chosen)
            def _():
                for slot in range(group):
                    place = (index[0] % group) ^ slot
                    place = pl.multiple_of(place * rows, rows)
                    out_ref[pl.ds(place, rows), :] = source[slot, :, at : at + width].astype(F32)

        at += width


def unpack(low, high, order, widths):
    count, rows, columns = low.shape
    group = min(4, count)
    steps = 2 * count // group
    place = lambda j, index: (jnp.bitwise_xor(index[0] // group, j), 0)
    return kernel_call(
        unpack_kernel,
        grid_spec=pltpu.PrefetchScalarGridSpec(
            num_scalar_prefetch=1,
            grid=(steps,),
            in_specs=[
                pl.BlockSpec(
                    (group, rows, columns), lambda j, i: (jnp.minimum(j, steps // 2 - 1), 0, 0)
                ),
                pl.BlockSpec(
                    (group, rows, columns), lambda j, i: (jnp.maximum(j - steps // 2, 0), 0, 0)
                ),
            ],
            out_specs=[pl.BlockSpec((group * rows, width), place) for width in widths],
        ),
        out_shape=[jax.ShapeDtypeStruct((2 * count * rows, width), F32) for width in widths],
        compiler_params=pltpu.CompilerParams(vmem_limit_bytes=24 << 20),
        cost_estimate=lasting(5),
        name="unpack",
    )(piece_index(order).reshape(1), low, high)


def shards(
    frames,
    clip_lengths,
    text_states,
    text_segments,
    gain_one,
    shift_one,
    gain_two,
    shift_two,
    gain_three,
    shift_three,
    query_weight,
    key_weight,
    value_weight,
    output_weight,
    cross_query,
    cross_key,
    cross_value,
    cross_output,
    inner_weight,
    outer_weight,
    cotangent,
):
    row_count, depth = frames.shape
    width_here = query_weight.shape[1]
    heads_here = width_here // HEAD_DIM
    blk_count, tp_count = lax.axis_size("blk"), lax.axis_size("tp")
    blk, tp = lax.axis_index("blk"), lax.axis_index("tp")
    core = blk % 2
    copies = blk_count // heads_here
    sub = row_count // copies
    half = row_count // tp_count
    mine = blk % copies
    scale = float(HEAD_DIM) ** (-0.5)
    bits = [1 << i for i in range(1, blk_count.bit_length() - 1)]
    order_one = [1] + bits
    order_two = [1, bits[1], bits[0]] + bits[2:]

    def own_rows(array):
        return lax.dynamic_slice_in_dim(array, tp * half, half, 0)

    def other_rows(array):
        return lax.dynamic_slice_in_dim(array, (1 - tp) * half, half, 0)

    inputs = frames.astype(F32)
    hat, _ = normalize(inputs)
    normed_one = (hat * gain_one + shift_one).astype(BF)
    q_t = (dg(query_weight, normed_one, ((0,), (1,))) * scale).astype(BF)
    k_t = dg(key_weight, normed_one, ((0,), (1,))).astype(BF)
    v_t = dg(value_weight, normed_one, ((0,), (1,))).astype(BF)

    weights_two = [output_weight, cross_query, cross_output]
    hops = [first_hop(w, core) for w in weights_two]
    text_k = dg(cross_key, text_states, ((0,), (1,))).astype(BF)
    text_v = dg(cross_value, text_states, ((0,), (1,))).astype(BF)
    text_own = jnp.stack([text_k, text_v])
    text_both = jnp.stack([text_own, over_x(text_own)], axis=1)

    def spread_heads(array):
        count = array.shape[0]
        array = array.reshape(count, heads_here, HEAD_DIM, copies, sub).transpose(1, 3, 0, 2, 4)
        return lax.all_to_all(
            array.reshape(blk_count, count, HEAD_DIM, sub), "blk", 0, 0, tiled=True
        )

    def bring_heads(array):
        got = lax.all_to_all(array, "blk", 0, 0, tiled=True)
        return got.reshape(heads_here, copies, array.shape[1], HEAD_DIM, sub)

    got = spread_heads(jnp.stack([q_t, k_t, v_t]))
    queries = got[:, 0].transpose(1, 0, 2).reshape(HEAD_DIM, blk_count * sub)
    both = got[:, 1:][:, :, :, None, :]
    bit = 1
    while bit < copies:
        both = jnp.concatenate([both, over_blk(both, bit)], axis=3)
        bit *= 2
    both = both.transpose(1, 2, 0, 3, 4).reshape(2, HEAD_DIM, blk_count * row_count)
    keys, values = both[0], both[1]
    rows_all = jnp.arange(blk_count, dtype=jnp.int32)[:, None] * row_count
    rows_all = (rows_all + mine * sub + jnp.arange(sub, dtype=jnp.int32)[None, :]).reshape(-1)
    _, first = clip_rows(rows_all, clip_lengths)
    flip = mine * sub
    out, log_total = attend(queries, keys, values, rows_all, first, flip)
    hops, out = lax.optimization_barrier((hops, out))
    output_both, query_both, cross_both = [
        list(pair) for pair in zip(weights_two, weld(hops, [over_blk(h, 1) for h in hops], core))
    ]

    out_low = out.astype(BF).reshape(HEAD_DIM, blk_count, sub).transpose(1, 0, 2)[:, None]
    attended = bring_heads(out_low)[:, :, 0]

    def token_half(array, which):
        array = array.reshape(heads_here, tp_count, copies // tp_count, HEAD_DIM, sub)
        array = lax.dynamic_index_in_dim(array, which, 1, keepdims=False)
        return array.transpose(0, 2, 1, 3).reshape(width_here, half)

    a_own, a_sent = token_half(attended, tp), token_half(attended, 1 - tp)
    a_both = [a_own, over_x(a_sent)]

    rows = blk * row_count + tp * half + jnp.arange(half, dtype=jnp.int32)
    segment, _ = clip_rows(rows, clip_lengths)
    x_low = own_rows(frames)
    row = lambda array: array.reshape(1, -1)
    norms = [row(gain_two), row(shift_two), row(gain_three), row(shift_three)]
    segment, text_segment = segment.reshape(1, -1), text_segments.reshape(-1, 1)
    first_sum, second_sum, h2_own, h3_own, qc_t, oc_t, c_own, c_sent = cross_forward(
        a_both, x_low, norms, output_both, query_both, cross_both,
        text_both[0], text_both[1], segment, text_segment, scale,
    )

    h3_other = over_x(h3_own)
    hidden, grad_pre, dh3_own, dh3_sent = hidden_pass(
        h3_own, h3_other, cotangent, inner_weight, outer_weight, tp
    )
    dh3_got = over_x(dh3_sent)
    hidden_both, y_kept, y_sent = hidden_grads(
        h3_own, h3_other, cotangent, hidden, grad_pre, outer_weight, tp
    )
    hidden_piece = lax.psum_scatter(hidden_both, "blk", scatter_dimension=0, tiled=True)
    dh3_got, y_kept = lax.optimization_barrier((dh3_got, y_kept))

    dx1, dx1_low, dx2_low, dqc_own, dqc_sent, da_own, da_sent, text_own, text_sent, small_cross = cross_backward(
        dh3_own, dh3_got, own_rows(cotangent), first_sum, second_sum, row(gain_two),
        row(gain_three), output_both, query_both, cross_both, text_both[0], text_both[1],
        qc_t, oc_t, segment, text_segment, scale,
    )
    da_other = over_x(da_sent)
    da_own = after(da_own, da_other)

    def as_heads(array):
        return array.reshape(heads_here, HEAD_DIM, copies // tp_count, sub).transpose(0, 2, 1, 3)

    low = jnp.where(tp == 0, as_heads(da_own), as_heads(da_other))
    high = jnp.where(tp == 0, as_heads(da_other), as_heads(da_own))
    sent = jnp.concatenate([low, high], axis=1).reshape(blk_count, 1, HEAD_DIM, sub)
    grads = lax.all_to_all(sent, "blk", 0, 0, tiled=True)[:, 0]
    grads = grads.transpose(1, 0, 2).reshape(HEAD_DIM, blk_count * sub)
    dx1_other, dx2_other, dqc_other, c_other = [
        over_x(value) for value in after((dx1_low, dx2_low, dqc_sent, c_sent), da_other)
    ]
    grads, dx1_other, dx2_other, dqc_other, c_other = lax.optimization_barrier(
        (grads, dx1_other, dx2_other, dqc_other, c_other)
    )
    dq, parts = attend_back(
        queries, keys, values, rows_all, first, flip, out, log_total, grads, sub
    )
    while parts.shape[0] > 2:
        got = over_blk(halves(parts, 1), parts.shape[0] // 2)
        parts = (halves(parts, 0).astype(F32) + got.astype(F32)).astype(BF)
    parts_got = over_blk(parts[1], 1)
    sent = combine(dq, parts, parts_got, scale)
    back = bring_heads(sent)
    text_got, h2_other, y_got = after(
        [over_x(value) for value in after((text_sent, h2_own, y_sent), da_other)], sent
    )
    text_part = text_own + text_got.astype(F32)
    pair_send, pair_keep = pair_grads(
        [
            (a_own, a_sent, dx1_low, dx1_other),
            (c_own, c_other, dx2_low, dx2_other),
            (dqc_own, dqc_other, h2_own, h2_other),
        ],
        core,
    )
    y_own = (second_sum + y_kept + y_got.astype(F32)).astype(BF)
    back, pair_send, hidden_piece = lax.optimization_barrier((back, pair_send, hidden_piece))
    hidden_both = lax.all_gather(hidden_piece, "blk", axis=0, tiled=True)
    back = back.transpose(2, 0, 3, 1, 4).reshape(3, width_here, row_count)
    dh1_own, dh1_sent = project_back(back, [query_weight, key_weight, value_weight], tp)
    dh1_got = over_x(dh1_sent)
    head_send, head_keep = head_grads(back, normed_one, core)
    pairs = Stream(pair_send, pair_keep, order_one, blk)
    heads = Stream(head_send, head_keep, order_two, blk)
    text = Butterfly(text_part, order_one, BF)
    y_other = over_x(y_own)
    streams = [pairs, heads, text]
    dh1_got, y_other = meet(streams, (dh1_got, y_other))
    result = in_order(y_own, y_other, tp)
    for stream in streams:
        stream.step()
    through, grad_gain_one, grad_shift_one = norm_back(
        x_low.astype(F32), gain_one, dh1_own + dh1_got.astype(F32)
    )
    dx = (dx1 + through).astype(BF)
    dx_other = over_x(dx)
    small = jnp.concatenate([grad_gain_one[None], grad_shift_one[None], small_cross])
    small_got = over_x(small)
    dx_other, small_got = meet(streams, (dx_other, small_got))
    grad_frames = in_order(dx, dx_other, tp)
    small = Butterfly(small + small_got, order_one, F32)
    while pairs.phase < len(order_one) - 1:
        for stream in streams:
            stream.step()
        meet(streams + [small], ())
        small.step()
    pair_piece, head_piece = pairs.piece(), heads.piece()
    width = head_piece.shape[1]
    parts = [pair_piece[:, at : at + width] for at in range(0, pair_piece.shape[1], width)]
    pieces = lax.all_gather(jnp.concatenate([head_piece] + parts), "blk")
    while small.phase is not None or text.phase is not None:
        small.step()
        text.step()
        meet([small, text], ())
    text_total = text.value.astype(BF)
    grad_text = dg(text_total[0], cross_key, ((0,), (1,)))
    grad_text = (grad_text + dg(text_total[1], cross_value, ((0,), (1,)))).astype(BF)
    text_got = over_x(grad_text)
    grad_cross_key = dg(text_states, text_total[0], ((0,), (1,)))
    grad_cross_value = dg(text_states, text_total[1], ((0,), (1,)))
    grad_text = grad_text.astype(F32) + text_got.astype(F32)
    grad_text, grad_cross_key, grad_cross_value, hidden_both = lax.optimization_barrier(
        (grad_text, grad_cross_key, grad_cross_value, hidden_both)
    )
    grad_outer, grad_inner = hidden_out(hidden_both)
    rows_of = (head_piece.shape[0], pair_piece.shape[0])
    grads = widen(
        after(pieces, grad_inner), [order_two, order_one], rows_of, [width_here] * 3, [depth] * 3
    )
    grad_query, grad_key, grad_value, grad_output, grad_cross_output, grad_cross_query = grads
    grad_cross_query = grad_cross_query.T
    small = small.value

    return (
        result,
        grad_frames,
        grad_text,
        small[0],
        small[1],
        small[2],
        small[3],
        small[4],
        small[5],
        grad_query,
        grad_key,
        grad_value,
        grad_output,
        grad_cross_query,
        grad_cross_key,
        grad_cross_value,
        grad_cross_output,
        grad_inner,
        grad_outer,
    )


def solution(mesh):
    return jax.shard_map(
        shards,
        mesh=mesh,
        in_specs=(
            P("blk", None),
            P(),
            P(),
            P(),
            P(),
            P(),
            P(),
            P(),
            P(),
            P(),
            P(None, "tp"),
            P(None, "tp"),
            P(None, "tp"),
            P("tp", None),
            P(None, "tp"),
            P(None, "tp"),
            P(None, "tp"),
            P("tp", None),
            P(None, "tp"),
            P("tp", None),
            P("blk", None),
        ),
        out_specs=(
            P("blk", None),
            P("blk", None),
            P(),
            P(),
            P(),
            P(),
            P(),
            P(),
            P(),
            P(None, "tp"),
            P(None, "tp"),
            P(None, "tp"),
            P("tp", None),
            P(None, "tp"),
            P(None, "tp"),
            P(None, "tp"),
            P("tp", None),
            P(None, "tp"),
            P("tp", None),
        ),
        check_vma=False,
    )
```

```python
import functools
import math
import jax
import jax.numpy as jnp
from jax import lax
from jax.experimental import pallas as pl
from jax.experimental.pallas import tpu as pltpu
from jax.sharding import PartitionSpec as P

HEAD_DIM = 64
NEGATIVE = -1e30
LARGE = 1 << 16
BF, F32 = jnp.bfloat16, jnp.float32


def lasting(microseconds):
    return pl.CostEstimate(flops=0, bytes_accessed=int(microseconds * 3.7e6), transcendentals=0)


def kernel_call(body, *, out_shape, least=LARGE, least_out=None, **options):
    many = isinstance(out_shape, (list, tuple))
    outs = [
        pltpu.HBM(o.shape, o.dtype) if math.prod(o.shape) >= (least_out or least) else o
        for o in (out_shape if many else [out_shape])
    ]
    call = pl.pallas_call(body, out_shape=outs if many else outs[0], **options)

    def run(*args):
        return call(
            *[
                pltpu.with_memory_space_constraint(a, pltpu.HBM) if a.size >= least else a
                for a in args
            ]
        )

    return run


def dg(left, right, dims):
    return lax.dot_general(left, right, (dims, ((), ())), preferred_element_type=F32)


def tile_ranges(positions, first, tile, chunk):
    rows = positions.reshape(-1, tile)
    starts = first.reshape(-1, tile)
    low = jnp.min(starts, axis=1) // chunk
    high = jnp.max(rows, axis=1) // chunk + 1
    clear = jnp.clip((jnp.max(starts, axis=1) + chunk - 1) // chunk, low, high)
    stop = jnp.clip((jnp.min(rows, axis=1) + 1) // chunk, clear, high)
    return jnp.stack([low, clear, stop, high], axis=1)


def allowed_keys(base, flip, chunk, rows, first):
    keys = (base + lax.broadcasted_iota(jnp.int32, (chunk, rows.shape[1]), 0)) ^ flip
    return (keys <= rows) & (keys >= first)


def attend_kernel(ranges, flips, q_ref, k_ref, v_ref, row_ref, first_ref, out_ref, log_ref, k_rows, chunk):
    tile = pl.program_id(0)
    total = k_ref.shape[1]

    @pl.when(tile == 0)
    def _():
        for base in range(0, total, chunk):
            k_rows[base : base + chunk, :] = k_ref[:, base : base + chunk].T

    queries = q_ref[...]
    rows, first = row_ref[...], first_ref[...]
    width = queries.shape[1]

    def work(masked):
        def step(index, carry):
            best, total_weight, acc = carry
            base = pl.multiple_of(index * chunk, chunk)
            score = jnp.dot(k_rows[pl.ds(base, chunk), :], queries, preferred_element_type=F32)
            if masked:
                allowed = allowed_keys(base, flips[0], chunk, rows, first)
                score = jnp.where(allowed, score, NEGATIVE)
            new_best = jnp.maximum(best, jnp.max(score, axis=0, keepdims=True))
            expo = jnp.exp(score - new_best)
            if masked:
                expo = jnp.where(allowed, expo, 0.0)
            fade = jnp.exp(best - new_best)
            total_weight = total_weight * fade + jnp.sum(expo, axis=0, keepdims=True)
            acc = acc * fade + jnp.dot(
                v_ref[:, pl.ds(base, chunk)], expo.astype(BF), preferred_element_type=F32
            )
            return new_best, total_weight, acc

        return step

    carry = (
        jnp.full((1, width), NEGATIVE, F32),
        jnp.zeros((1, width), F32),
        jnp.zeros((HEAD_DIM, width), F32),
    )
    carry = lax.fori_loop(ranges[tile, 0], ranges[tile, 1], work(True), carry)
    carry = lax.fori_loop(ranges[tile, 1], ranges[tile, 2], work(False), carry)
    best, total_weight, acc = lax.fori_loop(ranges[tile, 2], ranges[tile, 3], work(True), carry)
    out_ref[...] = acc / total_weight
    log_ref[...] = best + jnp.log(total_weight)


def attend(queries, keys, values, rows, first, flip, tile=512, chunk=1024):
    count, total = queries.shape[1], keys.shape[1]
    tile = min(tile, count)
    chunk = min(chunk, total)
    ranges = tile_ranges(rows, first, tile, chunk)
    whole = lambda i, r, f: (0, 0)
    part = lambda i, r, f: (0, i)
    return kernel_call(
        functools.partial(attend_kernel, chunk=chunk),
        grid_spec=pltpu.PrefetchScalarGridSpec(
            num_scalar_prefetch=2,
            grid=(count // tile,),
            in_specs=[
                pl.BlockSpec((HEAD_DIM, tile), part),
                pl.BlockSpec((HEAD_DIM, total), whole),
                pl.BlockSpec((HEAD_DIM, total), whole),
                pl.BlockSpec((1, tile), part),
                pl.BlockSpec((1, tile), part),
            ],
            out_specs=[pl.BlockSpec((HEAD_DIM, tile), part), pl.BlockSpec((1, tile), part)],
            scratch_shapes=[pltpu.VMEM((total, HEAD_DIM), BF)],
        ),
        out_shape=[
            jax.ShapeDtypeStruct((HEAD_DIM, count), F32),
            jax.ShapeDtypeStruct((1, count), F32),
        ],
        compiler_params=pltpu.CompilerParams(vmem_limit_bytes=(16 if total <= 4096 else 48) << 20),
        cost_estimate=lasting(15),
        least=1 << 30,
        name="attend",
    )(ranges, flip.reshape(1), queries, keys, values, rows.reshape(1, -1), first.reshape(1, -1))


def attend_back_kernel(
    ranges, flips, q_ref, k_ref, v_ref, row_ref, first_ref, out_ref, log_ref, do_ref,
    dq_ref, parts_ref, k_rows, v_rows, dk_ref, dv_ref, chunk,
):
    tile = pl.program_id(0)
    total = k_ref.shape[1]
    copies, blocks, _, _, sub = parts_ref.shape

    @pl.when(tile == 0)
    def _():
        for base in range(0, total, chunk):
            k_rows[base : base + chunk, :] = k_ref[:, base : base + chunk].T
            v_rows[base : base + chunk, :] = v_ref[:, base : base + chunk].T
        dk_ref[...] = jnp.zeros_like(dk_ref)
        dv_ref[...] = jnp.zeros_like(dv_ref)

    queries, grads = q_ref[...], do_ref[...]
    rows, first = row_ref[...], first_ref[...]
    log_total = log_ref[...]
    delta = jnp.sum(grads.astype(F32) * out_ref[...], axis=0, keepdims=True)

    def work(masked):
        def step(index, acc):
            base = pl.multiple_of(index * chunk, chunk)
            span = pl.ds(base, chunk)
            score = jnp.dot(k_rows[span, :], queries, preferred_element_type=F32)
            weights = jnp.exp(score - log_total)
            if masked:
                allowed = allowed_keys(base, flips[0], chunk, rows, first)
                weights = jnp.where(allowed, weights, 0.0)
            grad_weights = jnp.dot(v_rows[span, :], grads, preferred_element_type=F32)
            grad_score = (weights * (grad_weights - delta)).astype(BF)
            dv_ref[:, span] += dg(grads, weights.astype(BF), ((1,), (1,)))
            dk_ref[:, span] += dg(queries, grad_score, ((1,), (1,)))
            return acc + jnp.dot(k_ref[:, span], grad_score, preferred_element_type=F32)

        return step

    acc = jnp.zeros(queries.shape, F32)
    acc = lax.fori_loop(ranges[tile, 0], ranges[tile, 1], work(True), acc)
    acc = lax.fori_loop(ranges[tile, 1], ranges[tile, 2], work(False), acc)
    dq = lax.fori_loop(ranges[tile, 2], ranges[tile, 3], work(True), acc).astype(BF)
    for block in range(dq_ref.shape[0]):
        dq_ref[block] = dq[:, block * sub : (block + 1) * sub]

    @pl.when(tile == pl.num_programs(0) - 1)
    def _():
        for block in range(blocks):
            for copy in range(copies):
                at = (block * copies + copy) * sub
                parts_ref[copy, block, 0] = dk_ref[:, at : at + sub].astype(BF)
                parts_ref[copy, block, 1] = dv_ref[:, at : at + sub].astype(BF)


def attend_back(queries, keys, values, rows, first, flip, out, log_total, grads, sub, tile=512, chunk=1024):
    count, total = queries.shape[1], keys.shape[1]
    blocks, copies = count // sub, total // count
    tile = min(tile, count)
    chunk = min(chunk, total)
    ranges = tile_ranges(rows, first, tile, chunk)
    whole = lambda i, r, f: (0, 0)
    part = lambda i, r, f: (0, i)
    return kernel_call(
        functools.partial(attend_back_kernel, chunk=chunk),
        grid_spec=pltpu.PrefetchScalarGridSpec(
            num_scalar_prefetch=2,
            grid=(count // tile,),
            in_specs=[
                pl.BlockSpec((HEAD_DIM, tile), part),
                pl.BlockSpec((HEAD_DIM, total), whole),
                pl.BlockSpec((HEAD_DIM, total), whole),
                pl.BlockSpec((1, tile), part),
                pl.BlockSpec((1, tile), part),
                pl.BlockSpec((HEAD_DIM, tile), part),
                pl.BlockSpec((1, tile), part),
                pl.BlockSpec((HEAD_DIM, tile), part),
            ],
            out_specs=[
                pl.BlockSpec((tile // sub, HEAD_DIM, sub), lambda i, r, f: (i, 0, 0)),
                pl.BlockSpec((copies, blocks, 2, HEAD_DIM, sub), lambda i, r, f: (0, 0, 0, 0, 0)),
            ],
            scratch_shapes=[
                pltpu.VMEM((total, HEAD_DIM), BF),
                pltpu.VMEM((total, HEAD_DIM), BF),
                pltpu.VMEM((HEAD_DIM, total), F32),
                pltpu.VMEM((HEAD_DIM, total), F32),
            ],
        ),
        out_shape=[
            jax.ShapeDtypeStruct((blocks, HEAD_DIM, sub), BF),
            jax.ShapeDtypeStruct((copies, blocks, 2, HEAD_DIM, sub), BF),
        ],
        compiler_params=pltpu.CompilerParams(vmem_limit_bytes=(24 if total <= 4096 else 60) << 20),
        cost_estimate=lasting(17),
        least=1 << 30,
        name="attend_back",
    )(ranges, flip.reshape(1), queries, keys, values, rows.reshape(1, -1), first.reshape(1, -1), out, log_total, grads)


EPSILON = 1e-05
SWAP = [(0, 1), (1, 0)]


def after(values, token):
    return lax.optimization_barrier((values, token))[0]


def over_x(value):
    return lax.ppermute(value, "tp", SWAP)


def over_blk(value, bit):
    return lax.ppermute(value, "blk", [(i, i ^ bit) for i in range(lax.axis_size("blk"))])


def normalize(values):
    centre = values - jnp.mean(values, axis=-1, keepdims=True)
    spread = lax.rsqrt(jnp.mean(centre * centre, axis=-1, keepdims=True) + EPSILON)
    return centre * spread, spread


def norm_back(values, gain, grad):
    hat, spread = normalize(values)
    scaled = grad * gain
    through = spread * (
        scaled
        - jnp.mean(scaled, axis=-1, keepdims=True)
        - hat * jnp.mean(scaled * hat, axis=-1, keepdims=True)
    )
    return through, jnp.sum(grad * hat, axis=0), jnp.sum(grad, axis=0)


def clip_rows(positions, clip_lengths):
    index = jnp.arange(clip_lengths.shape[0], dtype=jnp.int32)
    starts = jnp.sum(jnp.where(index[None, :] < index[:, None], clip_lengths[None, :], 0), axis=1)
    ends = starts + clip_lengths
    segment = jnp.sum((positions[:, None] >= ends[None, :]).astype(jnp.int32), axis=1)
    match = segment[:, None] == index[None, :]
    first = jnp.sum(jnp.where(match, starts[None, :], 0), axis=1)
    return segment, first


def matmul(left, right):
    return jnp.dot(left, right, preferred_element_type=F32)


def matmul_nt(left, right):
    return dg(left, right, ((1,), (1,)))


def matmul_tn(left, right):
    return dg(left, right, ((0,), (0,)))


def first_hop(weight, core):
    return over_x(halves(weight, core))


def weld_kernel(core, *refs):
    count = len(refs) // 3
    for which in range(count):
        first, second, out = refs[which], refs[count + which], refs[2 * count + which]
        chosen = pl.program_id(0) == core[0]

        @pl.when(chosen)
        def _():
            out[...] = first[...]

        @pl.when(jnp.logical_not(chosen))
        def _():
            out[...] = second[...]


def weld(own, other, core):
    outs = [jax.ShapeDtypeStruct((2 * a.shape[0], a.shape[1]), a.dtype) for a in own]
    return kernel_call(
        weld_kernel,
        grid_spec=pltpu.PrefetchScalarGridSpec(
            num_scalar_prefetch=1,
            grid=(2,),
            in_specs=[whole_spec(a) for a in list(own) + list(other)],
            out_specs=[pl.BlockSpec(a.shape, lambda i, c: (i, 0)) for a in own],
        ),
        out_shape=outs,
        compiler_params=pltpu.CompilerParams(vmem_limit_bytes=24 << 20),
        cost_estimate=lasting(4),
        name="weld",
    )(core.reshape(1), *own, *other)


def in_order(own, other, tp):
    return jnp.concatenate([jnp.where(tp == 0, own, other), jnp.where(tp == 0, other, own)])


def whole_spec(array):
    shape = array.shape
    return pl.BlockSpec(shape, lambda *_: (0,) * len(shape))


def norm_rows(values):
    centre = values - jnp.mean(values, axis=-1, keepdims=True)
    spread = lax.rsqrt(jnp.mean(centre * centre, axis=-1, keepdims=True) + EPSILON)
    return centre * spread, spread


def norm_rows_back(values, gain, grad):
    hat, spread = norm_rows(values)
    scaled = grad * gain
    through = spread * (
        scaled
        - jnp.mean(scaled, axis=-1, keepdims=True)
        - hat * jnp.mean(scaled * hat, axis=-1, keepdims=True)
    )
    return through, jnp.sum(grad * hat, axis=0, keepdims=True), jnp.sum(grad, axis=0, keepdims=True)


def text_weights(keys, queries, allowed):
    score = dg(keys, queries, ((0,), (0,)))
    score = jnp.where(allowed, score, NEGATIVE)
    expo = jnp.exp(score - jnp.max(score, axis=0, keepdims=True))
    expo = jnp.where(allowed, expo, 0.0)
    return expo / jnp.sum(expo, axis=0, keepdims=True)


def embed_kernel(x_ref, gain, shift, wq_ref, wk_ref, wv_ref, rows_ref, out_ref, scale):
    hat, _ = norm_rows(x_ref[...].astype(F32))
    rows = (hat * gain[...] + shift[...]).astype(BF)
    rows_ref[...] = rows
    blocks, _, _, sub = out_ref.shape
    copies = rows.shape[0] // sub
    for which, weight in enumerate([wq_ref, wk_ref, wv_ref]):
        value = jnp.dot(rows, weight[...], preferred_element_type=F32)
        value = (value * scale if which == 0 else value).astype(BF).T
        for block in range(blocks):
            head, copy = divmod(block, copies)
            out_ref[block, which] = value[
                head * HEAD_DIM : (head + 1) * HEAD_DIM, copy * sub : (copy + 1) * sub
            ]


def embed(frames, gain, shift, weights, blocks, sub, scale):
    args = [frames, gain, shift, *weights]
    outs = [
        jax.ShapeDtypeStruct(frames.shape, BF),
        jax.ShapeDtypeStruct((blocks, 3, HEAD_DIM, sub), BF),
    ]
    return kernel_call(
        functools.partial(embed_kernel, scale=scale),
        grid=(1,),
        in_specs=[whole_spec(a) for a in args],
        out_specs=[whole_spec(o) for o in outs],
        out_shape=outs,
        compiler_params=pltpu.CompilerParams(vmem_limit_bytes=24 << 20),
        cost_estimate=lasting(5),
        least=1 << 30,
        name="embed",
    )(*args)


def cross_kernel(
    a_own, a_other, x_ref, gain_two, shift_two, gain_three, shift_three, wo_own, wo_other,
    wq_own, wq_other, wc_own, wc_other, tk_ref, tv_ref, segment, text_segment,
    x1_ref, x2_ref, h2_ref, h3_ref, q_ref, oc_ref, c_own, c_other, scale,
):
    width = a_own.shape[0]
    change = jnp.dot(a_own[...].T, wo_own[...], preferred_element_type=F32)
    change += jnp.dot(a_other[...].T, wo_other[...], preferred_element_type=F32)
    x1 = x_ref[...].astype(F32) + change
    x1_ref[...] = x1
    hat, _ = norm_rows(x1)
    h2 = (hat * gain_two[...] + shift_two[...]).astype(BF)
    h2_ref[...] = h2
    allowed = text_segment[...] == segment[...]
    crosses = []
    for side, wq in enumerate([wq_own, wq_other]):
        qc = (jnp.dot(h2, wq[...], preferred_element_type=F32) * scale).astype(BF)
        q_t = qc.T
        q_ref[side] = q_t
        parts = []
        for head in range(width // HEAD_DIM):
            span = slice(head * HEAD_DIM, (head + 1) * HEAD_DIM)
            weights = text_weights(tk_ref[side, span, :], q_t[span, :], allowed)
            parts.append(
                jnp.dot(tv_ref[side, span, :], weights.astype(BF), preferred_element_type=F32)
            )
        oc = jnp.concatenate(parts, axis=0)
        oc_ref[side] = oc
        crossed = oc.astype(BF)
        (c_own if side == 0 else c_other)[...] = crossed
        crosses.append(crossed.T)
    change = jnp.dot(crosses[0], wc_own[...], preferred_element_type=F32)
    change += jnp.dot(crosses[1], wc_other[...], preferred_element_type=F32)
    x2 = x1 + change
    x2_ref[...] = x2
    hat, _ = norm_rows(x2)
    h3_ref[...] = (hat * gain_three[...] + shift_three[...]).astype(BF)


def cross_forward(a_both, x_own, norms, output_both, query_both, cross_both, tk, tv, segment, text_segment, scale):
    half, depth = x_own.shape
    width = a_both[0].shape[0]
    args = [*a_both, x_own, *norms, *output_both, *query_both, *cross_both, tk, tv, segment, text_segment]
    shape = jax.ShapeDtypeStruct
    outs = [
        shape((half, depth), F32), shape((half, depth), F32), shape((half, depth), BF),
        shape((half, depth), BF), shape((2, width, half), BF), shape((2, width, half), F32),
        shape((width, half), BF), shape((width, half), BF),
    ]
    return kernel_call(
        functools.partial(cross_kernel, scale=scale),
        grid=(1,),
        in_specs=[whole_spec(a) for a in args],
        out_specs=[whole_spec(o) for o in outs],
        out_shape=outs,
        compiler_params=pltpu.CompilerParams(vmem_limit_bytes=28 << 20),
        cost_estimate=lasting(7),
        name="cross_forward",
    )(*args)


def cross_back_kernel(
    dh_own, dh_got, dy_ref, x1_ref, x2_ref, gain_two, gain_three, wo_own, wo_other,
    wq_own, wq_other, wc_own, wc_other, tk_ref, tv_ref, q_ref, oc_ref, segment, text_segment,
    dx1_ref, dx1_low_ref, dx2_low_ref, dq_own, dq_other, da_own, da_other, text_own, text_other,
    small_ref, scale,
):
    width = tk_ref.shape[1]
    dh3 = dh_own[...].astype(F32) + dh_got[...].astype(F32)
    through, gain_grad, shift_grad = norm_rows_back(x2_ref[...], gain_three[...], dh3)
    small_ref[2:3, :] = gain_grad
    small_ref[3:4, :] = shift_grad
    dx2 = dy_ref[...].astype(F32) + through
    low = dx2.astype(BF)
    dx2_low_ref[...] = low
    allowed = text_segment[...] == segment[...]
    dqs = []
    for side, wc in enumerate([wc_own, wc_other]):
        dc_t = dg(low, wc[...], ((1,), (1,))).astype(BF).T
        parts = []
        for head in range(width // HEAD_DIM):
            span = slice(head * HEAD_DIM, (head + 1) * HEAD_DIM)
            queries, grads = q_ref[side, span, :], dc_t[span, :]
            weights = text_weights(tk_ref[side, span, :], queries, allowed)
            delta = jnp.sum(grads.astype(F32) * oc_ref[side, span, :], axis=0, keepdims=True)
            grad_weights = dg(tv_ref[side, span, :], grads, ((0,), (0,)))
            grad_score = (weights * (grad_weights - delta)).astype(BF)
            dq = jnp.dot(tk_ref[side, span, :], grad_score, preferred_element_type=F32).astype(BF)
            parts.append(dq * jnp.asarray(scale, BF))
            text_ref = text_own if side == 0 else text_other
            text_ref[0, span, :] = dg(queries, grad_score, ((1,), (1,))).astype(text_ref.dtype)
            text_ref[1, span, :] = dg(grads, weights.astype(BF), ((1,), (1,))).astype(text_ref.dtype)
        dq = jnp.concatenate(parts, axis=0)
        (dq_own if side == 0 else dq_other)[...] = dq
        dqs.append(dq.T)
    dh2 = dg(dqs[0], wq_own[...], ((1,), (1,))) + dg(dqs[1], wq_other[...], ((1,), (1,)))
    through, gain_grad, shift_grad = norm_rows_back(x1_ref[...], gain_two[...], dh2)
    small_ref[0:1, :] = gain_grad
    small_ref[1:2, :] = shift_grad
    dx1 = dx2 + through
    dx1_ref[...] = dx1
    low = dx1.astype(BF)
    dx1_low_ref[...] = low
    for ref, wo in [(da_own, wo_own), (da_other, wo_other)]:
        ref[...] = dg(low, wo[...], ((1,), (1,))).astype(BF).T


def cross_backward(
    dh_own, dh_got, dy_own, x1, x2, gain_two, gain_three, output_both, query_both, cross_both,
    tk, tv, q_t, oc, segment, text_segment, scale,
):
    half, depth = x1.shape
    width, text = tk.shape[1], tk.shape[2]
    args = [
        dh_own, dh_got, dy_own, x1, x2, gain_two, gain_three, *output_both, *query_both,
        *cross_both, tk, tv, q_t, oc, segment, text_segment,
    ]
    shape = jax.ShapeDtypeStruct
    outs = [
        shape((half, depth), F32), shape((half, depth), BF), shape((half, depth), BF),
        *[shape((width, half), BF)] * 4, shape((2, width, text), F32), shape((2, width, text), BF),
        shape((4, depth), F32),
    ]
    return kernel_call(
        functools.partial(cross_back_kernel, scale=scale),
        grid=(1,),
        in_specs=[whole_spec(a) for a in args],
        out_specs=[whole_spec(o) for o in outs],
        out_shape=outs,
        compiler_params=pltpu.CompilerParams(vmem_limit_bytes=28 << 20),
        cost_estimate=lasting(9),
        name="cross_backward",
    )(*args)


def hidden_kernel(tp_ref, h_own, h_other, dy_ref, wi_ref, wo_ref, g_ref, du_ref, own_ref, other_ref, acc):
    step, half = pl.program_id(0), h_own.shape[0]
    tp = tp_ref[0]

    @pl.when(step == 0)
    def _():
        acc[...] = jnp.zeros_like(acc)

    for part, h_ref in enumerate([h_own, h_other]):
        rows = slice(part * half, (part + 1) * half)
        base = jnp.where(tp == part, 0, half)
        dy = dy_ref[pl.ds(pl.multiple_of(base, half), half), :]
        pre = jnp.dot(h_ref[...], wi_ref[...], preferred_element_type=F32)
        cdf = 0.5 * (1.0 + lax.erf(pre * (0.5**0.5)))
        density = jnp.exp(-0.5 * pre * pre) * 0.3989422804014327
        g_ref[rows, :] = (pre * cdf).astype(BF)
        grad = dg(dy, wo_ref[...], ((1,), (1,)))
        grad = (grad * (cdf + pre * density)).astype(BF)
        du_ref[rows, :] = grad
        acc[rows, :] += dg(grad, wi_ref[...], ((1,), (1,)))

    @pl.when(step == pl.num_programs(0) - 1)
    def _():
        own_ref[...] = acc[:half, :]
        other_ref[...] = acc[half:, :].astype(BF)


def hidden_pass(h_own, h_other, cotangent, inner, outer, tp, tile=512):
    half, depth = h_own.shape
    units = inner.shape[1]
    shape = jax.ShapeDtypeStruct
    return kernel_call(
        hidden_kernel,
        grid_spec=pltpu.PrefetchScalarGridSpec(
            num_scalar_prefetch=1,
            grid=(units // tile,),
            in_specs=[
                whole_spec(h_own), whole_spec(h_other), whole_spec(cotangent),
                pl.BlockSpec((depth, tile), lambda i, t: (0, i)),
                pl.BlockSpec((tile, depth), lambda i, t: (i, 0)),
            ],
            out_specs=[
                pl.BlockSpec((2 * half, tile), lambda i, t: (0, i)),
                pl.BlockSpec((2 * half, tile), lambda i, t: (0, i)),
                pl.BlockSpec((half, depth), lambda i, t: (0, 0)),
                pl.BlockSpec((half, depth), lambda i, t: (0, 0)),
            ],
            scratch_shapes=[pltpu.VMEM((2 * half, depth), F32)],
        ),
        out_shape=[
            shape((2 * half, units), BF), shape((2 * half, units), BF),
            shape((half, depth), F32), shape((half, depth), BF),
        ],
        compiler_params=pltpu.CompilerParams(vmem_limit_bytes=20 << 20),
        cost_estimate=lasting(10),
        least=1 << 30,
        name="hidden_pass",
    )(tp.reshape(1), h_own, h_other, cotangent, inner, outer)


def hidden_grads_kernel(
    place, h_own, h_other, dy_ref, g_ref, du_ref, wo_ref, both_ref, y_own, y_other, h_all, dy_all, acc
):
    step, half = pl.program_id(0), h_own.shape[0]
    tp = place[0]

    @pl.when(step == 0)
    def _():
        acc[...] = jnp.zeros_like(acc)
        h_all[:half, :] = h_own[...]
        h_all[half:, :] = h_other[...]
        for part in range(2):
            base = jnp.where(tp == part, 0, half)
            dy_all[part * half : (part + 1) * half, :] = dy_ref[
                pl.ds(pl.multiple_of(base, half), half), :
            ]

    acc[...] += jnp.dot(g_ref[...], wo_ref[...], preferred_element_type=F32)
    depth = h_own.shape[1]
    both_ref[:, :depth] = jnp.dot(g_ref[...].T, dy_all[...], preferred_element_type=F32).astype(BF)
    both_ref[:, depth:] = jnp.dot(du_ref[...].T, h_all[...], preferred_element_type=F32).astype(BF)

    @pl.when(step == pl.num_programs(0) - 1)
    def _():
        y_own[...] = acc[:half, :]
        y_other[...] = acc[half:, :].astype(BF)


def hidden_grads(h_own, h_other, cotangent, g, du, outer, tp, tile=256):
    half, depth = h_own.shape
    units = outer.shape[0]
    shape = jax.ShapeDtypeStruct
    across = lambda i, p: (0, i)
    down = lambda i, p: (i, 0)
    still = lambda i, p: (0, 0)
    return kernel_call(
        hidden_grads_kernel,
        grid_spec=pltpu.PrefetchScalarGridSpec(
            num_scalar_prefetch=1,
            grid=(units // tile,),
            in_specs=[
                whole_spec(h_own), whole_spec(h_other), whole_spec(cotangent),
                pl.BlockSpec((2 * half, tile), across), pl.BlockSpec((2 * half, tile), across),
                pl.BlockSpec((tile, depth), down),
            ],
            out_specs=[
                pl.BlockSpec((tile, 2 * depth), down),
                pl.BlockSpec((half, depth), still), pl.BlockSpec((half, depth), still),
            ],
            scratch_shapes=[
                pltpu.VMEM((2 * half, depth), BF),
                pltpu.VMEM((2 * half, depth), BF),
                pltpu.VMEM((2 * half, depth), F32),
            ],
        ),
        out_shape=[
            shape((units, 2 * depth), BF), shape((half, depth), F32), shape((half, depth), BF),
        ],
        compiler_params=pltpu.CompilerParams(vmem_limit_bytes=20 << 20),
        cost_estimate=lasting(9),
        least=1 << 30,
        least_out=LARGE,
        name="hidden_grads",
    )(tp.reshape(1), h_own, h_other, cotangent, g, du, outer)


def hidden_out_kernel(both_ref, outer_ref, inner_ref):
    depth = outer_ref.shape[1]
    outer_ref[...] = both_ref[:, :depth].astype(F32)
    inner_ref[...] = both_ref[:, depth:].astype(F32).T


def hidden_out(both, tile=256):
    units, depth = both.shape[0], both.shape[1] // 2
    return kernel_call(
        hidden_out_kernel,
        grid=(units // tile,),
        in_specs=[pl.BlockSpec((tile, 2 * depth), lambda i: (i, 0))],
        out_specs=[
            pl.BlockSpec((tile, depth), lambda i: (i, 0)), pl.BlockSpec((depth, tile), lambda i: (0, i))
        ],
        out_shape=[
            jax.ShapeDtypeStruct((units, depth), F32), jax.ShapeDtypeStruct((depth, units), F32)
        ],
        compiler_params=pltpu.CompilerParams(vmem_limit_bytes=16 << 20),
        cost_estimate=lasting(9),
        name="hidden_out",
    )(both)


def pair_grads_kernel(core, *refs):
    send, keep = refs[-2:]
    ins = refs[:-2]
    rows = send.shape[0]
    for which in range(len(ins) // 4):
        left_own, left_other, right_own, right_other = ins[4 * which : 4 * which + 4]
        depth = right_own.shape[1]
        for ref, side in [(send, 1 - core[0]), (keep, core[0])]:
            span = pl.ds(pl.multiple_of(side * rows, rows), rows)
            total = jnp.dot(left_own[span, :], right_own[...], preferred_element_type=F32)
            total += jnp.dot(left_other[span, :], right_other[...], preferred_element_type=F32)
            ref[:, which * depth : (which + 1) * depth] = total.astype(BF)


def pair_grads(groups, core):
    args = [array for group in groups for array in group]
    features, depth = groups[0][0].shape[0], groups[0][2].shape[1]
    columns = depth * len(groups)
    out = jax.ShapeDtypeStruct((features // 2, columns), BF)
    return kernel_call(
        pair_grads_kernel,
        grid_spec=pltpu.PrefetchScalarGridSpec(
            num_scalar_prefetch=1,
            grid=(1,),
            in_specs=[whole_spec(a) for a in args],
            out_specs=[whole_spec(out), whole_spec(out)],
        ),
        out_shape=[out, out],
        compiler_params=pltpu.CompilerParams(vmem_limit_bytes=24 << 20),
        cost_estimate=lasting(4),
        name="pair_grads",
    )(core.reshape(1), *args)


def fold_kernel(sides, *refs):
    count = len(refs) // 4
    ins, outs = refs[: 2 * count], refs[2 * count :]
    first = pl.program_id(0) < pl.num_programs(0) // 2
    for which in range(count):
        total = ins[2 * which][...].astype(F32) + ins[2 * which + 1][...].astype(F32)
        total = total.astype(BF)

        @pl.when(first)
        def _():
            outs[2 * which][...] = total

        @pl.when(jnp.logical_not(first))
        def _():
            outs[2 * which + 1][...] = total


def fold(pairs, sides):
    least = min(keep.shape[0] for keep, _ in pairs)
    if least % 16:
        sums = [(keep.astype(F32) + got.astype(F32)).astype(BF) for keep, got in pairs]
        return [(halves(t, 1 - side), halves(t, side)) for t, side in zip(sums, sides)]
    parts = 2 if least % 32 == 0 else 1
    args, in_specs, out_specs, outs = [], [], [], []
    for which, (keep, got) in enumerate(pairs):
        rows, columns = keep.shape
        block = rows // (2 * parts)
        place = lambda i, s, which=which: (
            jnp.where(i < parts, (1 - s[which]) * parts + i, s[which] * parts + i - parts), 0
        )
        args += [keep, got]
        in_specs += [pl.BlockSpec((block, columns), place)] * 2
        out_specs += [
            pl.BlockSpec((block, columns), lambda i, s: (jnp.minimum(i, parts - 1), 0)),
            pl.BlockSpec((block, columns), lambda i, s: (jnp.maximum(i - parts, 0), 0)),
        ]
        outs += [jax.ShapeDtypeStruct((rows // 2, columns), BF)] * 2
    got = kernel_call(
        fold_kernel,
        grid_spec=pltpu.PrefetchScalarGridSpec(
            num_scalar_prefetch=1,
            grid=(2 * parts,),
            in_specs=in_specs,
            out_specs=out_specs,
        ),
        out_shape=outs,
        compiler_params=pltpu.CompilerParams(vmem_limit_bytes=12 << 20),
        cost_estimate=lasting(3),
        name="fold",
    )(jnp.stack(sides), *args)
    return [(got[2 * i], got[2 * i + 1]) for i in range(len(pairs))]


def piece_places(count, order):
    places = []
    for device in range(count):
        index = 0
        for bit in order:
            index = index * 2 + (device // bit) % 2
        places.append(index)
    return places


def widen_kernel(devices, *refs, group, height):
    ins, outs = refs[: 2 * group], refs[2 * group :]
    columns = ins[0].shape[2]
    for slot in range(group):
        rows = ins[slot].shape[1]
        place = slice(slot * rows, (slot + 1) * rows)
        width = outs[0].shape[1]
        for which in range(3):
            outs[which][place, :] = ins[slot][0, :, which * width : (which + 1) * width].astype(F32)
    turned = []
    for slot in range(group):
        source = ins[group + slot]
        place = slice(slot * height, (slot + 1) * height)
        depth = outs[3].shape[1]
        at = 0
        for which in range(3):
            filled, found = 0, []
            while filled < depth:
                part, column = divmod(at, columns)
                count = min(columns - column, depth - filled)
                found.append(
                    source[0, part * height : (part + 1) * height, column : column + count]
                )
                if which < 2:
                    outs[3 + which][place, filled : filled + count] = found[-1].astype(F32)
                filled, at = filled + count, at + count
        turned.append(jnp.concatenate([value.astype(F32) for value in found], axis=1))
    outs[5][...] = jnp.concatenate(turned, axis=0).T


def widen(gathered, head_order, pair_order, rows, height, width, depth):
    count, total, columns = gathered.shape
    group = max(4, 128 // height)
    tables = []
    for order in (head_order, pair_order):
        places = piece_places(count, order)
        tables.append([places.index(place) for place in range(count)])
    spec = lambda kind, slot: pl.BlockSpec(
        (1, rows, columns), lambda j, t: (t[kind, j * group + slot], kind, 0)
    )
    shape = jax.ShapeDtypeStruct
    outs = [shape((count * rows, width), F32)] * 3 + [shape((count * height, depth), F32)] * 2
    outs += [shape((depth, count * height), F32)]
    down = lambda j, t: (j, 0)
    return kernel_call(
        functools.partial(widen_kernel, group=group, height=height),
        grid_spec=pltpu.PrefetchScalarGridSpec(
            num_scalar_prefetch=1,
            grid=(count // group,),
            in_specs=[spec(kind, slot) for kind in range(2) for slot in range(group)],
            out_specs=[pl.BlockSpec((group * rows, width), down)] * 3
            + [pl.BlockSpec((group * height, depth), down)] * 2
            + [pl.BlockSpec((depth, group * height), lambda j, t: (0, j))],
        ),
        out_shape=outs,
        compiler_params=pltpu.CompilerParams(vmem_limit_bytes=24 << 20),
        cost_estimate=lasting(7),
        name="widen",
    )(jnp.asarray(tables, jnp.int32), *[gathered] * (2 * group))


class Stream:
    def __init__(self, send, keep, order, blk):
        self.order, self.blk, self.phase, self.keep = order, blk, 0, keep
        self.got, self.sent = over_blk(send, order[0]), send

    def step(self):
        count, phase = len(self.order), self.phase
        if phase is None:
            return
        self.phase += 1
        if phase < count - 1:
            bit = self.order[phase + 1]
            ((send, self.keep),) = fold([(self.keep, self.got)], [(self.blk // bit) % 2])
            self.got, self.sent = over_blk(send, bit), send
        elif phase < 2 * count - 1:
            if phase == count - 1:
                piece = self.keep.astype(F32) + self.got.astype(F32)
                self.keep = piece.astype(BF)[None]
            else:
                self.keep = join(self.keep, self.got)
            self.got, self.sent = over_blk(self.keep, self.order[2 * count - 2 - phase]), self.keep
            if phase == 2 * count - 2:
                self.phase = None

    def piece(self):
        return (self.keep.astype(F32) + self.got.astype(F32)).astype(BF)

    def result(self, widths):
        return unpack(self.keep, self.got, self.order, widths)


def step_together(streams):
    bits = [stream.order[stream.phase + 1] for stream in streams]
    sides = [(stream.blk // bit) % 2 for stream, bit in zip(streams, bits)]
    halved = fold([(stream.keep, stream.got) for stream in streams], sides)
    for stream, (send, keep), bit in zip(streams, halved, bits):
        stream.phase += 1
        stream.keep, stream.sent, stream.got = keep, send, over_blk(send, bit)


def last_kernel(head_keep, head_got, pair_keep, pair_got, out_ref):
    rows, columns = head_keep.shape
    out_ref[:rows, :] = (head_keep[...].astype(F32) + head_got[...].astype(F32)).astype(BF)
    height = pair_keep.shape[0]
    pair = (pair_keep[...].astype(F32) + pair_got[...].astype(F32)).astype(BF)
    for part in range(pair.shape[1] // columns):
        at = rows + part * height
        out_ref[at : at + height, :] = pair[:, part * columns : (part + 1) * columns]


def last_halves(heads, pairs):
    args = [heads.keep, heads.got, pairs.keep, pairs.got]
    rows, columns = heads.keep.shape
    height = pairs.keep.shape[0] * (pairs.keep.shape[1] // columns)
    out = jax.ShapeDtypeStruct((rows + height, columns), BF)
    return kernel_call(
        last_kernel,
        grid=(1,),
        in_specs=[whole_spec(a) for a in args],
        out_specs=whole_spec(out),
        out_shape=out,
        cost_estimate=lasting(2),
        name="last_halves",
    )(*args)


class Butterfly:
    def __init__(self, value, order, wire):
        self.value, self.order, self.phase, self.wire = value, order, 0, wire
        self.got, self.sent = over_blk(value.astype(wire), order[0]), value

    def step(self):
        if self.phase is None:
            return
        self.value = self.value + self.got.astype(F32)
        self.phase += 1
        if self.phase < len(self.order):
            self.got = over_blk(self.value.astype(self.wire), self.order[self.phase])
            self.sent = self.value
        else:
            self.got, self.phase = jnp.zeros((), F32), None


def meet(streams, others):
    got, others = lax.optimization_barrier(([s.got for s in streams], others))
    for stream, value in zip(streams, got):
        stream.got = value
    return others


def project_back_kernel(tp, back_ref, *refs):
    weights, (own_ref, other_ref) = refs[:3], refs[3:]
    half = own_ref.shape[0]
    total = None
    for which, weight in enumerate(weights):
        part = dg(back_ref[which].T, weight[...], ((1,), (1,)))
        total = part if total is None else total + part
    first, second = total[:half, :], total[half:, :]
    own_ref[...] = jnp.where(tp[0] == 0, first, second)
    other_ref[...] = jnp.where(tp[0] == 0, second, first).astype(BF)


def project_back(back, weights, tp):
    rows, depth = back.shape[2], weights[0].shape[0]
    args = [back, *weights]
    outs = [
        jax.ShapeDtypeStruct((rows // 2, depth), F32), jax.ShapeDtypeStruct((rows // 2, depth), BF)
    ]
    return kernel_call(
        project_back_kernel,
        grid_spec=pltpu.PrefetchScalarGridSpec(
            num_scalar_prefetch=1,
            grid=(1,),
            in_specs=[whole_spec(a) for a in args],
            out_specs=[whole_spec(o) for o in outs],
        ),
        out_shape=outs,
        compiler_params=pltpu.CompilerParams(vmem_limit_bytes=16 << 20),
        cost_estimate=lasting(4),
        name="project_back",
    )(tp.reshape(1), *args)


def head_grads_kernel(core, back_ref, rows_ref, send, keep, turned):
    turned[...] = rows_ref[...].T
    rows, width = send.shape[0], back_ref.shape[1]
    for ref, side in [(send, 1 - core[0]), (keep, core[0])]:
        part = turned[pl.ds(pl.multiple_of(side * rows, rows), rows), :]
        for which in range(3):
            ref[:, which * width : (which + 1) * width] = dg(
                part, back_ref[which], ((1,), (1,))
            ).astype(BF)


def head_grads(back, normed, core):
    rows, depth = normed.shape
    out = jax.ShapeDtypeStruct((depth // 2, 3 * back.shape[1]), BF)
    return kernel_call(
        head_grads_kernel,
        grid_spec=pltpu.PrefetchScalarGridSpec(
            num_scalar_prefetch=1,
            grid=(1,),
            in_specs=[whole_spec(back), whole_spec(normed)],
            out_specs=[whole_spec(out), whole_spec(out)],
            scratch_shapes=[pltpu.VMEM((depth, rows), BF)],
        ),
        out_shape=[out, out],
        compiler_params=pltpu.CompilerParams(vmem_limit_bytes=16 << 20),
        cost_estimate=lasting(4),
        name="head_grads",
    )(core.reshape(1), back, normed)


def combine_kernel(dq_ref, parts_ref, got_ref, out_ref, scale):
    out_ref[:, 0] = dq_ref[...] * jnp.asarray(scale, BF)
    out_ref[:, 1:] = (parts_ref[0].astype(F32) + got_ref[...].astype(F32)).astype(BF)


def combine(dq, parts, got, scale):
    blocks, _, sub = dq.shape
    part = min(4, blocks)
    return kernel_call(
        functools.partial(combine_kernel, scale=scale),
        grid=(blocks // part,),
        in_specs=[
            pl.BlockSpec((part, HEAD_DIM, sub), lambda i: (i, 0, 0)),
            pl.BlockSpec((1, part, 2, HEAD_DIM, sub), lambda i: (0, i, 0, 0, 0)),
            pl.BlockSpec((part, 2, HEAD_DIM, sub), lambda i: (i, 0, 0, 0)),
        ],
        out_specs=pl.BlockSpec((part, 3, HEAD_DIM, sub), lambda i: (i, 0, 0, 0)),
        out_shape=jax.ShapeDtypeStruct((blocks, 3, HEAD_DIM, sub), BF),
        cost_estimate=lasting(3.5),
        name="combine",
    )(dq, parts, got)


def join_kernel(low_ref, high_ref, out_ref):
    for part, ref in enumerate([low_ref, high_ref]):

        @pl.when(pl.program_id(0) == part)
        def _():
            out_ref[...] = ref[...]


def join(low, high):
    shape = low.shape
    still = lambda i: (0,) * len(shape)
    return kernel_call(
        join_kernel,
        grid=(2,),
        in_specs=[pl.BlockSpec(shape, still)] * 2,
        out_specs=pl.BlockSpec(shape, lambda i: (i,) + (0,) * (len(shape) - 1)),
        out_shape=jax.ShapeDtypeStruct((2 * shape[0],) + shape[1:], low.dtype),
        compiler_params=pltpu.CompilerParams(vmem_limit_bytes=12 << 20),
        cost_estimate=lasting(2),
        name="join",
    )(low, high)


def halves(value, which):
    rows = value.shape[0] // 2
    return lax.dynamic_slice_in_dim(value, which * rows, rows, 0)


def piece_index(order):
    blk = lax.axis_index("blk")
    index = 0
    for bit in order:
        index = index * 2 + (blk // bit) % 2
    return index


def unpack_kernel(index, low_ref, high_ref, *out_refs):
    low = pl.program_id(0) < pl.num_programs(0) // 2
    group, rows, _ = low_ref.shape
    at = 0
    for out_ref in out_refs:
        width = out_ref.shape[1]
        for source, chosen in [(low_ref, low), (high_ref, jnp.logical_not(low))]:

            @pl.when(chosen)
            def _():
                for slot in range(group):
                    place = (index[0] % group) ^ slot
                    place = pl.multiple_of(place * rows, rows)
                    out_ref[pl.ds(place, rows), :] = source[slot, :, at : at + width].astype(F32)

        at += width


def unpack(low, high, order, widths):
    count, rows, columns = low.shape
    group = min(4, count)
    steps = 2 * count // group
    place = lambda j, index: (jnp.bitwise_xor(index[0] // group, j), 0)
    return kernel_call(
        unpack_kernel,
        grid_spec=pltpu.PrefetchScalarGridSpec(
            num_scalar_prefetch=1,
            grid=(steps,),
            in_specs=[
                pl.BlockSpec(
                    (group, rows, columns), lambda j, i: (jnp.minimum(j, steps // 2 - 1), 0, 0)
                ),
                pl.BlockSpec(
                    (group, rows, columns), lambda j, i: (jnp.maximum(j - steps // 2, 0), 0, 0)
                ),
            ],
            out_specs=[pl.BlockSpec((group * rows, width), place) for width in widths],
        ),
        out_shape=[jax.ShapeDtypeStruct((2 * count * rows, width), F32) for width in widths],
        compiler_params=pltpu.CompilerParams(vmem_limit_bytes=24 << 20),
        cost_estimate=lasting(5),
        name="unpack",
    )(piece_index(order).reshape(1), low, high)


def shards(
    frames,
    clip_lengths,
    text_states,
    text_segments,
    gain_one,
    shift_one,
    gain_two,
    shift_two,
    gain_three,
    shift_three,
    query_weight,
    key_weight,
    value_weight,
    output_weight,
    cross_query,
    cross_key,
    cross_value,
    cross_output,
    inner_weight,
    outer_weight,
    cotangent,
):
    row_count, depth = frames.shape
    width_here = query_weight.shape[1]
    heads_here = width_here // HEAD_DIM
    blk_count, tp_count = lax.axis_size("blk"), lax.axis_size("tp")
    blk, tp = lax.axis_index("blk"), lax.axis_index("tp")
    core = blk % 2
    copies = blk_count // heads_here
    sub = row_count // copies
    half = row_count // tp_count
    mine = blk % copies
    scale = float(HEAD_DIM) ** (-0.5)
    bits = [1 << i for i in range(1, blk_count.bit_length() - 1)]
    order_one = [1] + bits
    order_two = [1, bits[1], bits[0]] + bits[2:]

    def own_rows(array):
        return lax.dynamic_slice_in_dim(array, tp * half, half, 0)

    def other_rows(array):
        return lax.dynamic_slice_in_dim(array, (1 - tp) * half, half, 0)

    row = lambda array: array.reshape(1, -1)
    qkv_weights = [query_weight, key_weight, value_weight]
    if sub % 128 == 0:
        normed_one, qkv = embed(
            frames, row(gain_one), row(shift_one), qkv_weights, blk_count, sub, scale
        )
    else:
        hat, _ = normalize(frames.astype(F32))
        normed_one = (hat * gain_one + shift_one).astype(BF)
        qkv = jnp.stack([dg(weight, normed_one, ((0,), (1,))) for weight in qkv_weights])
        qkv = (qkv * jnp.array([scale, 1.0, 1.0], F32)[:, None, None]).astype(BF)
        qkv = qkv.reshape(3, heads_here, HEAD_DIM, copies, sub).transpose(1, 3, 0, 2, 4)
        qkv = qkv.reshape(blk_count, 3, HEAD_DIM, sub)

    weights_two = [output_weight, cross_query, cross_output]
    hops = [first_hop(w, core) for w in after(weights_two, qkv)]
    text_k = dg(cross_key, text_states, ((0,), (1,))).astype(BF)
    text_v = dg(cross_value, text_states, ((0,), (1,))).astype(BF)
    text_own = jnp.stack([text_k, text_v])
    text_both = jnp.stack([text_own, over_x(text_own)], axis=1)

    def bring_heads(array):
        got = lax.all_to_all(array, "blk", 0, 0, tiled=True)
        return got.reshape(heads_here, copies, array.shape[1], HEAD_DIM, sub)

    got = lax.all_to_all(qkv, "blk", 0, 0, tiled=True)
    queries = got[:, 0].transpose(1, 0, 2).reshape(HEAD_DIM, blk_count * sub)
    both = got[:, 1:][:, :, :, None, :]
    bit = 1
    while bit < copies:
        both = jnp.concatenate([both, over_blk(both, bit)], axis=3)
        bit *= 2
    both = both.transpose(1, 2, 0, 3, 4).reshape(2, HEAD_DIM, blk_count * row_count)
    keys, values = both[0], both[1]
    rows_all = jnp.arange(blk_count, dtype=jnp.int32)[:, None] * row_count
    rows_all = (rows_all + mine * sub + jnp.arange(sub, dtype=jnp.int32)[None, :]).reshape(-1)
    _, first = clip_rows(rows_all, clip_lengths)
    flip = mine * sub
    out, log_total = attend(queries, keys, values, rows_all, first, flip)
    hops, out = lax.optimization_barrier((hops, out))
    output_both, query_both, cross_both = [
        list(pair) for pair in zip(weights_two, weld(hops, [over_blk(h, 1) for h in hops], core))
    ]

    out_low = out.astype(BF).reshape(HEAD_DIM, blk_count, sub).transpose(1, 0, 2)[:, None]
    attended = bring_heads(out_low)[:, :, 0]

    attended, output_both, query_both, cross_both = lax.optimization_barrier(
        (attended, output_both, query_both, cross_both)
    )

    def token_half(array, which):
        array = array.reshape(heads_here, tp_count, copies // tp_count, HEAD_DIM, sub)
        array = lax.dynamic_index_in_dim(array, which, 1, keepdims=False)
        return array.transpose(0, 2, 1, 3).reshape(width_here, half)

    a_own, a_sent = token_half(attended, tp), token_half(attended, 1 - tp)
    a_both = [a_own, over_x(a_sent)]

    rows = blk * row_count + tp * half + jnp.arange(half, dtype=jnp.int32)
    segment, _ = clip_rows(rows, clip_lengths)
    x_low = own_rows(frames)
    norms = [row(gain_two), row(shift_two), row(gain_three), row(shift_three)]
    segment, text_segment = segment.reshape(1, -1), text_segments.reshape(-1, 1)
    first_sum, second_sum, h2_own, h3_own, qc_t, oc_t, c_own, c_sent = cross_forward(
        a_both, x_low, norms, output_both, query_both, cross_both,
        text_both[0], text_both[1], segment, text_segment, scale,
    )

    h3_other = over_x(h3_own)
    hidden, grad_pre, dh3_own, dh3_sent = hidden_pass(
        h3_own, h3_other, cotangent, inner_weight, outer_weight, tp
    )
    dh3_got = over_x(dh3_sent)
    hidden_both, y_kept, y_sent = hidden_grads(
        h3_own, h3_other, cotangent, hidden, grad_pre, outer_weight, tp
    )
    hidden_piece = lax.psum_scatter(hidden_both, "blk", scatter_dimension=0, tiled=True)
    dh3_got, y_kept = lax.optimization_barrier((dh3_got, y_kept))

    dx1, dx1_low, dx2_low, dqc_own, dqc_sent, da_own, da_sent, text_own, text_sent, small_cross = cross_backward(
        dh3_own, dh3_got, own_rows(cotangent), first_sum, second_sum, row(gain_two),
        row(gain_three), output_both, query_both, cross_both, text_both[0], text_both[1],
        qc_t, oc_t, segment, text_segment, scale,
    )
    da_other = over_x(da_sent)
    da_own = after(da_own, da_other)

    def as_heads(array):
        return array.reshape(heads_here, HEAD_DIM, copies // tp_count, sub).transpose(0, 2, 1, 3)

    low = jnp.where(tp == 0, as_heads(da_own), as_heads(da_other))
    high = jnp.where(tp == 0, as_heads(da_other), as_heads(da_own))
    sent = jnp.concatenate([low, high], axis=1).reshape(blk_count, 1, HEAD_DIM, sub)
    grads = lax.all_to_all(sent, "blk", 0, 0, tiled=True)[:, 0]
    grads = grads.transpose(1, 0, 2).reshape(HEAD_DIM, blk_count * sub)
    dx1_other, dx2_other, dqc_other, c_other = [
        over_x(value) for value in after((dx1_low, dx2_low, dqc_sent, c_sent), da_other)
    ]
    grads, dx1_other, dx2_other, dqc_other, c_other = lax.optimization_barrier(
        (grads, dx1_other, dx2_other, dqc_other, c_other)
    )
    dq, parts = attend_back(
        queries, keys, values, rows_all, first, flip, out, log_total, grads, sub
    )
    while parts.shape[0] > 2:
        got = over_blk(halves(parts, 1), parts.shape[0] // 2)
        parts = (halves(parts, 0).astype(F32) + got.astype(F32)).astype(BF)
    parts_got = over_blk(parts[1], 1)
    sent = combine(dq, parts, parts_got, scale)
    back = bring_heads(sent)
    text_got, h2_other, y_got = after(
        [over_x(value) for value in after((text_sent, h2_own, y_sent), da_other)], sent
    )
    text_part = text_own + text_got.astype(F32)
    pair_send, pair_keep = pair_grads(
        [
            (a_own, a_sent, dx1_low, dx1_other),
            (c_own, c_other, dx2_low, dx2_other),
            (dqc_own, dqc_other, h2_own, h2_other),
        ],
        core,
    )
    y_own = (second_sum + y_kept + y_got.astype(F32)).astype(BF)
    back, pair_send = lax.optimization_barrier((back, pair_send))
    back = back.transpose(2, 0, 3, 1, 4).reshape(3, width_here, row_count)
    dh1_own, dh1_sent = project_back(back, [query_weight, key_weight, value_weight], tp)
    dh1_got = over_x(dh1_sent)
    head_send, head_keep = head_grads(back, normed_one, core)
    head_send, hidden_piece = lax.optimization_barrier((head_send, hidden_piece))
    hidden_both = lax.all_gather(hidden_piece, "blk", axis=0, tiled=True)
    pairs = Stream(pair_send, pair_keep, order_one, blk)
    heads = Stream(head_send, head_keep, order_two, blk)
    text = Butterfly(text_part, order_one, BF)
    y_other = over_x(y_own)
    streams = [pairs, heads, text]
    dh1_got, y_other = meet(streams, (dh1_got, y_other))
    result = in_order(y_own, y_other, tp)
    step_together([pairs, heads])
    text.step()
    through, grad_gain_one, grad_shift_one = norm_back(
        x_low.astype(F32), gain_one, dh1_own + dh1_got.astype(F32)
    )
    dx = (dx1 + through).astype(BF)
    dx_other = over_x(dx)
    small = jnp.concatenate([grad_gain_one[None], grad_shift_one[None], small_cross])
    small_got = over_x(small)
    dx_other, small_got = meet(streams, (dx_other, small_got))
    grad_frames = in_order(dx, dx_other, tp)
    small = Butterfly(small + small_got, order_one, F32)
    while pairs.phase < len(order_one) - 1:
        step_together([pairs, heads])
        text.step()
        meet(streams + [small], ())
        small.step()
    pieces = lax.all_gather(last_halves(heads, pairs), "blk")
    while small.phase is not None or text.phase is not None:
        small.step()
        text.step()
        meet([small, text], ())
    text_total = text.value.astype(BF)
    grad_text = dg(text_total[0], cross_key, ((0,), (1,)))
    grad_text = (grad_text + dg(text_total[1], cross_value, ((0,), (1,)))).astype(BF)
    text_got = over_x(grad_text)
    grad_cross_key = dg(text_states, text_total[0], ((0,), (1,)))
    grad_cross_value = dg(text_states, text_total[1], ((0,), (1,)))
    grad_text = grad_text.astype(F32) + text_got.astype(F32)
    grad_text, grad_cross_key, grad_cross_value, hidden_both = lax.optimization_barrier(
        (grad_text, grad_cross_key, grad_cross_value, hidden_both)
    )
    grad_outer, grad_inner = hidden_out(hidden_both)
    grads = widen(
        after(pieces, grad_inner), order_two, order_one, heads.keep.shape[0], pairs.keep.shape[0],
        width_here, depth,
    )
    grad_query, grad_key, grad_value, grad_output, grad_cross_output, grad_cross_query = grads
    small = small.value

    return (
        result,
        grad_frames,
        grad_text,
        small[0],
        small[1],
        small[2],
        small[3],
        small[4],
        small[5],
        grad_query,
        grad_key,
        grad_value,
        grad_output,
        grad_cross_query,
        grad_cross_key,
        grad_cross_value,
        grad_cross_output,
        grad_inner,
        grad_outer,
    )


def solution(mesh):
    return jax.shard_map(
        shards,
        mesh=mesh,
        in_specs=(
            P("blk", None),
            P(),
            P(),
            P(),
            P(),
            P(),
            P(),
            P(),
            P(),
            P(),
            P(None, "tp"),
            P(None, "tp"),
            P(None, "tp"),
            P("tp", None),
            P(None, "tp"),
            P(None, "tp"),
            P(None, "tp"),
            P("tp", None),
            P(None, "tp"),
            P("tp", None),
            P("blk", None),
        ),
        out_specs=(
            P("blk", None),
            P("blk", None),
            P(),
            P(),
            P(),
            P(),
            P(),
            P(),
            P(),
            P(None, "tp"),
            P(None, "tp"),
            P(None, "tp"),
            P("tp", None),
            P(None, "tp"),
            P(None, "tp"),
            P(None, "tp"),
            P("tp", None),
            P(None, "tp"),
            P("tp", None),
        ),
        check_vma=False,
    )
```

```python
import functools
import math
import jax
import jax.numpy as jnp
from jax import lax
from jax.experimental import pallas as pl
from jax.experimental.pallas import tpu as pltpu
from jax.sharding import PartitionSpec as P

HEAD_DIM = 64
NEGATIVE = -1e30
LARGE = 1 << 16
BF, F32 = jnp.bfloat16, jnp.float32


def lasting(microseconds):
    return pl.CostEstimate(flops=0, bytes_accessed=int(microseconds * 3.7e6), transcendentals=0)


def kernel_call(body, *, out_shape, least=LARGE, least_out=None, **options):
    many = isinstance(out_shape, (list, tuple))
    outs = [
        pltpu.HBM(o.shape, o.dtype) if math.prod(o.shape) >= (least_out or least) else o
        for o in (out_shape if many else [out_shape])
    ]
    call = pl.pallas_call(body, out_shape=outs if many else outs[0], **options)

    def run(*args):
        return call(
            *[
                pltpu.with_memory_space_constraint(a, pltpu.HBM) if a.size >= least else a
                for a in args
            ]
        )

    return run


def dg(left, right, dims):
    return lax.dot_general(left, right, (dims, ((), ())), preferred_element_type=F32)


def tile_ranges(positions, first, tile, chunk):
    rows = positions.reshape(-1, tile)
    starts = first.reshape(-1, tile)
    low = jnp.min(starts, axis=1) // chunk
    high = jnp.max(rows, axis=1) // chunk + 1
    clear = jnp.clip((jnp.max(starts, axis=1) + chunk - 1) // chunk, low, high)
    stop = jnp.clip((jnp.min(rows, axis=1) + 1) // chunk, clear, high)
    return jnp.stack([low, clear, stop, high], axis=1)


def allowed_keys(base, flip, chunk, rows, first):
    keys = (base + lax.broadcasted_iota(jnp.int32, (chunk, rows.shape[1]), 0)) ^ flip
    return (keys <= rows) & (keys >= first)


def attend_kernel(ranges, flips, q_ref, k_ref, v_ref, row_ref, first_ref, out_ref, log_ref, k_rows, chunk):
    tile = pl.program_id(0)
    total = k_ref.shape[1]

    @pl.when(tile == 0)
    def _():
        for base in range(0, total, chunk):
            k_rows[base : base + chunk, :] = k_ref[:, base : base + chunk].T

    queries = q_ref[...]
    rows, first = row_ref[...], first_ref[...]
    width = queries.shape[1]

    def work(masked):
        def step(index, carry):
            best, total_weight, acc = carry
            base = pl.multiple_of(index * chunk, chunk)
            score = jnp.dot(k_rows[pl.ds(base, chunk), :], queries, preferred_element_type=F32)
            if masked:
                allowed = allowed_keys(base, flips[0], chunk, rows, first)
                score = jnp.where(allowed, score, NEGATIVE)
            new_best = jnp.maximum(best, jnp.max(score, axis=0, keepdims=True))
            expo = jnp.exp(score - new_best)
            if masked:
                expo = jnp.where(allowed, expo, 0.0)
            fade = jnp.exp(best - new_best)
            total_weight = total_weight * fade + jnp.sum(expo, axis=0, keepdims=True)
            acc = acc * fade + jnp.dot(
                v_ref[:, pl.ds(base, chunk)], expo.astype(BF), preferred_element_type=F32
            )
            return new_best, total_weight, acc

        return step

    carry = (
        jnp.full((1, width), NEGATIVE, F32),
        jnp.zeros((1, width), F32),
        jnp.zeros((HEAD_DIM, width), F32),
    )
    carry = lax.fori_loop(ranges[tile, 0], ranges[tile, 1], work(True), carry)
    carry = lax.fori_loop(ranges[tile, 1], ranges[tile, 2], work(False), carry)
    best, total_weight, acc = lax.fori_loop(ranges[tile, 2], ranges[tile, 3], work(True), carry)
    out_ref[...] = acc / total_weight
    log_ref[...] = best + jnp.log(total_weight)


def attend(queries, keys, values, rows, first, flip, tile=512, chunk=1024):
    count, total = queries.shape[1], keys.shape[1]
    tile = min(tile, count)
    chunk = min(chunk, total)
    ranges = tile_ranges(rows, first, tile, chunk)
    whole = lambda i, r, f: (0, 0)
    part = lambda i, r, f: (0, i)
    return kernel_call(
        functools.partial(attend_kernel, chunk=chunk),
        grid_spec=pltpu.PrefetchScalarGridSpec(
            num_scalar_prefetch=2,
            grid=(count // tile,),
            in_specs=[
                pl.BlockSpec((HEAD_DIM, tile), part),
                pl.BlockSpec((HEAD_DIM, total), whole),
                pl.BlockSpec((HEAD_DIM, total), whole),
                pl.BlockSpec((1, tile), part),
                pl.BlockSpec((1, tile), part),
            ],
            out_specs=[pl.BlockSpec((HEAD_DIM, tile), part), pl.BlockSpec((1, tile), part)],
            scratch_shapes=[pltpu.VMEM((total, HEAD_DIM), BF)],
        ),
        out_shape=[
            jax.ShapeDtypeStruct((HEAD_DIM, count), F32),
            jax.ShapeDtypeStruct((1, count), F32),
        ],
        compiler_params=pltpu.CompilerParams(vmem_limit_bytes=(16 if total <= 4096 else 48) << 20),
        cost_estimate=lasting(15),
        least=1 << 30,
        name="attend",
    )(ranges, flip.reshape(1), queries, keys, values, rows.reshape(1, -1), first.reshape(1, -1))


def attend_back_kernel(
    ranges, flips, q_ref, k_ref, v_ref, row_ref, first_ref, out_ref, log_ref, do_ref,
    dq_ref, parts_ref, k_rows, v_rows, dk_ref, dv_ref, chunk,
):
    tile = pl.program_id(0)
    total = k_ref.shape[1]
    copies, blocks, _, _, sub = parts_ref.shape

    @pl.when(tile == 0)
    def _():
        for base in range(0, total, chunk):
            k_rows[base : base + chunk, :] = k_ref[:, base : base + chunk].T
            v_rows[base : base + chunk, :] = v_ref[:, base : base + chunk].T
        dk_ref[...] = jnp.zeros_like(dk_ref)
        dv_ref[...] = jnp.zeros_like(dv_ref)

    queries, grads = q_ref[...], do_ref[...]
    rows, first = row_ref[...], first_ref[...]
    log_total = log_ref[...]
    delta = jnp.sum(grads.astype(F32) * out_ref[...], axis=0, keepdims=True)

    def work(masked):
        def step(index, acc):
            base = pl.multiple_of(index * chunk, chunk)
            span = pl.ds(base, chunk)
            score = jnp.dot(k_rows[span, :], queries, preferred_element_type=F32)
            weights = jnp.exp(score - log_total)
            if masked:
                allowed = allowed_keys(base, flips[0], chunk, rows, first)
                weights = jnp.where(allowed, weights, 0.0)
            grad_weights = jnp.dot(v_rows[span, :], grads, preferred_element_type=F32)
            grad_score = (weights * (grad_weights - delta)).astype(BF)
            dv_ref[:, span] += dg(grads, weights.astype(BF), ((1,), (1,)))
            dk_ref[:, span] += dg(queries, grad_score, ((1,), (1,)))
            return acc + jnp.dot(k_ref[:, span], grad_score, preferred_element_type=F32)

        return step

    acc = jnp.zeros(queries.shape, F32)
    acc = lax.fori_loop(ranges[tile, 0], ranges[tile, 1], work(True), acc)
    acc = lax.fori_loop(ranges[tile, 1], ranges[tile, 2], work(False), acc)
    dq = lax.fori_loop(ranges[tile, 2], ranges[tile, 3], work(True), acc).astype(BF)
    for block in range(dq_ref.shape[0]):
        dq_ref[block] = dq[:, block * sub : (block + 1) * sub]

    @pl.when(tile == pl.num_programs(0) - 1)
    def _():
        for block in range(blocks):
            for copy in range(copies):
                at = (block * copies + copy) * sub
                parts_ref[copy, block, 0] = dk_ref[:, at : at + sub].astype(BF)
                parts_ref[copy, block, 1] = dv_ref[:, at : at + sub].astype(BF)


def attend_back(queries, keys, values, rows, first, flip, out, log_total, grads, sub, tile=512, chunk=1024):
    count, total = queries.shape[1], keys.shape[1]
    blocks, copies = count // sub, total // count
    tile = min(tile, count)
    chunk = min(chunk, total)
    ranges = tile_ranges(rows, first, tile, chunk)
    whole = lambda i, r, f: (0, 0)
    part = lambda i, r, f: (0, i)
    return kernel_call(
        functools.partial(attend_back_kernel, chunk=chunk),
        grid_spec=pltpu.PrefetchScalarGridSpec(
            num_scalar_prefetch=2,
            grid=(count // tile,),
            in_specs=[
                pl.BlockSpec((HEAD_DIM, tile), part),
                pl.BlockSpec((HEAD_DIM, total), whole),
                pl.BlockSpec((HEAD_DIM, total), whole),
                pl.BlockSpec((1, tile), part),
                pl.BlockSpec((1, tile), part),
                pl.BlockSpec((HEAD_DIM, tile), part),
                pl.BlockSpec((1, tile), part),
                pl.BlockSpec((HEAD_DIM, tile), part),
            ],
            out_specs=[
                pl.BlockSpec((tile // sub, HEAD_DIM, sub), lambda i, r, f: (i, 0, 0)),
                pl.BlockSpec((copies, blocks, 2, HEAD_DIM, sub), lambda i, r, f: (0, 0, 0, 0, 0)),
            ],
            scratch_shapes=[
                pltpu.VMEM((total, HEAD_DIM), BF),
                pltpu.VMEM((total, HEAD_DIM), BF),
                pltpu.VMEM((HEAD_DIM, total), F32),
                pltpu.VMEM((HEAD_DIM, total), F32),
            ],
        ),
        out_shape=[
            jax.ShapeDtypeStruct((blocks, HEAD_DIM, sub), BF),
            jax.ShapeDtypeStruct((copies, blocks, 2, HEAD_DIM, sub), BF),
        ],
        compiler_params=pltpu.CompilerParams(vmem_limit_bytes=(24 if total <= 4096 else 60) << 20),
        cost_estimate=lasting(17),
        least=1 << 30,
        name="attend_back",
    )(ranges, flip.reshape(1), queries, keys, values, rows.reshape(1, -1), first.reshape(1, -1), out, log_total, grads)


EPSILON = 1e-05
SWAP = [(0, 1), (1, 0)]


def after(values, token):
    return lax.optimization_barrier((values, token))[0]


def over_x(value):
    return lax.ppermute(value, "tp", SWAP)


def over_blk(value, bit):
    return lax.ppermute(value, "blk", [(i, i ^ bit) for i in range(lax.axis_size("blk"))])


def normalize(values):
    centre = values - jnp.mean(values, axis=-1, keepdims=True)
    spread = lax.rsqrt(jnp.mean(centre * centre, axis=-1, keepdims=True) + EPSILON)
    return centre * spread, spread


def norm_back(values, gain, grad):
    hat, spread = normalize(values)
    scaled = grad * gain
    through = spread * (
        scaled
        - jnp.mean(scaled, axis=-1, keepdims=True)
        - hat * jnp.mean(scaled * hat, axis=-1, keepdims=True)
    )
    return through, jnp.sum(grad * hat, axis=0), jnp.sum(grad, axis=0)


def clip_rows(positions, clip_lengths):
    index = jnp.arange(clip_lengths.shape[0], dtype=jnp.int32)
    starts = jnp.sum(jnp.where(index[None, :] < index[:, None], clip_lengths[None, :], 0), axis=1)
    ends = starts + clip_lengths
    segment = jnp.sum((positions[:, None] >= ends[None, :]).astype(jnp.int32), axis=1)
    match = segment[:, None] == index[None, :]
    first = jnp.sum(jnp.where(match, starts[None, :], 0), axis=1)
    return segment, first


def matmul(left, right):
    return jnp.dot(left, right, preferred_element_type=F32)


def matmul_nt(left, right):
    return dg(left, right, ((1,), (1,)))


def matmul_tn(left, right):
    return dg(left, right, ((0,), (0,)))


def first_hop(weight, core):
    return over_x(halves(weight, core))


def weld_kernel(core, *refs):
    count = len(refs) // 3
    for which in range(count):
        first, second, out = refs[which], refs[count + which], refs[2 * count + which]
        chosen = pl.program_id(0) == core[0]

        @pl.when(chosen)
        def _():
            out[...] = first[...]

        @pl.when(jnp.logical_not(chosen))
        def _():
            out[...] = second[...]


def weld(own, other, core):
    outs = [jax.ShapeDtypeStruct((2 * a.shape[0], a.shape[1]), a.dtype) for a in own]
    return kernel_call(
        weld_kernel,
        grid_spec=pltpu.PrefetchScalarGridSpec(
            num_scalar_prefetch=1,
            grid=(2,),
            in_specs=[whole_spec(a) for a in list(own) + list(other)],
            out_specs=[pl.BlockSpec(a.shape, lambda i, c: (i, 0)) for a in own],
        ),
        out_shape=outs,
        compiler_params=pltpu.CompilerParams(vmem_limit_bytes=24 << 20),
        cost_estimate=lasting(4),
        name="weld",
    )(core.reshape(1), *own, *other)


def in_order(own, other, tp):
    return jnp.concatenate([jnp.where(tp == 0, own, other), jnp.where(tp == 0, other, own)])


def whole_spec(array):
    shape = array.shape
    return pl.BlockSpec(shape, lambda *_: (0,) * len(shape))


def norm_rows(values):
    centre = values - jnp.mean(values, axis=-1, keepdims=True)
    spread = lax.rsqrt(jnp.mean(centre * centre, axis=-1, keepdims=True) + EPSILON)
    return centre * spread, spread


def norm_rows_back(values, gain, grad):
    hat, spread = norm_rows(values)
    scaled = grad * gain
    through = spread * (
        scaled
        - jnp.mean(scaled, axis=-1, keepdims=True)
        - hat * jnp.mean(scaled * hat, axis=-1, keepdims=True)
    )
    return through, jnp.sum(grad * hat, axis=0, keepdims=True), jnp.sum(grad, axis=0, keepdims=True)


def text_weights(keys, queries, allowed):
    score = dg(keys, queries, ((0,), (0,)))
    score = jnp.where(allowed, score, NEGATIVE)
    expo = jnp.exp(score - jnp.max(score, axis=0, keepdims=True))
    expo = jnp.where(allowed, expo, 0.0)
    return expo / jnp.sum(expo, axis=0, keepdims=True)


def embed_kernel(x_ref, gain, shift, wq_ref, wk_ref, wv_ref, rows_ref, out_ref, scale):
    hat, _ = norm_rows(x_ref[...].astype(F32))
    rows = (hat * gain[...] + shift[...]).astype(BF)
    rows_ref[...] = rows
    blocks, _, _, sub = out_ref.shape
    copies = rows.shape[0] // sub
    for which, weight in enumerate([wq_ref, wk_ref, wv_ref]):
        value = jnp.dot(rows, weight[...], preferred_element_type=F32)
        value = (value * scale if which == 0 else value).astype(BF).T
        for block in range(blocks):
            head, copy = divmod(block, copies)
            out_ref[block, which] = value[
                head * HEAD_DIM : (head + 1) * HEAD_DIM, copy * sub : (copy + 1) * sub
            ]


def embed(frames, gain, shift, weights, blocks, sub, scale):
    args = [frames, gain, shift, *weights]
    outs = [
        jax.ShapeDtypeStruct(frames.shape, BF),
        jax.ShapeDtypeStruct((blocks, 3, HEAD_DIM, sub), BF),
    ]
    return kernel_call(
        functools.partial(embed_kernel, scale=scale),
        grid=(1,),
        in_specs=[whole_spec(a) for a in args],
        out_specs=[whole_spec(o) for o in outs],
        out_shape=outs,
        compiler_params=pltpu.CompilerParams(vmem_limit_bytes=24 << 20),
        cost_estimate=lasting(5),
        least=1 << 30,
        name="embed",
    )(*args)


def cross_kernel(
    a_own, a_other, x_ref, gain_two, shift_two, gain_three, shift_three, wo_own, wo_other,
    wq_own, wq_other, wc_own, wc_other, tk_ref, tv_ref, segment, text_segment,
    x1_ref, x2_ref, h2_ref, h3_ref, q_ref, oc_ref, c_own, c_other, scale,
):
    width = a_own.shape[0]
    change = jnp.dot(a_own[...].T, wo_own[...], preferred_element_type=F32)
    change += jnp.dot(a_other[...].T, wo_other[...], preferred_element_type=F32)
    x1 = x_ref[...].astype(F32) + change
    x1_ref[...] = x1
    hat, _ = norm_rows(x1)
    h2 = (hat * gain_two[...] + shift_two[...]).astype(BF)
    h2_ref[...] = h2
    allowed = text_segment[...] == segment[...]
    crosses = []
    for side, wq in enumerate([wq_own, wq_other]):
        qc = (jnp.dot(h2, wq[...], preferred_element_type=F32) * scale).astype(BF)
        q_t = qc.T
        q_ref[side] = q_t
        parts = []
        for head in range(width // HEAD_DIM):
            span = slice(head * HEAD_DIM, (head + 1) * HEAD_DIM)
            weights = text_weights(tk_ref[side, span, :], q_t[span, :], allowed)
            parts.append(
                jnp.dot(tv_ref[side, span, :], weights.astype(BF), preferred_element_type=F32)
            )
        oc = jnp.concatenate(parts, axis=0)
        oc_ref[side] = oc
        crossed = oc.astype(BF)
        (c_own if side == 0 else c_other)[...] = crossed
        crosses.append(crossed.T)
    change = jnp.dot(crosses[0], wc_own[...], preferred_element_type=F32)
    change += jnp.dot(crosses[1], wc_other[...], preferred_element_type=F32)
    x2 = x1 + change
    x2_ref[...] = x2
    hat, _ = norm_rows(x2)
    h3_ref[...] = (hat * gain_three[...] + shift_three[...]).astype(BF)


def cross_forward(a_both, x_own, norms, output_both, query_both, cross_both, tk, tv, segment, text_segment, scale):
    half, depth = x_own.shape
    width = a_both[0].shape[0]
    args = [*a_both, x_own, *norms, *output_both, *query_both, *cross_both, tk, tv, segment, text_segment]
    shape = jax.ShapeDtypeStruct
    outs = [
        shape((half, depth), F32), shape((half, depth), F32), shape((half, depth), BF),
        shape((half, depth), BF), shape((2, width, half), BF), shape((2, width, half), F32),
        shape((width, half), BF), shape((width, half), BF),
    ]
    return kernel_call(
        functools.partial(cross_kernel, scale=scale),
        grid=(1,),
        in_specs=[whole_spec(a) for a in args],
        out_specs=[whole_spec(o) for o in outs],
        out_shape=outs,
        compiler_params=pltpu.CompilerParams(vmem_limit_bytes=28 << 20),
        cost_estimate=lasting(7),
        name="cross_forward",
    )(*args)


def cross_back_kernel(
    dh_own, dh_got, dy_ref, x1_ref, x2_ref, gain_two, gain_three, wo_own, wo_other,
    wq_own, wq_other, wc_own, wc_other, tk_ref, tv_ref, q_ref, oc_ref, segment, text_segment,
    dx1_ref, dx1_low_ref, dx2_low_ref, dq_own, dq_other, da_own, da_other, text_own, text_other,
    small_ref, scale,
):
    width = tk_ref.shape[1]
    dh3 = dh_own[...].astype(F32) + dh_got[...].astype(F32)
    through, gain_grad, shift_grad = norm_rows_back(x2_ref[...], gain_three[...], dh3)
    small_ref[2:3, :] = gain_grad
    small_ref[3:4, :] = shift_grad
    dx2 = dy_ref[...].astype(F32) + through
    low = dx2.astype(BF)
    dx2_low_ref[...] = low
    allowed = text_segment[...] == segment[...]
    dqs = []
    for side, wc in enumerate([wc_own, wc_other]):
        dc_t = dg(low, wc[...], ((1,), (1,))).astype(BF).T
        parts = []
        for head in range(width // HEAD_DIM):
            span = slice(head * HEAD_DIM, (head + 1) * HEAD_DIM)
            queries, grads = q_ref[side, span, :], dc_t[span, :]
            weights = text_weights(tk_ref[side, span, :], queries, allowed)
            delta = jnp.sum(grads.astype(F32) * oc_ref[side, span, :], axis=0, keepdims=True)
            grad_weights = dg(tv_ref[side, span, :], grads, ((0,), (0,)))
            grad_score = (weights * (grad_weights - delta)).astype(BF)
            dq = jnp.dot(tk_ref[side, span, :], grad_score, preferred_element_type=F32).astype(BF)
            parts.append(dq * jnp.asarray(scale, BF))
            text_ref = text_own if side == 0 else text_other
            text_ref[0, span, :] = dg(queries, grad_score, ((1,), (1,))).astype(text_ref.dtype)
            text_ref[1, span, :] = dg(grads, weights.astype(BF), ((1,), (1,))).astype(text_ref.dtype)
        dq = jnp.concatenate(parts, axis=0)
        (dq_own if side == 0 else dq_other)[...] = dq
        dqs.append(dq.T)
    dh2 = dg(dqs[0], wq_own[...], ((1,), (1,))) + dg(dqs[1], wq_other[...], ((1,), (1,)))
    through, gain_grad, shift_grad = norm_rows_back(x1_ref[...], gain_two[...], dh2)
    small_ref[0:1, :] = gain_grad
    small_ref[1:2, :] = shift_grad
    dx1 = dx2 + through
    dx1_ref[...] = dx1
    low = dx1.astype(BF)
    dx1_low_ref[...] = low
    for ref, wo in [(da_own, wo_own), (da_other, wo_other)]:
        ref[...] = dg(low, wo[...], ((1,), (1,))).astype(BF).T


def cross_backward(
    dh_own, dh_got, dy_own, x1, x2, gain_two, gain_three, output_both, query_both, cross_both,
    tk, tv, q_t, oc, segment, text_segment, scale,
):
    half, depth = x1.shape
    width, text = tk.shape[1], tk.shape[2]
    args = [
        dh_own, dh_got, dy_own, x1, x2, gain_two, gain_three, *output_both, *query_both,
        *cross_both, tk, tv, q_t, oc, segment, text_segment,
    ]
    shape = jax.ShapeDtypeStruct
    outs = [
        shape((half, depth), F32), shape((half, depth), BF), shape((half, depth), BF),
        *[shape((width, half), BF)] * 4, shape((2, width, text), F32), shape((2, width, text), BF),
        shape((4, depth), F32),
    ]
    return kernel_call(
        functools.partial(cross_back_kernel, scale=scale),
        grid=(1,),
        in_specs=[whole_spec(a) for a in args],
        out_specs=[whole_spec(o) for o in outs],
        out_shape=outs,
        compiler_params=pltpu.CompilerParams(vmem_limit_bytes=28 << 20),
        cost_estimate=lasting(9),
        name="cross_backward",
    )(*args)


def hidden_kernel(tp_ref, h_own, h_other, dy_ref, wi_ref, wo_ref, g_ref, du_ref, own_ref, other_ref, acc):
    step, half = pl.program_id(0), h_own.shape[0]
    tp = tp_ref[0]

    @pl.when(step == 0)
    def _():
        acc[...] = jnp.zeros_like(acc)

    for part, h_ref in enumerate([h_own, h_other]):
        rows = slice(part * half, (part + 1) * half)
        base = jnp.where(tp == part, 0, half)
        dy = dy_ref[pl.ds(pl.multiple_of(base, half), half), :]
        pre = jnp.dot(h_ref[...], wi_ref[...], preferred_element_type=F32)
        cdf = 0.5 * (1.0 + lax.erf(pre * (0.5**0.5)))
        density = jnp.exp(-0.5 * pre * pre) * 0.3989422804014327
        g_ref[rows, :] = (pre * cdf).astype(BF)
        grad = dg(dy, wo_ref[...], ((1,), (1,)))
        grad = (grad * (cdf + pre * density)).astype(BF)
        du_ref[rows, :] = grad
        acc[rows, :] += dg(grad, wi_ref[...], ((1,), (1,)))

    @pl.when(step == pl.num_programs(0) - 1)
    def _():
        own_ref[...] = acc[:half, :]
        other_ref[...] = acc[half:, :].astype(BF)


def hidden_pass(h_own, h_other, cotangent, inner, outer, tp, tile=512):
    half, depth = h_own.shape
    units = inner.shape[1]
    shape = jax.ShapeDtypeStruct
    return kernel_call(
        hidden_kernel,
        grid_spec=pltpu.PrefetchScalarGridSpec(
            num_scalar_prefetch=1,
            grid=(units // tile,),
            in_specs=[
                whole_spec(h_own), whole_spec(h_other), whole_spec(cotangent),
                pl.BlockSpec((depth, tile), lambda i, t: (0, i)),
                pl.BlockSpec((tile, depth), lambda i, t: (i, 0)),
            ],
            out_specs=[
                pl.BlockSpec((2 * half, tile), lambda i, t: (0, i)),
                pl.BlockSpec((2 * half, tile), lambda i, t: (0, i)),
                pl.BlockSpec((half, depth), lambda i, t: (0, 0)),
                pl.BlockSpec((half, depth), lambda i, t: (0, 0)),
            ],
            scratch_shapes=[pltpu.VMEM((2 * half, depth), F32)],
        ),
        out_shape=[
            shape((2 * half, units), BF), shape((2 * half, units), BF),
            shape((half, depth), F32), shape((half, depth), BF),
        ],
        compiler_params=pltpu.CompilerParams(vmem_limit_bytes=20 << 20),
        cost_estimate=lasting(10),
        least=1 << 30,
        name="hidden_pass",
    )(tp.reshape(1), h_own, h_other, cotangent, inner, outer)


def hidden_grads_kernel(
    place, h_own, h_other, dy_ref, g_ref, du_ref, wo_ref, both_ref, y_own, y_other, h_all, dy_all, acc
):
    step, half = pl.program_id(0), h_own.shape[0]
    tp = place[0]

    @pl.when(step == 0)
    def _():
        acc[...] = jnp.zeros_like(acc)
        h_all[:half, :] = h_own[...]
        h_all[half:, :] = h_other[...]
        for part in range(2):
            base = jnp.where(tp == part, 0, half)
            dy_all[part * half : (part + 1) * half, :] = dy_ref[
                pl.ds(pl.multiple_of(base, half), half), :
            ]

    acc[...] += jnp.dot(g_ref[...], wo_ref[...], preferred_element_type=F32)
    depth = h_own.shape[1]
    both_ref[:, :depth] = jnp.dot(g_ref[...].T, dy_all[...], preferred_element_type=F32).astype(BF)
    both_ref[:, depth:] = jnp.dot(du_ref[...].T, h_all[...], preferred_element_type=F32).astype(BF)

    @pl.when(step == pl.num_programs(0) - 1)
    def _():
        y_own[...] = acc[:half, :]
        y_other[...] = acc[half:, :].astype(BF)


def hidden_grads(h_own, h_other, cotangent, g, du, outer, tp, tile=256):
    half, depth = h_own.shape
    units = outer.shape[0]
    shape = jax.ShapeDtypeStruct
    across = lambda i, p: (0, i)
    down = lambda i, p: (i, 0)
    still = lambda i, p: (0, 0)
    return kernel_call(
        hidden_grads_kernel,
        grid_spec=pltpu.PrefetchScalarGridSpec(
            num_scalar_prefetch=1,
            grid=(units // tile,),
            in_specs=[
                whole_spec(h_own), whole_spec(h_other), whole_spec(cotangent),
                pl.BlockSpec((2 * half, tile), across), pl.BlockSpec((2 * half, tile), across),
                pl.BlockSpec((tile, depth), down),
            ],
            out_specs=[
                pl.BlockSpec((tile, 2 * depth), down),
                pl.BlockSpec((half, depth), still), pl.BlockSpec((half, depth), still),
            ],
            scratch_shapes=[
                pltpu.VMEM((2 * half, depth), BF),
                pltpu.VMEM((2 * half, depth), BF),
                pltpu.VMEM((2 * half, depth), F32),
            ],
        ),
        out_shape=[
            shape((units, 2 * depth), BF), shape((half, depth), F32), shape((half, depth), BF),
        ],
        compiler_params=pltpu.CompilerParams(vmem_limit_bytes=20 << 20),
        cost_estimate=lasting(9),
        least=1 << 30,
        least_out=LARGE,
        name="hidden_grads",
    )(tp.reshape(1), h_own, h_other, cotangent, g, du, outer)


def hidden_out_kernel(both_ref, outer_ref, inner_ref):
    depth = outer_ref.shape[1]
    outer_ref[...] = both_ref[:, :depth].astype(F32)
    inner_ref[...] = both_ref[:, depth:].astype(F32).T


def hidden_out(both, tile=256):
    units, depth = both.shape[0], both.shape[1] // 2
    return kernel_call(
        hidden_out_kernel,
        grid=(units // tile,),
        in_specs=[pl.BlockSpec((tile, 2 * depth), lambda i: (i, 0))],
        out_specs=[
            pl.BlockSpec((tile, depth), lambda i: (i, 0)), pl.BlockSpec((depth, tile), lambda i: (0, i))
        ],
        out_shape=[
            jax.ShapeDtypeStruct((units, depth), F32), jax.ShapeDtypeStruct((depth, units), F32)
        ],
        compiler_params=pltpu.CompilerParams(vmem_limit_bytes=16 << 20),
        cost_estimate=lasting(9),
        name="hidden_out",
    )(both)


def pair_grads_kernel(core, *refs):
    send, keep = refs[-2:]
    ins = refs[:-2]
    rows = send.shape[0]
    for which in range(len(ins) // 4):
        left_own, left_other, right_own, right_other = ins[4 * which : 4 * which + 4]
        depth = right_own.shape[1]
        for ref, side in [(send, 1 - core[0]), (keep, core[0])]:
            span = pl.ds(pl.multiple_of(side * rows, rows), rows)
            total = jnp.dot(left_own[span, :], right_own[...], preferred_element_type=F32)
            total += jnp.dot(left_other[span, :], right_other[...], preferred_element_type=F32)
            ref[:, which * depth : (which + 1) * depth] = total.astype(BF)


def pair_grads(groups, core):
    args = [array for group in groups for array in group]
    features, depth = groups[0][0].shape[0], groups[0][2].shape[1]
    columns = depth * len(groups)
    out = jax.ShapeDtypeStruct((features // 2, columns), BF)
    return kernel_call(
        pair_grads_kernel,
        grid_spec=pltpu.PrefetchScalarGridSpec(
            num_scalar_prefetch=1,
            grid=(1,),
            in_specs=[whole_spec(a) for a in args],
            out_specs=[whole_spec(out), whole_spec(out)],
        ),
        out_shape=[out, out],
        compiler_params=pltpu.CompilerParams(vmem_limit_bytes=24 << 20),
        cost_estimate=lasting(4),
        name="pair_grads",
    )(core.reshape(1), *args)


def fold_kernel(sides, *refs):
    count = len(refs) // 4
    ins, outs = refs[: 2 * count], refs[2 * count :]
    first = pl.program_id(0) < pl.num_programs(0) // 2
    for which in range(count):
        total = ins[2 * which][...].astype(F32) + ins[2 * which + 1][...].astype(F32)
        total = total.astype(BF)

        @pl.when(first)
        def _():
            outs[2 * which][...] = total

        @pl.when(jnp.logical_not(first))
        def _():
            outs[2 * which + 1][...] = total


def fold(pairs, sides):
    least = min(keep.shape[0] for keep, _ in pairs)
    if least % 16:
        sums = [(keep.astype(F32) + got.astype(F32)).astype(BF) for keep, got in pairs]
        return [(halves(t, 1 - side), halves(t, side)) for t, side in zip(sums, sides)]
    parts = 2 if least % 32 == 0 else 1
    args, in_specs, out_specs, outs = [], [], [], []
    for which, (keep, got) in enumerate(pairs):
        rows, columns = keep.shape
        block = rows // (2 * parts)
        place = lambda i, s, which=which: (
            jnp.where(i < parts, (1 - s[which]) * parts + i, s[which] * parts + i - parts), 0
        )
        args += [keep, got]
        in_specs += [pl.BlockSpec((block, columns), place)] * 2
        out_specs += [
            pl.BlockSpec((block, columns), lambda i, s: (jnp.minimum(i, parts - 1), 0)),
            pl.BlockSpec((block, columns), lambda i, s: (jnp.maximum(i - parts, 0), 0)),
        ]
        outs += [jax.ShapeDtypeStruct((rows // 2, columns), BF)] * 2
    got = kernel_call(
        fold_kernel,
        grid_spec=pltpu.PrefetchScalarGridSpec(
            num_scalar_prefetch=1,
            grid=(2 * parts,),
            in_specs=in_specs,
            out_specs=out_specs,
        ),
        out_shape=outs,
        compiler_params=pltpu.CompilerParams(vmem_limit_bytes=12 << 20),
        cost_estimate=lasting(3),
        name="fold",
    )(jnp.stack(sides), *args)
    return [(got[2 * i], got[2 * i + 1]) for i in range(len(pairs))]


def piece_places(count, order):
    places = []
    for device in range(count):
        index = 0
        for bit in order:
            index = index * 2 + (device // bit) % 2
        places.append(index)
    return places


def widen_kernel(devices, *refs, group, height):
    ins, outs = refs[: 2 * group], refs[2 * group :]
    columns = ins[0].shape[2]
    for slot in range(group):
        rows = ins[slot].shape[1]
        place = slice(slot * rows, (slot + 1) * rows)
        width = outs[0].shape[1]
        for which in range(3):
            outs[which][place, :] = ins[slot][0, :, which * width : (which + 1) * width].astype(F32)
    turned = []
    for slot in range(group):
        source = ins[group + slot]
        place = slice(slot * height, (slot + 1) * height)
        depth = outs[3].shape[1]
        at = 0
        for which in range(3):
            filled, found = 0, []
            while filled < depth:
                part, column = divmod(at, columns)
                count = min(columns - column, depth - filled)
                found.append(
                    source[0, part * height : (part + 1) * height, column : column + count]
                )
                if which < 2:
                    outs[3 + which][place, filled : filled + count] = found[-1].astype(F32)
                filled, at = filled + count, at + count
        turned.append(jnp.concatenate([value.astype(F32) for value in found], axis=1))
    outs[5][...] = jnp.concatenate(turned, axis=0).T


def widen(gathered, head_order, pair_order, rows, height, width, depth):
    count, total, columns = gathered.shape
    group = max(4, 128 // height)
    tables = []
    for order in (head_order, pair_order):
        places = piece_places(count, order)
        tables.append([places.index(place) for place in range(count)])
    spec = lambda kind, slot: pl.BlockSpec(
        (1, rows, columns), lambda j, t: (t[kind, j * group + slot], kind, 0)
    )
    shape = jax.ShapeDtypeStruct
    outs = [shape((count * rows, width), F32)] * 3 + [shape((count * height, depth), F32)] * 2
    outs += [shape((depth, count * height), F32)]
    down = lambda j, t: (j, 0)
    return kernel_call(
        functools.partial(widen_kernel, group=group, height=height),
        grid_spec=pltpu.PrefetchScalarGridSpec(
            num_scalar_prefetch=1,
            grid=(count // group,),
            in_specs=[spec(kind, slot) for kind in range(2) for slot in range(group)],
            out_specs=[pl.BlockSpec((group * rows, width), down)] * 3
            + [pl.BlockSpec((group * height, depth), down)] * 2
            + [pl.BlockSpec((depth, group * height), lambda j, t: (0, j))],
        ),
        out_shape=outs,
        compiler_params=pltpu.CompilerParams(vmem_limit_bytes=24 << 20),
        cost_estimate=lasting(7),
        name="widen",
    )(jnp.asarray(tables, jnp.int32), *[gathered] * (2 * group))


class Stream:
    def __init__(self, send, keep, order, blk):
        self.order, self.blk, self.phase, self.keep = order, blk, 0, keep
        self.got, self.sent = over_blk(send, order[0]), send

    def step(self):
        count, phase = len(self.order), self.phase
        if phase is None:
            return
        self.phase += 1
        if phase < count - 1:
            bit = self.order[phase + 1]
            ((send, self.keep),) = fold([(self.keep, self.got)], [(self.blk // bit) % 2])
            self.got, self.sent = over_blk(send, bit), send
        elif phase < 2 * count - 1:
            if phase == count - 1:
                piece = self.keep.astype(F32) + self.got.astype(F32)
                self.keep = piece.astype(BF)[None]
            else:
                self.keep = join(self.keep, self.got)
            self.got, self.sent = over_blk(self.keep, self.order[2 * count - 2 - phase]), self.keep
            if phase == 2 * count - 2:
                self.phase = None

    def piece(self):
        return (self.keep.astype(F32) + self.got.astype(F32)).astype(BF)

    def result(self, widths):
        return unpack(self.keep, self.got, self.order, widths)


def step_together(streams):
    bits = [stream.order[stream.phase + 1] for stream in streams]
    sides = [(stream.blk // bit) % 2 for stream, bit in zip(streams, bits)]
    halved = fold([(stream.keep, stream.got) for stream in streams], sides)
    for stream, (send, keep), bit in zip(streams, halved, bits):
        stream.phase += 1
        stream.keep, stream.sent, stream.got = keep, send, over_blk(send, bit)


def last_kernel(head_keep, head_got, pair_keep, pair_got, out_ref):
    rows, columns = head_keep.shape
    out_ref[:rows, :] = (head_keep[...].astype(F32) + head_got[...].astype(F32)).astype(BF)
    height = pair_keep.shape[0]
    pair = (pair_keep[...].astype(F32) + pair_got[...].astype(F32)).astype(BF)
    for part in range(pair.shape[1] // columns):
        at = rows + part * height
        out_ref[at : at + height, :] = pair[:, part * columns : (part + 1) * columns]


def last_halves(heads, pairs):
    args = [heads.keep, heads.got, pairs.keep, pairs.got]
    rows, columns = heads.keep.shape
    height = pairs.keep.shape[0] * (pairs.keep.shape[1] // columns)
    out = jax.ShapeDtypeStruct((rows + height, columns), BF)
    return kernel_call(
        last_kernel,
        grid=(1,),
        in_specs=[whole_spec(a) for a in args],
        out_specs=whole_spec(out),
        out_shape=out,
        cost_estimate=lasting(2),
        name="last_halves",
    )(*args)


class Butterfly:
    def __init__(self, value, order, wire):
        self.value, self.order, self.phase, self.wire = value, order, 0, wire
        self.got, self.sent = over_blk(value.astype(wire), order[0]), value

    def step(self):
        if self.phase is None:
            return
        self.value = self.value + self.got.astype(F32)
        self.phase += 1
        if self.phase < len(self.order):
            self.got = over_blk(self.value.astype(self.wire), self.order[self.phase])
            self.sent = self.value
        else:
            self.got, self.phase = jnp.zeros((), F32), None


def meet(streams, others):
    got, others = lax.optimization_barrier(([s.got for s in streams], others))
    for stream, value in zip(streams, got):
        stream.got = value
    return others


def project_back_kernel(tp, back_ref, *refs):
    weights, (own_ref, other_ref) = refs[:3], refs[3:]
    half = own_ref.shape[0]
    total = None
    for which, weight in enumerate(weights):
        part = dg(back_ref[which].T, weight[...], ((1,), (1,)))
        total = part if total is None else total + part
    first, second = total[:half, :], total[half:, :]
    own_ref[...] = jnp.where(tp[0] == 0, first, second)
    other_ref[...] = jnp.where(tp[0] == 0, second, first).astype(BF)


def project_back(back, weights, tp):
    rows, depth = back.shape[2], weights[0].shape[0]
    args = [back, *weights]
    outs = [
        jax.ShapeDtypeStruct((rows // 2, depth), F32), jax.ShapeDtypeStruct((rows // 2, depth), BF)
    ]
    return kernel_call(
        project_back_kernel,
        grid_spec=pltpu.PrefetchScalarGridSpec(
            num_scalar_prefetch=1,
            grid=(1,),
            in_specs=[whole_spec(a) for a in args],
            out_specs=[whole_spec(o) for o in outs],
        ),
        out_shape=outs,
        compiler_params=pltpu.CompilerParams(vmem_limit_bytes=16 << 20),
        cost_estimate=lasting(4),
        name="project_back",
    )(tp.reshape(1), *args)


def head_grads_kernel(core, back_ref, rows_ref, send, keep, turned):
    turned[...] = rows_ref[...].T
    rows, width = send.shape[0], back_ref.shape[1]
    for ref, side in [(send, 1 - core[0]), (keep, core[0])]:
        part = turned[pl.ds(pl.multiple_of(side * rows, rows), rows), :]
        for which in range(3):
            ref[:, which * width : (which + 1) * width] = dg(
                part, back_ref[which], ((1,), (1,))
            ).astype(BF)


def head_grads(back, normed, core):
    rows, depth = normed.shape
    out = jax.ShapeDtypeStruct((depth // 2, 3 * back.shape[1]), BF)
    return kernel_call(
        head_grads_kernel,
        grid_spec=pltpu.PrefetchScalarGridSpec(
            num_scalar_prefetch=1,
            grid=(1,),
            in_specs=[whole_spec(back), whole_spec(normed)],
            out_specs=[whole_spec(out), whole_spec(out)],
            scratch_shapes=[pltpu.VMEM((depth, rows), BF)],
        ),
        out_shape=[out, out],
        compiler_params=pltpu.CompilerParams(vmem_limit_bytes=16 << 20),
        cost_estimate=lasting(4),
        name="head_grads",
    )(core.reshape(1), back, normed)


def combine_kernel(dq_ref, parts_ref, got_ref, out_ref, scale):
    out_ref[:, 0] = dq_ref[...] * jnp.asarray(scale, BF)
    out_ref[:, 1:] = (parts_ref[0].astype(F32) + got_ref[...].astype(F32)).astype(BF)


def combine(dq, parts, got, scale):
    blocks, _, sub = dq.shape
    part = min(4, blocks)
    return kernel_call(
        functools.partial(combine_kernel, scale=scale),
        grid=(blocks // part,),
        in_specs=[
            pl.BlockSpec((part, HEAD_DIM, sub), lambda i: (i, 0, 0)),
            pl.BlockSpec((1, part, 2, HEAD_DIM, sub), lambda i: (0, i, 0, 0, 0)),
            pl.BlockSpec((part, 2, HEAD_DIM, sub), lambda i: (i, 0, 0, 0)),
        ],
        out_specs=pl.BlockSpec((part, 3, HEAD_DIM, sub), lambda i: (i, 0, 0, 0)),
        out_shape=jax.ShapeDtypeStruct((blocks, 3, HEAD_DIM, sub), BF),
        cost_estimate=lasting(3.5),
        name="combine",
    )(dq, parts, got)


def join_kernel(low_ref, high_ref, out_ref):
    for part, ref in enumerate([low_ref, high_ref]):

        @pl.when(pl.program_id(0) == part)
        def _():
            out_ref[...] = ref[...]


def join(low, high):
    shape = low.shape
    still = lambda i: (0,) * len(shape)
    return kernel_call(
        join_kernel,
        grid=(2,),
        in_specs=[pl.BlockSpec(shape, still)] * 2,
        out_specs=pl.BlockSpec(shape, lambda i: (i,) + (0,) * (len(shape) - 1)),
        out_shape=jax.ShapeDtypeStruct((2 * shape[0],) + shape[1:], low.dtype),
        compiler_params=pltpu.CompilerParams(vmem_limit_bytes=12 << 20),
        cost_estimate=lasting(2),
        name="join",
    )(low, high)


def halves(value, which):
    rows = value.shape[0] // 2
    return lax.dynamic_slice_in_dim(value, which * rows, rows, 0)


def piece_index(order):
    blk = lax.axis_index("blk")
    index = 0
    for bit in order:
        index = index * 2 + (blk // bit) % 2
    return index


def unpack_kernel(index, low_ref, high_ref, *out_refs):
    low = pl.program_id(0) < pl.num_programs(0) // 2
    group, rows, _ = low_ref.shape
    at = 0
    for out_ref in out_refs:
        width = out_ref.shape[1]
        for source, chosen in [(low_ref, low), (high_ref, jnp.logical_not(low))]:

            @pl.when(chosen)
            def _():
                for slot in range(group):
                    place = (index[0] % group) ^ slot
                    place = pl.multiple_of(place * rows, rows)
                    out_ref[pl.ds(place, rows), :] = source[slot, :, at : at + width].astype(F32)

        at += width


def unpack(low, high, order, widths):
    count, rows, columns = low.shape
    group = min(4, count)
    steps = 2 * count // group
    place = lambda j, index: (jnp.bitwise_xor(index[0] // group, j), 0)
    return kernel_call(
        unpack_kernel,
        grid_spec=pltpu.PrefetchScalarGridSpec(
            num_scalar_prefetch=1,
            grid=(steps,),
            in_specs=[
                pl.BlockSpec(
                    (group, rows, columns), lambda j, i: (jnp.minimum(j, steps // 2 - 1), 0, 0)
                ),
                pl.BlockSpec(
                    (group, rows, columns), lambda j, i: (jnp.maximum(j - steps // 2, 0), 0, 0)
                ),
            ],
            out_specs=[pl.BlockSpec((group * rows, width), place) for width in widths],
        ),
        out_shape=[jax.ShapeDtypeStruct((2 * count * rows, width), F32) for width in widths],
        compiler_params=pltpu.CompilerParams(vmem_limit_bytes=24 << 20),
        cost_estimate=lasting(5),
        name="unpack",
    )(piece_index(order).reshape(1), low, high)


def shards(
    frames,
    clip_lengths,
    text_states,
    text_segments,
    gain_one,
    shift_one,
    gain_two,
    shift_two,
    gain_three,
    shift_three,
    query_weight,
    key_weight,
    value_weight,
    output_weight,
    cross_query,
    cross_key,
    cross_value,
    cross_output,
    inner_weight,
    outer_weight,
    cotangent,
):
    row_count, depth = frames.shape
    width_here = query_weight.shape[1]
    heads_here = width_here // HEAD_DIM
    blk_count, tp_count = lax.axis_size("blk"), lax.axis_size("tp")
    blk, tp = lax.axis_index("blk"), lax.axis_index("tp")
    core = blk % 2
    copies = blk_count // heads_here
    sub = row_count // copies
    half = row_count // tp_count
    mine = blk % copies
    scale = float(HEAD_DIM) ** (-0.5)
    bits = [1 << i for i in range(1, blk_count.bit_length() - 1)]
    order_one = [1] + bits
    order_two = [1, bits[1], bits[0]] + bits[2:]

    def own_rows(array):
        return lax.dynamic_slice_in_dim(array, tp * half, half, 0)

    def other_rows(array):
        return lax.dynamic_slice_in_dim(array, (1 - tp) * half, half, 0)

    row = lambda array: array.reshape(1, -1)
    qkv_weights = [query_weight, key_weight, value_weight]
    if sub % 128 == 0:
        normed_one, qkv = embed(
            frames, row(gain_one), row(shift_one), qkv_weights, blk_count, sub, scale
        )
    else:
        hat, _ = normalize(frames.astype(F32))
        normed_one = (hat * gain_one + shift_one).astype(BF)
        qkv = jnp.stack([dg(weight, normed_one, ((0,), (1,))) for weight in qkv_weights])
        qkv = (qkv * jnp.array([scale, 1.0, 1.0], F32)[:, None, None]).astype(BF)
        qkv = qkv.reshape(3, heads_here, HEAD_DIM, copies, sub).transpose(1, 3, 0, 2, 4)
        qkv = qkv.reshape(blk_count, 3, HEAD_DIM, sub)

    weights_two = [output_weight, cross_query, cross_output]
    hops = [first_hop(w, core) for w in after(weights_two, qkv)]
    text_k = dg(cross_key, text_states, ((0,), (1,))).astype(BF)
    text_v = dg(cross_value, text_states, ((0,), (1,))).astype(BF)
    text_own = jnp.stack([text_k, text_v])
    text_both = jnp.stack([text_own, over_x(text_own)], axis=1)

    def bring_heads(array):
        got = lax.all_to_all(array, "blk", 0, 0, tiled=True)
        return got.reshape(heads_here, copies, array.shape[1], HEAD_DIM, sub)

    got = lax.all_to_all(qkv, "blk", 0, 0, tiled=True)
    queries = got[:, 0].transpose(1, 0, 2).reshape(HEAD_DIM, blk_count * sub)
    both = got[:, 1:][:, :, :, None, :]
    bit = 1
    while bit < copies:
        both = jnp.concatenate([both, over_blk(both, bit)], axis=3)
        bit *= 2
    both = both.transpose(1, 2, 0, 3, 4).reshape(2, HEAD_DIM, blk_count * row_count)
    keys, values = both[0], both[1]
    rows_all = jnp.arange(blk_count, dtype=jnp.int32)[:, None] * row_count
    rows_all = (rows_all + mine * sub + jnp.arange(sub, dtype=jnp.int32)[None, :]).reshape(-1)
    _, first = clip_rows(rows_all, clip_lengths)
    flip = mine * sub
    out, log_total = attend(queries, keys, values, rows_all, first, flip)
    hops, out = lax.optimization_barrier((hops, out))
    output_both, query_both, cross_both = [
        list(pair) for pair in zip(weights_two, weld(hops, [over_blk(h, 1) for h in hops], core))
    ]

    out_low = out.astype(BF).reshape(HEAD_DIM, blk_count, sub).transpose(1, 0, 2)[:, None]
    attended = bring_heads(out_low)[:, :, 0]

    attended, output_both, query_both, cross_both = lax.optimization_barrier(
        (attended, output_both, query_both, cross_both)
    )

    def token_half(array, which):
        array = array.reshape(heads_here, tp_count, copies // tp_count, HEAD_DIM, sub)
        array = lax.dynamic_index_in_dim(array, which, 1, keepdims=False)
        return array.transpose(0, 2, 1, 3).reshape(width_here, half)

    a_own, a_sent = token_half(attended, tp), token_half(attended, 1 - tp)
    a_both = [a_own, over_x(a_sent)]

    rows = blk * row_count + tp * half + jnp.arange(half, dtype=jnp.int32)
    segment, _ = clip_rows(rows, clip_lengths)
    x_low = own_rows(frames)
    norms = [row(gain_two), row(shift_two), row(gain_three), row(shift_three)]
    segment, text_segment = segment.reshape(1, -1), text_segments.reshape(-1, 1)
    first_sum, second_sum, h2_own, h3_own, qc_t, oc_t, c_own, c_sent = cross_forward(
        a_both, x_low, norms, output_both, query_both, cross_both,
        text_both[0], text_both[1], segment, text_segment, scale,
    )

    h3_other = over_x(h3_own)
    hidden, grad_pre, dh3_own, dh3_sent = hidden_pass(
        h3_own, h3_other, cotangent, inner_weight, outer_weight, tp
    )
    dh3_got = over_x(dh3_sent)
    hidden_both, y_kept, y_sent = hidden_grads(
        h3_own, h3_other, cotangent, hidden, grad_pre, outer_weight, tp
    )
    hidden_piece = lax.psum_scatter(hidden_both, "blk", scatter_dimension=0, tiled=True)
    dh3_got, y_kept = lax.optimization_barrier((dh3_got, y_kept))

    dx1, dx1_low, dx2_low, dqc_own, dqc_sent, da_own, da_sent, text_own, text_sent, small_cross = cross_backward(
        dh3_own, dh3_got, own_rows(cotangent), first_sum, second_sum, row(gain_two),
        row(gain_three), output_both, query_both, cross_both, text_both[0], text_both[1],
        qc_t, oc_t, segment, text_segment, scale,
    )
    da_other = over_x(da_sent)
    da_own = after(da_own, da_other)

    def as_heads(array):
        return array.reshape(heads_here, HEAD_DIM, copies // tp_count, sub).transpose(0, 2, 1, 3)

    low = jnp.where(tp == 0, as_heads(da_own), as_heads(da_other))
    high = jnp.where(tp == 0, as_heads(da_other), as_heads(da_own))
    sent = jnp.concatenate([low, high], axis=1).reshape(blk_count, 1, HEAD_DIM, sub)
    grads = lax.all_to_all(sent, "blk", 0, 0, tiled=True)[:, 0]
    grads = grads.transpose(1, 0, 2).reshape(HEAD_DIM, blk_count * sub)
    dx1_other, dqc_other, c_other = [
        over_x(value) for value in after((dx1_low, dqc_sent, c_sent), da_other)
    ]
    grads, dx1_other, dqc_other, c_other = lax.optimization_barrier(
        (grads, dx1_other, dqc_other, c_other)
    )
    dq, parts = attend_back(
        queries, keys, values, rows_all, first, flip, out, log_total, grads, sub
    )
    while parts.shape[0] > 2:
        got = over_blk(halves(parts, 1), parts.shape[0] // 2)
        parts = (halves(parts, 0).astype(F32) + got.astype(F32)).astype(BF)
    parts_got = over_blk(parts[1], 1)
    sent = combine(dq, parts, parts_got, scale)
    back = bring_heads(sent)
    text_got, h2_other, y_got, dx2_other = after(
        [over_x(value) for value in after((text_sent, h2_own, y_sent, dx2_low), da_other)], sent
    )
    text_part = text_own + text_got.astype(F32)
    pair_send, pair_keep = pair_grads(
        [
            (a_own, a_sent, dx1_low, dx1_other),
            (c_own, c_other, dx2_low, dx2_other),
            (dqc_own, dqc_other, h2_own, h2_other),
        ],
        core,
    )
    y_own = (second_sum + y_kept + y_got.astype(F32)).astype(BF)
    back, pair_send = lax.optimization_barrier((back, pair_send))
    back = back.transpose(2, 0, 3, 1, 4).reshape(3, width_here, row_count)
    dh1_own, dh1_sent = project_back(back, [query_weight, key_weight, value_weight], tp)
    dh1_got = over_x(dh1_sent)
    head_send, head_keep = head_grads(back, normed_one, core)
    head_send, hidden_piece = lax.optimization_barrier((head_send, hidden_piece))
    hidden_both = lax.all_gather(hidden_piece, "blk", axis=0, tiled=True)
    pairs = Stream(pair_send, pair_keep, order_one, blk)
    heads = Stream(head_send, head_keep, order_two, blk)
    text = Butterfly(text_part, order_one, BF)
    y_other = over_x(y_own)
    streams = [pairs, heads, text]
    dh1_got, y_other = meet(streams, (dh1_got, y_other))
    result = in_order(y_own, y_other, tp)
    step_together([pairs, heads])
    text.step()
    through, grad_gain_one, grad_shift_one = norm_back(
        x_low.astype(F32), gain_one, dh1_own + dh1_got.astype(F32)
    )
    dx = (dx1 + through).astype(BF)
    dx_other = over_x(dx)
    small = jnp.concatenate([grad_gain_one[None], grad_shift_one[None], small_cross])
    small_got = over_x(small)
    dx_other, small_got = meet(streams, (dx_other, small_got))
    grad_frames = in_order(dx, dx_other, tp)
    small = Butterfly(small + small_got, order_one, F32)
    while pairs.phase < len(order_one) - 1:
        step_together([pairs, heads])
        text.step()
        meet(streams + [small], ())
        small.step()
    pieces = lax.all_gather(last_halves(heads, pairs), "blk")
    while small.phase is not None or text.phase is not None:
        small.step()
        text.step()
        meet([small, text], ())
    text_total = text.value.astype(BF)
    grad_text = dg(text_total[0], cross_key, ((0,), (1,)))
    grad_text = (grad_text + dg(text_total[1], cross_value, ((0,), (1,)))).astype(BF)
    text_got = over_x(grad_text)
    grad_cross_key = dg(text_states, text_total[0], ((0,), (1,)))
    grad_cross_value = dg(text_states, text_total[1], ((0,), (1,)))
    grad_text = grad_text.astype(F32) + text_got.astype(F32)
    grad_text, grad_cross_key, grad_cross_value, hidden_both = lax.optimization_barrier(
        (grad_text, grad_cross_key, grad_cross_value, hidden_both)
    )
    grad_outer, grad_inner = hidden_out(hidden_both)
    grads = widen(
        after(pieces, grad_inner), order_two, order_one, heads.keep.shape[0], pairs.keep.shape[0],
        width_here, depth,
    )
    grad_query, grad_key, grad_value, grad_output, grad_cross_output, grad_cross_query = grads
    small = small.value

    return (
        result,
        grad_frames,
        grad_text,
        small[0],
        small[1],
        small[2],
        small[3],
        small[4],
        small[5],
        grad_query,
        grad_key,
        grad_value,
        grad_output,
        grad_cross_query,
        grad_cross_key,
        grad_cross_value,
        grad_cross_output,
        grad_inner,
        grad_outer,
    )


def solution(mesh):
    return jax.shard_map(
        shards,
        mesh=mesh,
        in_specs=(
            P("blk", None),
            P(),
            P(),
            P(),
            P(),
            P(),
            P(),
            P(),
            P(),
            P(),
            P(None, "tp"),
            P(None, "tp"),
            P(None, "tp"),
            P("tp", None),
            P(None, "tp"),
            P(None, "tp"),
            P(None, "tp"),
            P("tp", None),
            P(None, "tp"),
            P("tp", None),
            P("blk", None),
        ),
        out_specs=(
            P("blk", None),
            P("blk", None),
            P(),
            P(),
            P(),
            P(),
            P(),
            P(),
            P(),
            P(None, "tp"),
            P(None, "tp"),
            P(None, "tp"),
            P("tp", None),
            P(None, "tp"),
            P(None, "tp"),
            P(None, "tp"),
            P("tp", None),
            P(None, "tp"),
            P("tp", None),
        ),
        check_vma=False,
    )
```
